32 devices in a mesh: seq: 2 (over core), blk: 8 (over z, x), head: 2 (over y).
Axes of the slice: x: 2, y: 2, z: 4, core: 2. Of those that a mesh axis runs over, the one named last changes fastest.
Arguments:
- hidden: bfloat16 [2048, 1024], P(('seq', 'blk')), may hold values from -6 to 6
- memory: bfloat16 [1024, 1024], P('seq'), may hold values from -6 to 6
- lengths: int32 [2], P('seq'), may hold values from 512 to 1024, as said below
- out_grad: bfloat16 [2048, 1024], P(('seq', 'blk')), may hold values from -6 to 6
- ln_self: float32 [1024], replicated, may hold values from 0.5 to 1.5
- self_query: bfloat16 [1024, 1024], P(None, 'head'), may hold values from -0.046875 to 0.046875
- self_key: bfloat16 [1024, 512], P(None, 'head'), may hold values from -0.1875 to 0.1875
- self_value: bfloat16 [1024, 512], P(None, 'head'), may hold values from -0.1875 to 0.1875
- self_out: bfloat16 [1024, 1024], P(None, 'head'), may hold values from -1 to 1
- rel_bias: float32 [32, 16], P(None, 'head'), may hold values from -4 to 4
- ln_cross: float32 [1024], replicated, may hold values from 0.5 to 1.5
- cross_query: bfloat16 [1024, 1024], P(None, 'head'), may hold values from -0.046875 to 0.046875
- cross_key: bfloat16 [1024, 512], P(None, 'head'), may hold values from -0.1875 to 0.1875
- cross_value: bfloat16 [1024, 512], P(None, 'head'), may hold values from -0.1875 to 0.1875
- cross_out: bfloat16 [1024, 1024], P(None, 'head'), may hold values from -0.5 to 0.5
- ln_ffn: float32 [1024], replicated, may hold values from 0.5 to 1.5
- ffn_gate: bfloat16 [1024, 2816], P(None, 'head'), may hold values from -0.1875 to 0.1875
- ffn_up: bfloat16 [1024, 2816], P(None, 'head'), may hold values from -0.1875 to 0.1875
- feedforward_down_weight: bfloat16 [1024, 2816], P(None, 'head'), may hold values from -0.109375 to 0.109375
Outputs:
- layer_out: bfloat16 [2048, 1024], P(('seq', 'blk'))
- hidden_grad: float32 [2048, 1024], P(('seq', 'blk'))
- memory_grad: float32 [1024, 1024], P(('seq', 'blk', 'head'))
- grad_ln_self: float32 [1024], P(('seq', 'blk'))
- grad_self_query: float32 [1024, 1024], P(('seq', 'blk'), 'head')
- grad_self_key: float32 [1024, 512], P(('seq', 'blk'), 'head')
- grad_self_value: float32 [1024, 512], P(('seq', 'blk'), 'head')
- grad_self_out: float32 [1024, 1024], P(('seq', 'blk'), 'head')
- grad_rel_bias: float32 [32, 16], P(None, 'head')
- grad_ln_cross: float32 [1024], P(('seq', 'blk'))
- grad_cross_query: float32 [1024, 1024], P(('seq', 'blk'), 'head')
- grad_cross_key: float32 [1024, 512], P(('seq', 'blk'), 'head')
- grad_cross_value: float32 [1024, 512], P(('seq', 'blk'), 'head')
- grad_cross_out: float32 [1024, 1024], P(('seq', 'blk'), 'head')
- grad_ln_ffn: float32 [1024], P(('seq', 'blk'))
- grad_ffn_gate: float32 [1024, 2816], P(('seq', 'blk'), 'head')
- grad_ffn_up: float32 [1024, 2816], P(('seq', 'blk'), 'head')
- grad_ffn_down: float32 [1024, 2816], P(('seq', 'blk'), 'head')
The draws below stay inside these ranges and needn't reach their ends.
Inputs may be any that keep to these rules, and one draw needn't show every extreme that they name: `lengths`: one sequence has all 1024 positions valid; every other has 512 or more.
All inputs are finite; a program needn't handle non-finite values.
Results may differ from the reference program's by a relative error of at most 0.04.
Values may be sent and summed in bfloat16 or wider, within the bound.
A program may use at most 192 MiB of HBM per device.

```python
import math
import jax
import jax.numpy as jnp
import numpy as np
from jax import lax

D = 1024
HEADS = 16
HEAD_DIM = 64
GROUPS = 8
FF = 2816
BUCKETS = 32
MAX_DIST = 128
MEM = 512
SEQ_CAP = 1024
SEQS = 2
TOKENS = 2048


def draw_lengths(key, part):
    chosen = jax.random.randint(jax.random.fold_in(key, 1), (), 0, SEQS)
    others = jax.random.randint(jax.random.fold_in(key, 2), (SEQS,), SEQ_CAP // 2, SEQ_CAP)
    return jnp.where(jnp.arange(SEQS) == chosen, SEQ_CAP, others).astype(jnp.int32)


def raised(result, stream_key, source, target, blocks, factor):
    owner, partner = [(jnp.arange(result.shape[axis_at]) // (result.shape[axis_at] // blocks)).reshape([-1 if axis == axis_at else 1 for axis in range(result.ndim)]) for axis_at in (source, target)]
    chosen = jax.random.permutation(stream_key, blocks)[partner]
    strong = (owner == chosen) | (owner == (partner + blocks // 2) % blocks)
    return jnp.where(strong, factor * result, result)


def block_levels(key, extent, cuts, smallest, high):
    level, own = 1.0, jax.random.fold_in(key, 6)
    for axis_at, parts in cuts:
        steps = jnp.exp(jax.random.uniform(jax.random.fold_in(own, axis_at), (parts,), jnp.float32, smallest / len(cuts), high / len(cuts)))
        level = level * jnp.repeat(steps, extent[axis_at] // parts).reshape([-1 if axis == axis_at else 1 for axis in range(len(extent))])
    return level


def bell_draw(stream_key, shape, width, limit, cuts=(), kind=jnp.bfloat16):
    loudness = block_levels(stream_key, shape, cuts, -0.22, 0.18) if cuts else 1.0
    drawn = jax.random.normal(stream_key, shape, jnp.float32) * width * loudness
    return jnp.minimum(jnp.maximum(drawn, -limit), limit).astype(kind)


def bell_draw_with(own_key, shape, spread, reach, cuts, heavy, kind=jnp.bfloat16):
    entries = spread * jax.random.normal(own_key, shape, jnp.float32)
    if cuts:
        entries = entries * block_levels(own_key, shape, cuts, -0.22, 0.18)
    return jnp.clip(raised(entries, jax.random.fold_in(own_key, 3), *heavy), -reach, reach).astype(kind)


def setup_inputs(seed: int = 0) -> dict:
    seeds = jax.random.split(jax.random.key(seed), 20)
    return {
        "hidden": bell_draw_with(seeds[0], (TOKENS, D), 1.0, 6.0, ((0, 16),), (0, 1, 16, 2.0)),
        "memory": bell_draw(seeds[1], (SEQS * MEM, D), 1.0, 6.0, ((0, 2),)),
        "lengths": draw_lengths(jax.random.fold_in(seeds[19], 71), 0),
        "out_grad": bell_draw_with(seeds[3], (TOKENS, D), 1.0, 6.0, ((0, 16),), (0, 1, 16, 2.0)),
        "ln_self": jnp.clip(1.0 + 0.1 * jax.random.normal(seeds[4], (D,), jnp.float32), 0.5, 1.5),
        "self_query": bell_draw(seeds[5], (D, HEADS * HEAD_DIM), (16 * D) ** -0.5, 0.046875, ((1, 2),)),
        "self_key": bell_draw(seeds[6], (D, GROUPS * HEAD_DIM), D ** -0.5, 0.1875, ((1, 2),)),
        "self_value": bell_draw(seeds[7], (D, GROUPS * HEAD_DIM), D ** -0.5, 0.1875, ((1, 2),)),
        "self_out": bell_draw(seeds[8], (D, HEADS * HEAD_DIM), (max(4, HEADS * HEAD_DIM // 32)) ** -0.5, 1.0, ((1, 2),)),
        "rel_bias": bell_draw(seeds[9], (BUCKETS, HEADS), 1.0, 4.0, ((1, 2),), jnp.float32),
        "ln_cross": jnp.clip(1.0 + 0.1 * jax.random.normal(seeds[10], (D,), jnp.float32), 0.5, 1.5),
        "cross_query": bell_draw(seeds[11], (D, HEADS * HEAD_DIM), (16 * D) ** -0.5, 0.046875, ((1, 2),)),
        "cross_key": bell_draw(seeds[12], (D, GROUPS * HEAD_DIM), D ** -0.5, 0.1875, ((1, 2),)),
        "cross_value": bell_draw(seeds[13], (D, GROUPS * HEAD_DIM), D ** -0.5, 0.1875, ((1, 2),)),
        "cross_out": bell_draw(seeds[14], (D, HEADS * HEAD_DIM), (max(1, HEADS * HEAD_DIM // 8)) ** -0.5, 0.5, ((1, 2),)),
        "ln_ffn": jnp.clip(1.0 + 0.1 * jax.random.normal(seeds[15], (D,), jnp.float32), 0.5, 1.5),
        "ffn_gate": bell_draw(seeds[16], (D, FF), D ** -0.5, 0.1875, ((1, 2),)),
        "ffn_up": bell_draw(seeds[17], (D, FF), D ** -0.5, 0.1875, ((1, 2),)),
        "feedforward_down_weight": bell_draw(seeds[18], (D, FF), FF ** -0.5, 0.109375, ((1, 2),)),
    }


@jax.custom_vjp
def low(v):
    return lax.optimization_barrier(v.astype(jnp.bfloat16)).astype(jnp.float32)

@jax.custom_vjp
def low_back(v):
    return v

def low_keep(v):
    return (low(v), None)

def low_pass(kept, grad):
    return (grad,)

def back_keep(v):
    return (v, None)

def back_low(kept, grad):
    return (low(grad),)
low.defvjp(low_keep, low_pass)
low_back.defvjp(back_keep, back_low)
EPSILON = 1e-06
MASKED = -1e+30
HIGHEST = lax.Precision.HIGHEST

def both_ways(value):
    return low_back(low(value))

def bucket_of(distance, bucket_count, far_reach):
    exact_span = bucket_count // 2
    thresholds = np.ceil(exact_span * (far_reach / exact_span) ** (np.arange(1, exact_span) / exact_span))
    bucket_index = jnp.minimum(distance, exact_span)
    for threshold in thresholds:
        bucket_index = bucket_index + (distance >= int(threshold)).astype(jnp.int32)
    return bucket_index

def rms_scale(values, norm_gain):
    return values * lax.rsqrt(lax.optimization_barrier(jnp.mean(values * values, axis=-1, keepdims=True)) + EPSILON) * norm_gain

def project(left, right):
    return jnp.dot(left, right, precision=HIGHEST)

def project_t(left, right):
    return jnp.dot(left, right.T, precision=HIGHEST)

def attend(queries, key_rows, value_rows, query_first, length, bias_table, causal):
    query_count = queries.shape[0]
    key_count = key_rows.shape[0]
    repeat = HEADS // GROUPS
    grouped = queries.reshape(query_count, GROUPS, repeat, HEAD_DIM)
    key_grid = key_rows.reshape(key_count, GROUPS, HEAD_DIM)
    value_grid = value_rows.reshape(key_count, GROUPS, HEAD_DIM)
    scores = jnp.einsum('tgrd,pgd->grtp', grouped, key_grid, precision=HIGHEST).reshape(HEADS, query_count, key_count)
    if causal:
        query_pos = query_first + jnp.arange(query_count, dtype=jnp.int32)
        key_pos = jnp.arange(key_count, dtype=jnp.int32)
        distance = query_pos[:, None] - key_pos[None, :]
        by_distance = jnp.take(bias_table, bucket_of(key_pos, BUCKETS, MAX_DIST), axis=0)
        bias_grid = jnp.take(by_distance, jnp.maximum(distance, 0), axis=0)
        scores = low_back(scores + jnp.transpose(bias_grid, (2, 0, 1)))
        allowed = (distance >= 0) & (key_pos[None, :] < length)
        scores = jnp.where(allowed[None], scores, MASKED)
    else:
        scores = low_back(scores)
    weights = low(jax.nn.softmax(scores, axis=-1))
    mixed = jnp.einsum('grtp,pgd->tgrd', weights.reshape(GROUPS, repeat, query_count, key_count), value_grid, precision=HIGHEST)
    return mixed.reshape(query_count, HEADS * HEAD_DIM)

def attention(queries, key_rows, value_rows, length, bias_table, causal):
    row_count = queries.shape[0]
    block_size = math.gcd(row_count, 512)
    blocks = queries.reshape(row_count // block_size, block_size, queries.shape[1])
    block_firsts = jnp.arange(row_count // block_size, dtype=jnp.int32) * block_size

    def one_block(operands):
        return attend(operands[0], key_rows, value_rows, operands[1], length, bias_table, causal)
    mixed = lax.map(jax.checkpoint(one_block), (blocks, block_firsts))
    return mixed.reshape(row_count, queries.shape[1])

def decoder_layer(rows_in, memory_rows, length, params):
    ln_self, self_query, self_key, self_value, self_out, rel_bias, ln_cross, cross_query, cross_key, cross_value, cross_out, ln_ffn, ffn_gate, ffn_up, feedforward_down_weight = params
    normed = low(rms_scale(rows_in, ln_self))
    queries = both_ways(project(normed, self_query))
    key_rows = both_ways(project(normed, self_key))
    value_rows = both_ways(project(normed, self_value))
    attended = both_ways(attention(queries, key_rows, value_rows, length, rel_bias, True))
    after_self = rows_in + low_back(project_t(attended, self_out))
    normed = low(rms_scale(after_self, ln_cross))
    queries = both_ways(project(normed, cross_query))
    key_rows = both_ways(project(memory_rows, cross_key))
    value_rows = both_ways(project(memory_rows, cross_value))
    attended = both_ways(attention(queries, key_rows, value_rows, length, rel_bias, False))
    after_cross = after_self + low_back(project_t(attended, cross_out))
    normed = low(rms_scale(after_cross, ln_ffn))
    gate_rows = low_back(project(normed, ffn_gate))
    upward = low_back(project(normed, ffn_up))
    inner_rows = low(jax.nn.gelu(gate_rows, approximate=True) * upward)
    return after_cross + low_back(project_t(inner_rows, feedforward_down_weight))

def reference(hidden, memory, lengths, out_grad, ln_self, self_query, self_key, self_value, self_out, rel_bias, ln_cross, cross_query, cross_key, cross_value, cross_out, ln_ffn, ffn_gate, ffn_up, feedforward_down_weight):
    params = tuple((weight_array.astype(jnp.float32) for weight_array in (ln_self, self_query, self_key, self_value, self_out, rel_bias, ln_cross, cross_query, cross_key, cross_value, cross_out, ln_ffn, ffn_gate, ffn_up, feedforward_down_weight)))
    rows_all = hidden.astype(jnp.float32).reshape(SEQS, SEQ_CAP, D)
    memory_all = memory.astype(jnp.float32).reshape(SEQS, MEM, D)
    cotangent = out_grad.astype(jnp.float32).reshape(SEQS, SEQ_CAP, D)
    positions = jnp.arange(SEQ_CAP, dtype=jnp.int32)

    def per_sequence(totals, inputs):
        rows_one, memory_one, length, cot_one = inputs
        output, pullback = jax.vjp(lambda rows_arg, memory_arg, params_arg: decoder_layer(rows_arg, memory_arg, length, params_arg), rows_one, memory_one, params)
        kept = (positions < length).astype(jnp.float32)[:, None]
        rows_grad, memory_grad, params_grad = pullback(cot_one * kept)
        totals = jax.tree.map(jnp.add, totals, params_grad)
        return (totals, (output, rows_grad, memory_grad))
    totals, results = lax.scan(per_sequence, jax.tree.map(jnp.zeros_like, params), (rows_all, memory_all, lengths, cotangent))
    outputs, rows_grads, memory_grads = results
    return (outputs.reshape(TOKENS, D).astype(jnp.bfloat16), rows_grads.reshape(TOKENS, D), memory_grads.reshape(SEQS * MEM, D), totals[0], totals[1], totals[2], totals[3], totals[4], totals[5], totals[6], totals[7], totals[8], totals[9], totals[10], totals[11], totals[12], totals[13], totals[14])
```

```python
import functools

import jax
import jax.numpy as jnp
import numpy as np
from jax import lax
from jax.experimental import pallas as pl
from jax.experimental.pallas import tpu as pltpu
from jax.sharding import PartitionSpec as P

MESH = pl.DeviceIdType.MESH

HEAD_DIM = 64
BUCKETS = 32
MAX_DIST = 128


EPSILON = 1e-06
MASKED = -1e30
HIGHEST = lax.Precision.HIGHEST


def bucket_of(distance, bucket_count, far_reach):
    exact_span = bucket_count // 2
    thresholds = np.ceil(
        exact_span * (far_reach / exact_span) ** (np.arange(1, exact_span) / exact_span)
    )
    bucket_index = jnp.minimum(distance, exact_span)
    for threshold in thresholds:
        bucket_index = bucket_index + (distance >= int(threshold)).astype(jnp.int32)
    return bucket_index


def block_rows(row_count, limit):
    for candidate in range(min(row_count, limit), 0, -1):
        if row_count % candidate == 0:
            return candidate
    return 1


def matmul(left, right):
    return jnp.dot(left, right, preferred_element_type=jnp.float32)


def matmul_t(left, right):
    return lax.dot_general(
        left, right, (((1,), (1,)), ((), ())), preferred_element_type=jnp.float32
    )


def matmul_tn(left, right):
    return lax.dot_general(
        left, right, (((0,), (0,)), ((), ())), preferred_element_type=jnp.float32
    )


def blk_bits(blk_count):
    return blk_count.bit_length() - 1


def reduce_kernel(bits, widths, small_shape, *refs):
    count = len(widths)
    parts = refs[:count]
    small_in = refs[count]
    outs = refs[count + 1 : 2 * count + 1]
    small_out = refs[2 * count + 1]
    rest = refs[2 * count + 2 :]
    stages = bits + 1
    landing = [rest[piece * stages : (piece + 1) * stages] for piece in range(count)]
    small_land, small_acc, send_sem, recv_sem, small_send, small_recv = rest[count * stages :]
    seq, blk, head = (lax.axis_index(name) for name in ("seq", "blk", "head"))
    my_bits = [lax.rem(blk // (1 << bit), 2) for bit in range(bits)]

    def partner(stage):
        if stage == 0:
            return (1 - seq, blk, head)
        bit = stage - 1
        return (seq, blk + (1 - 2 * my_bits[bit]) * (1 << bit), head)

    barrier = pltpu.get_barrier_semaphore()
    for stage in range(stages):
        pl.semaphore_signal(barrier, inc=1, device_id=partner(stage), device_id_type=MESH)
    pl.semaphore_wait(barrier, stages)

    def view(ref, stage, mine):
        if stage == 0:
            return ref.at[seq if mine else 1 - seq]
        index = [seq]
        for bit in reversed(range(bits)):
            if bit < stage - 1:
                index.append(my_bits[bit])
            elif bit == stage - 1:
                index.append(my_bits[bit] if mine else 1 - my_bits[bit])
            else:
                index.append(slice(None))
        return ref.at[tuple(index)]

    def copy_of(piece, stage):
        return pltpu.make_async_remote_copy(
            src_ref=view(parts[piece], stage, False),
            dst_ref=landing[piece][stage],
            send_sem=send_sem.at[piece, stage],
            recv_sem=recv_sem.at[piece, stage],
            device_id=partner(stage),
            device_id_type=MESH,
        )

    def fold(piece, stage):
        mine = view(parts[piece], stage, True)
        got = landing[piece][stage]
        if stage == stages - 1:
            outs[piece][...] = mine[...].astype(jnp.float32) + got[...].astype(jnp.float32)
            return
        lead = got.shape[:-2]
        total = int(np.prod(lead))
        for flat in range(total):
            index = tuple(int(value) for value in np.unravel_index(flat, lead))
            mine[index] = (
                mine[index].astype(jnp.float32) + got[index].astype(jnp.float32)
            ).astype(jnp.bfloat16)

    def small_copy(stage):
        return pltpu.make_async_remote_copy(
            src_ref=small_acc.at[stage],
            dst_ref=small_land.at[stage],
            send_sem=small_send.at[stage],
            recv_sem=small_recv.at[stage],
            device_id=partner(stage),
            device_id_type=MESH,
        )

    small_acc[0] = small_in[...]
    for step in range(count + stages):
        for stage in reversed(range(stages + 1)):
            piece = step - stage
            if not 0 <= piece < count:
                continue
            if stage > 0:
                copy_of(piece, stage - 1).wait_recv()
                fold(piece, stage - 1)
            if stage < stages:
                copy_of(piece, stage).start()
        if step <= stages:
            if step > 0:
                small_copy(step - 1).wait_recv()
                total = small_acc[step - 1] + small_land[step - 1]
                if step < stages:
                    small_acc[step] = total
                else:
                    small_out[...] = total
            if step < stages:
                small_copy(step).start()
    for piece in range(count):
        for stage in range(stages):
            copy_of(piece, stage).wait_send()
    for stage in range(stages):
        small_copy(stage).wait_send()


def reduce_gradients(parts, small, blk_count):
    bits = blk_bits(blk_count)
    stages = bits + 1
    rows = parts[0].shape[0] // (2 * blk_count)
    widths = [part.shape[1] for part in parts]
    lead = (2,) * (bits + 1)
    shaped = [part.reshape(*lead, rows, part.shape[1]) for part in parts]
    scratch = []
    for width in widths:
        for stage in range(stages):
            scratch.append(pltpu.VMEM((2,) * (bits - stage) + (rows, width), jnp.bfloat16))
    scratch += [
        pltpu.VMEM((stages, *small.shape), jnp.float32),
        pltpu.VMEM((stages, *small.shape), jnp.float32),
        pltpu.SemaphoreType.DMA((len(parts), stages)),
        pltpu.SemaphoreType.DMA((len(parts), stages)),
        pltpu.SemaphoreType.DMA((stages,)),
        pltpu.SemaphoreType.DMA((stages,)),
    ]
    vmem = pl.BlockSpec(memory_space=pltpu.VMEM)
    return pl.pallas_call(
        functools.partial(reduce_kernel, bits, widths, small.shape),
        out_shape=[jax.ShapeDtypeStruct((rows, width), jnp.float32) for width in widths]
        + [jax.ShapeDtypeStruct(small.shape, jnp.float32)],
        in_specs=[vmem] * (len(parts) + 1),
        out_specs=[vmem] * (len(parts) + 1),
        scratch_shapes=scratch,
        compiler_params=pltpu.CompilerParams(
            collective_id=0, has_side_effects=True, vmem_limit_bytes=56 * 1024 * 1024
        ),
        name="grad_reduce",
    )(*shaped, small)


def rms_scale(values, norm_gain):
    return (
        values * lax.rsqrt(jnp.mean(values * values, axis=-1, keepdims=True) + EPSILON) * norm_gain
    )


def rms_back(values, norm_gain, normed_grad):
    scale = lax.rsqrt(jnp.mean(values * values, axis=-1, keepdims=True) + EPSILON)
    unit = values * scale
    unit_grad = normed_grad * norm_gain
    values_grad = scale * (unit_grad - unit * jnp.mean(unit_grad * unit, axis=-1, keepdims=True))
    return (values_grad, jnp.sum(normed_grad * unit, axis=0))


def toeplitz(bias_line, row_count, col_count):
    heads_here, line_length = bias_line.shape
    tiled = jnp.tile(bias_line, (1, row_count + 1))
    tiled = tiled[:, row_count - 1 : row_count - 1 + row_count * (line_length - 1)]
    return tiled.reshape(heads_here, row_count, line_length - 1)[:, :, :col_count]


def diagonal_sums(grid, line_length):
    heads_here, row_count, col_count = grid.shape
    padded = jnp.pad(grid, ((0, 0), (0, 0), (0, line_length - 1 - col_count)))
    flat = padded.reshape(heads_here, row_count * (line_length - 1))
    flat = jnp.pad(flat, ((0, 0), (row_count - 1, line_length + 1)))
    return jnp.sum(flat.reshape(heads_here, row_count + 1, line_length), axis=1)


def score_block(query_matrix, key_block, query_first, key_first, length, bias_table):
    row_count, groups_here, repeat, head_size = query_matrix.shape
    col_count = key_block.shape[0]
    key_grid = key_block.reshape(col_count, groups_here, head_size)
    scores = jnp.einsum(
        "tgrd,pgd->grtp", query_matrix, key_grid, preferred_element_type=jnp.float32
    )
    line_length = row_count + col_count - 1
    distance = query_first - key_first + row_count - 1 - jnp.arange(line_length, dtype=jnp.int32)
    buckets = bucket_of(jnp.maximum(distance, 0), BUCKETS, MAX_DIST)
    one_hot = (buckets[:, None] == jnp.arange(BUCKETS, dtype=jnp.int32)[None, :]).astype(
        jnp.float32
    )
    bias_line = lax.dot_general(bias_table, one_hot, (((0,), (1,)), ((), ())), precision=HIGHEST)
    bias_grid = toeplitz(bias_line, row_count, col_count).reshape(
        groups_here, repeat, row_count, col_count
    )
    query_pos = query_first + jnp.arange(row_count, dtype=jnp.int32)
    key_pos = key_first + jnp.arange(col_count, dtype=jnp.int32)
    allowed = (query_pos[:, None] >= key_pos[None, :]) & (key_pos[None, :] < length)
    return (scores + bias_grid, allowed, one_hot)


def body(
    hidden,
    memory,
    lengths,
    out_grad,
    ln_self,
    self_query,
    self_key,
    self_value,
    self_out,
    rel_bias,
    ln_cross,
    cross_query,
    cross_key,
    cross_value,
    cross_out,
    ln_ffn,
    ffn_gate,
    ffn_up,
    feedforward_down_weight,
):
    tok_rows = hidden.shape[0]
    groups_here = self_key.shape[1] // HEAD_DIM
    heads_here = self_query.shape[1] // HEAD_DIM
    repeat = heads_here // groups_here
    block_count = lax.axis_size("blk")
    seq_rows = tok_rows * block_count
    query_first = lax.axis_index("blk") * tok_rows
    length = lengths[0]
    rows_in = hidden.astype(jnp.float32)

    def head_running_total(partial_sum):
        return lax.psum(partial_sum.astype(jnp.bfloat16), "head").astype(jnp.float32)

    normed_self = rms_scale(rows_in, ln_self).astype(jnp.bfloat16)
    queries = matmul(normed_self, self_query).astype(jnp.bfloat16)
    key_rows = matmul(normed_self, self_key).astype(jnp.bfloat16)
    value_rows = matmul(normed_self, self_value).astype(jnp.bfloat16)
    query_matrix = queries.reshape(tok_rows, groups_here, repeat, HEAD_DIM)
    start_state = (
        jnp.full((groups_here, repeat, tok_rows), MASKED, jnp.float32),
        jnp.zeros((groups_here, repeat, tok_rows), jnp.float32),
        jnp.zeros((groups_here, repeat, tok_rows, HEAD_DIM), jnp.float32),
    )
    first_row = jnp.int32(0)
    both = lax.all_gather(jnp.concatenate([key_rows, value_rows], axis=1), "blk", axis=0, tiled=True)
    key_piece, value_piece = jnp.split(both, 2, axis=1)
    piece_rows = key_piece.shape[0]
    fold_inner_size = block_rows(piece_rows, 1024)

    def visit_block(block_index, current):
        old_max, old_total, old_acc = current
        key_block = lax.dynamic_slice_in_dim(
            key_piece, block_index * fold_inner_size, fold_inner_size, 0
        )
        value_block = lax.dynamic_slice_in_dim(
            value_piece, block_index * fold_inner_size, fold_inner_size, 0
        )
        scores, allowed, one_hot = score_block(
            query_matrix,
            key_block,
            query_first,
            first_row + block_index * fold_inner_size,
            length,
            rel_bias,
        )
        new_max = jnp.maximum(old_max, jnp.max(jnp.where(allowed, scores, MASKED), axis=-1))
        weights = jnp.where(allowed, jnp.exp(scores - new_max[..., None]), 0.0)
        rescale = jnp.exp(old_max - new_max)
        updated_total = old_total * rescale + jnp.sum(weights, axis=-1)
        value_grid = value_block.reshape(fold_inner_size, groups_here, HEAD_DIM)
        updated_accumulator = old_acc * rescale[..., None] + jnp.einsum(
            "grtp,pgd->grtd",
            weights.astype(jnp.bfloat16),
            value_grid,
            preferred_element_type=jnp.float32,
        )
        return (new_max, updated_total, updated_accumulator)

    row_max, row_total, accumulated = lax.fori_loop(
        0, piece_rows // fold_inner_size, visit_block, start_state
    )
    attended_precise = accumulated / row_total[..., None]
    log_total = row_max + jnp.log(row_total)
    attended = (
        jnp.transpose(attended_precise, (2, 0, 1, 3))
        .reshape(tok_rows, heads_here * HEAD_DIM)
        .astype(jnp.bfloat16)
    )
    after_self = rows_in + head_running_total(matmul_t(attended, self_out))
    normed_cross = rms_scale(after_self, ln_cross).astype(jnp.bfloat16)
    cross_queries = matmul(normed_cross, cross_query).astype(jnp.bfloat16)
    share_rows = memory.shape[0] // block_count
    memory_rows = lax.dynamic_slice_in_dim(
        memory, lax.axis_index("blk") * share_rows, share_rows, 0
    )
    memory_keys = matmul(memory, cross_key).astype(jnp.bfloat16)
    memory_values = matmul(memory, cross_value).astype(jnp.bfloat16)
    memory_count = memory.shape[0]
    cross_grid = cross_queries.reshape(tok_rows, groups_here, repeat, HEAD_DIM)
    memory_key_grid = memory_keys.reshape(memory_count, groups_here, HEAD_DIM)
    memory_value_grid = memory_values.reshape(memory_count, groups_here, HEAD_DIM)
    cross_scores = jnp.einsum(
        "tgrd,mgd->grtm", cross_grid, memory_key_grid, preferred_element_type=jnp.float32
    )
    cross_probs = jax.nn.softmax(cross_scores, axis=-1)
    cross_weights = cross_probs.astype(jnp.bfloat16)
    cross_attended = (
        jnp.einsum(
            "grtm,mgd->tgrd", cross_weights, memory_value_grid, preferred_element_type=jnp.float32
        )
        .reshape(tok_rows, heads_here * HEAD_DIM)
        .astype(jnp.bfloat16)
    )
    after_cross = after_self + head_running_total(matmul_t(cross_attended, cross_out))
    normed_ffn = rms_scale(after_cross, ln_ffn).astype(jnp.bfloat16)
    gate_rows = matmul(normed_ffn, ffn_gate)
    upward = matmul(normed_ffn, ffn_up)
    activated, gelu_pull = jax.vjp(
        lambda gate_arg, up_arg: jax.nn.gelu(gate_arg, approximate=True) * up_arg, gate_rows, upward
    )
    inner_rows = activated.astype(jnp.bfloat16)
    final_rows = after_cross + head_running_total(matmul_t(inner_rows, feedforward_down_weight))
    positions = query_first + jnp.arange(tok_rows, dtype=jnp.int32)
    final_grad = out_grad.astype(jnp.float32) * (positions < length).astype(jnp.float32)[:, None]
    ffn_branch_grad = final_grad.astype(jnp.bfloat16)
    grad_ffn_down = matmul_tn(ffn_branch_grad, inner_rows)
    inner_grad = matmul(ffn_branch_grad, feedforward_down_weight)
    gate_grad, up_grad = gelu_pull(inner_grad)
    gate_grad = gate_grad.astype(jnp.bfloat16)
    up_grad = up_grad.astype(jnp.bfloat16)
    grad_ffn_gate = matmul_tn(normed_ffn, gate_grad)
    grad_ffn_up = matmul_tn(normed_ffn, up_grad)
    normed_grad = head_running_total(matmul_t(gate_grad, ffn_gate) + matmul_t(up_grad, ffn_up))
    norm_part, grad_ln_ffn = rms_back(after_cross, ln_ffn, normed_grad)
    cross_cot = final_grad + norm_part
    cross_branch_grad = cross_cot.astype(jnp.bfloat16)
    grad_cross_out = matmul_tn(cross_branch_grad, cross_attended)
    cross_attended_grad = matmul(cross_branch_grad, cross_out).astype(jnp.bfloat16)
    cross_att_grid = cross_attended_grad.reshape(tok_rows, groups_here, repeat, HEAD_DIM)
    cross_prob_grad = jnp.einsum(
        "tgrd,mgd->grtm", cross_att_grid, memory_value_grid, preferred_element_type=jnp.float32
    )
    cross_delta = jnp.sum(cross_probs * cross_prob_grad, axis=-1, keepdims=True)
    cross_score_grad = (cross_probs * (cross_prob_grad - cross_delta)).astype(jnp.bfloat16)
    cross_query_grad = (
        jnp.einsum(
            "grtm,mgd->tgrd", cross_score_grad, memory_key_grid, preferred_element_type=jnp.float32
        )
        .reshape(tok_rows, heads_here * HEAD_DIM)
        .astype(jnp.bfloat16)
    )
    memory_key_part = jnp.einsum(
        "grtm,tgrd->mgd", cross_score_grad, cross_grid, preferred_element_type=jnp.float32
    ).reshape(memory_count, groups_here * HEAD_DIM)
    memory_value_part = jnp.einsum(
        "grtm,tgrd->mgd", cross_weights, cross_att_grid, preferred_element_type=jnp.float32
    ).reshape(memory_count, groups_here * HEAD_DIM)
    memory_key_sum, memory_value_sum = (
        lax.psum_scatter(
            memory_key_part.astype(jnp.bfloat16), "blk", scatter_dimension=0, tiled=True
        ).astype(jnp.float32),
        lax.psum_scatter(
            memory_value_part.astype(jnp.bfloat16), "blk", scatter_dimension=0, tiled=True
        ).astype(jnp.float32),
    )
    memory_key_grad = memory_key_sum.astype(jnp.bfloat16)
    memory_value_grad = memory_value_sum.astype(jnp.bfloat16)
    grad_cross_key = matmul_tn(memory_rows, memory_key_grad)
    grad_cross_value = matmul_tn(memory_rows, memory_value_grad)
    memory_grad = lax.psum_scatter(
        (matmul_t(memory_key_grad, cross_key) + matmul_t(memory_value_grad, cross_value)).astype(
            jnp.bfloat16
        ),
        "head",
        scatter_dimension=0,
        tiled=True,
    ).astype(jnp.float32)
    grad_cross_query = matmul_tn(normed_cross, cross_query_grad)
    normed_grad = head_running_total(matmul_t(cross_query_grad, cross_query))
    norm_part, grad_ln_cross = rms_back(after_self, ln_cross, normed_grad)
    self_cot = cross_cot + norm_part
    self_branch_grad = self_cot.astype(jnp.bfloat16)
    grad_self_out = matmul_tn(self_branch_grad, attended)
    attended_grad = matmul(self_branch_grad, self_out).astype(jnp.bfloat16)
    attended_gradient_matrix = attended_grad.reshape(tok_rows, groups_here, repeat, HEAD_DIM)
    row_delta_terms = jnp.einsum(
        "cskq,skcq->skc", attended_gradient_matrix.astype(jnp.float32), attended_precise
    )
    all_keys, all_values = key_piece, value_piece
    inner_size = block_rows(seq_rows, 1024)

    def visit_keys(block_index, current):
        query_acc, key_acc, value_acc, bias_acc = current
        block_first = block_index * inner_size
        key_block = lax.dynamic_slice_in_dim(all_keys, block_first, inner_size, 0)
        value_block = lax.dynamic_slice_in_dim(all_values, block_first, inner_size, 0)
        scores, allowed, one_hot = score_block(
            query_matrix, key_block, query_first, block_first, length, rel_bias
        )
        self_probs = jnp.where(allowed, jnp.exp(scores - log_total[..., None]), 0.0)
        key_grid = key_block.reshape(inner_size, groups_here, HEAD_DIM)
        value_grid = value_block.reshape(inner_size, groups_here, HEAD_DIM)
        prob_grad = jnp.einsum(
            "tgrd,pgd->grtp",
            attended_gradient_matrix,
            value_grid,
            preferred_element_type=jnp.float32,
        )
        score_grad = (self_probs * (prob_grad - row_delta_terms[..., None])).astype(jnp.bfloat16)
        query_acc = query_acc + jnp.einsum(
            "grtp,pgd->grtd", score_grad, key_grid, preferred_element_type=jnp.float32
        )
        key_part = jnp.einsum(
            "grtp,tgrd->pgd", score_grad, query_matrix, preferred_element_type=jnp.float32
        ).reshape(inner_size, groups_here * HEAD_DIM)
        value_part = jnp.einsum(
            "grtp,tgrd->pgd",
            self_probs.astype(jnp.bfloat16),
            attended_gradient_matrix,
            preferred_element_type=jnp.float32,
        ).reshape(inner_size, groups_here * HEAD_DIM)
        key_acc = lax.dynamic_update_slice_in_dim(key_acc, key_part, block_first, 0)
        value_acc = lax.dynamic_update_slice_in_dim(value_acc, value_part, block_first, 0)
        line_grad = diagonal_sums(
            score_grad.astype(jnp.float32).reshape(heads_here, tok_rows, inner_size),
            tok_rows + inner_size - 1,
        )
        bias_acc = bias_acc + jnp.dot(line_grad, one_hot, precision=HIGHEST)
        return (query_acc, key_acc, value_acc, bias_acc)

    query_acc, key_acc, value_acc, bias_part = lax.fori_loop(
        0,
        seq_rows // inner_size,
        visit_keys,
        (
            jnp.zeros((groups_here, repeat, tok_rows, HEAD_DIM), jnp.float32),
            jnp.zeros((seq_rows, groups_here * HEAD_DIM), jnp.float32),
            jnp.zeros((seq_rows, groups_here * HEAD_DIM), jnp.float32),
            jnp.zeros((heads_here, BUCKETS), jnp.float32),
        ),
    )
    key_sum, value_sum = (
        lax.psum_scatter(
            key_acc.astype(jnp.bfloat16), "blk", scatter_dimension=0, tiled=True
        ).astype(jnp.float32),
        lax.psum_scatter(
            value_acc.astype(jnp.bfloat16), "blk", scatter_dimension=0, tiled=True
        ).astype(jnp.float32),
    )
    key_grad = key_sum.astype(jnp.bfloat16)
    value_grad = value_sum.astype(jnp.bfloat16)
    query_grad = (
        jnp.transpose(query_acc, (2, 0, 1, 3))
        .reshape(tok_rows, heads_here * HEAD_DIM)
        .astype(jnp.bfloat16)
    )
    grad_self_query = matmul_tn(normed_self, query_grad)
    grad_self_key = matmul_tn(normed_self, key_grad)
    grad_self_value = matmul_tn(normed_self, value_grad)
    normed_grad = head_running_total(
        matmul_t(query_grad, self_query)
        + matmul_t(key_grad, self_key)
        + matmul_t(value_grad, self_value)
    )
    norm_part, grad_ln_self = rms_back(rows_in, ln_self, normed_grad)
    hidden_grad = self_cot + norm_part
    big = [
        grad_ffn_gate, grad_ffn_up, grad_ffn_down, grad_cross_out, grad_cross_query,
        grad_cross_key, grad_cross_value, grad_self_out, grad_self_query, grad_self_key,
        grad_self_value,
    ]
    width = ln_self.shape[0]
    bias_flat = bias_part.reshape(-1)
    small = jnp.stack(
        [grad_ln_self, grad_ln_cross, grad_ln_ffn, jnp.pad(bias_flat, (0, width - bias_flat.size))]
        + [jnp.zeros_like(grad_ln_self)] * 4
    )
    sums = reduce_gradients([part.astype(jnp.bfloat16) for part in big], small, block_count)
    small_sum = sums[-1]
    share = width // (lax.axis_size("seq") * block_count)
    first = (lax.axis_index("seq") * block_count + lax.axis_index("blk")) * share
    ln_sums = lax.dynamic_slice(small_sum, (0, first), (3, share))
    bias_total = small_sum[3, : bias_flat.size].reshape(heads_here, BUCKETS).T
    gradient_sums = (
        ln_sums[0], sums[8], sums[9], sums[10], sums[7], ln_sums[1], sums[4], sums[5], sums[6],
        sums[3], ln_sums[2], sums[0], sums[1], sums[2],
    )
    return (
        final_rows.astype(jnp.bfloat16),
        hidden_grad,
        memory_grad,
        gradient_sums[0],
        gradient_sums[1],
        gradient_sums[2],
        gradient_sums[3],
        gradient_sums[4],
        bias_total,
        gradient_sums[5],
        gradient_sums[6],
        gradient_sums[7],
        gradient_sums[8],
        gradient_sums[9],
        gradient_sums[10],
        gradient_sums[11],
        gradient_sums[12],
        gradient_sums[13],
    )


def solution(mesh):
    in_specs = (
        P(("seq", "blk"), None),
        P("seq", None),
        P("seq"),
        P(("seq", "blk"), None),
        P(),
        P(None, "head"),
        P(None, "head"),
        P(None, "head"),
        P(None, "head"),
        P(None, "head"),
        P(),
        P(None, "head"),
        P(None, "head"),
        P(None, "head"),
        P(None, "head"),
        P(),
        P(None, "head"),
        P(None, "head"),
        P(None, "head"),
    )
    out_specs = (
        P(("seq", "blk"), None),
        P(("seq", "blk"), None),
        P(("seq", "blk", "head"), None),
        P(("seq", "blk")),
        P(("seq", "blk"), "head"),
        P(("seq", "blk"), "head"),
        P(("seq", "blk"), "head"),
        P(("seq", "blk"), "head"),
        P(None, "head"),
        P(("seq", "blk")),
        P(("seq", "blk"), "head"),
        P(("seq", "blk"), "head"),
        P(("seq", "blk"), "head"),
        P(("seq", "blk"), "head"),
        P(("seq", "blk")),
        P(("seq", "blk"), "head"),
        P(("seq", "blk"), "head"),
        P(("seq", "blk"), "head"),
    )
    return jax.shard_map(body, mesh=mesh, in_specs=in_specs, out_specs=out_specs, check_vma=False)
```

```python
import functools

import jax
import jax.numpy as jnp
import numpy as np
from jax import lax
from jax.experimental import pallas as pl
from jax.experimental.pallas import tpu as pltpu
from jax.sharding import PartitionSpec as P

MESH = pl.DeviceIdType.MESH
HEAD_DIM = 64
BUCKETS = 32
MAX_DIST = 128
EPSILON = 1e-06
MASKED = -1e30
BF = jnp.bfloat16
F32 = jnp.float32
TILE = 256
GELU_A = float(np.sqrt(2.0 / np.pi))
GELU_B = 0.044715

NAMES = ("sk", "sv", "sq", "ck", "cv", "so", "cq", "co", "fg", "fu", "fd")


def bucket_starts():
    exact = BUCKETS // 2
    far = np.ceil(exact * (MAX_DIST / exact) ** (np.arange(1, exact) / exact))
    return [*range(1, exact + 1), *(int(value) for value in far)]


def dot(left, right):
    return jnp.dot(left, right, preferred_element_type=F32)


def dot_nt(left, right):
    return lax.dot_general(left, right, (((1,), (1,)), ((), ())), preferred_element_type=F32)


def lane_tiles(width, step=512):
    return [(first, min(step, width - first)) for first in range(0, width, step)]


def layer_kernel(shapes, stop, *refs):
    bits, rows, width, groups, mem_rows = shapes
    stages = bits + 1
    blk_count = 1 << bits
    pairs = groups // 2
    half_count = blk_count // 2
    long = half_count > 4
    refs = list(refs)

    def take(count):
        taken, refs[:count] = refs[:count], []
        return taken

    lengths, rel_bias, hidden, out_grad, ln_self, ln_cross, ln_ffn, memory_in = take(8)
    weights_in = dict(zip(NAMES, take(11)))
    layer_out, hidden_grad, memory_grad = take(3)
    grads_out = dict(zip(NAMES, take(11)))
    (small_out,) = take(1)
    weight = dict(zip(NAMES, take(11)))
    landing = {name: take(stages) for name in NAMES}
    (memory, kbuf, vbuf, vT, kT, tab, near, scores, qs, cqs, ags, att_self, att_cross) = take(13)
    (lse, probs, mk, mv, mkT, mvT, pushed, landed) = take(8)
    (after_self, after_cross, cot, ns, ns_t, nc, nc_t, nf, nf_t, bg, bg_t) = take(11)
    (att_tok, catt_tok, inner, gate_grad, up_grad, qgrad) = take(6)
    (dkv,) = take(1)
    dkv_land = take(bits)
    (dmem,) = take(1)
    dmem_land = take(bits)
    (mem_push, mem_land, small, small_land, bias_sum) = take(5)
    (load_sem, hx_send, hx_recv, ag_send, ag_recv, rs_send, rs_recv) = take(7)
    (dk_send, dk_recv, dm_send, dm_recv, mg_send, mg_recv, sm_send, sm_recv) = take(8)

    seq, blk, head = (lax.axis_index(name) for name in ("seq", "blk", "head"))
    mine = [lax.rem(blk // (1 << bit), 2) for bit in range(bits)]

    def across(bit):
        return (seq, blk + (1 - 2 * mine[bit]) * (1 << bit), head)

    other_seq = (1 - seq, blk, head)
    other_head = (seq, blk, 1 - head)

    loads = {
        name: pltpu.make_async_copy(weights_in[name], weight[name], load_sem.at[slot])
        for slot, name in enumerate(NAMES)
    }
    memory_load = pltpu.make_async_copy(memory_in, memory, load_sem.at[len(NAMES)])
    for name in ("sk", "sv", "sq"):
        loads[name].start()
    memory_load.start()
    for name in NAMES[3:]:
        loads[name].start()

    barrier = pltpu.get_barrier_semaphore()
    friends = [other_seq, other_head, *(across(bit) for bit in range(bits))]
    for friend in friends:
        pl.semaphore_signal(barrier, inc=1, device_id=friend, device_id_type=MESH)

    def whole(name, lanes=slice(None)):
        value = weight[name][(Ellipsis, lanes)]
        return value.reshape(width, value.shape[-1])

    def row_tile(name, tile):
        value = weight[name][tile // 2, tile % 2]
        return value.reshape(TILE, value.shape[-1])

    def inverse_norm(values):
        return lax.rsqrt(jnp.mean(values * values, axis=-1, keepdims=True) + EPSILON)

    def norm_into(values, gain, plain, turned):
        result = (values * inverse_norm(values) * gain[...]).astype(BF)
        plain[...] = result
        turned[...] = result.T

    def norm_back(values, gain, normed_grad, slot):
        scale = inverse_norm(values)
        unit = values * scale
        unit_grad = normed_grad * gain[...]
        line = jnp.sum(normed_grad * unit, axis=0, keepdims=True)
        for tile in range(width // 128):
            small[0, slot * (width // 128) + tile : slot * (width // 128) + tile + 1, :] = line[
                :, tile * 128 : (tile + 1) * 128
            ]
        return scale * (unit_grad - unit * jnp.mean(unit_grad * unit, axis=-1, keepdims=True))

    def hx(which, tile):
        return pltpu.make_async_remote_copy(
            src_ref=pushed.at[which, tile],
            dst_ref=landed.at[which, tile],
            send_sem=hx_send.at[which, tile],
            recv_sem=hx_recv.at[which, tile],
            device_id=other_head,
            device_id_type=MESH,
        )

    def push(which, tile, value):
        pushed[which, tile] = value.astype(BF)
        hx(which, tile).start()

    def summed(which, tile):
        hx(which, tile).wait_recv()
        return pushed[which, tile].astype(F32) + landed[which, tile].astype(F32)

    tiles = width // TILE

    def summed_all(which):
        return jnp.concatenate([summed(which, tile) for tile in range(tiles)], axis=1)

    def bit_order(name):
        if name in ("fd", "cq", "sq"):
            return [*range(1, bits), 0]
        return list(range(bits))

    def bit_view(order, stage, keep):
        index = []
        for bit in reversed(range(bits)):
            place = order.index(bit)
            if place < stage:
                index.append(mine[bit])
            elif place == stage:
                index.append(mine[bit] if keep else 1 - mine[bit])
            else:
                index.append(slice(None))
        return tuple(index)

    def rs_view(name, stage, keep):
        if stage == 0:
            return weight[name].at[seq if keep else 1 - seq]
        return weight[name].at[(seq, *bit_view(bit_order(name), stage - 1, keep))]

    def rs_copy(name, stage):
        slot = NAMES.index(name)
        target = other_seq if stage == 0 else across(bit_order(name)[stage - 1])
        return pltpu.make_async_remote_copy(
            src_ref=rs_view(name, stage, False),
            dst_ref=landing[name][stage],
            send_sem=rs_send.at[slot, stage],
            recv_sem=rs_recv.at[slot, stage],
            device_id=target,
            device_id_type=MESH,
        )

    def rs_start(name):
        rs_copy(name, 0).start()

    def fold_into(kept, got):
        lead = got.shape[:-2]
        total = int(np.prod(lead))

        def body(flat, carry):
            index, left = [], flat
            for extent in reversed(lead):
                index.append(lax.rem(left, extent))
                left = left // extent
            index = tuple(reversed(index))
            kept[index] = (kept[index].astype(F32) + got[index].astype(F32)).astype(BF)
            return carry

        if total == 1:
            kept[...] = (kept[...].astype(F32) + got[...].astype(F32)).astype(BF)
        else:
            lax.fori_loop(0, total, body, 0)

    def rs_step(name, stage):
        rs_copy(name, stage).wait_recv()
        kept, got = rs_view(name, stage, True), landing[name][stage]
        if stage == stages - 1:
            grads_out[name][...] = kept[...].astype(F32) + got[...].astype(F32)
        else:
            fold_into(kept, got)
            rs_copy(name, stage + 1).start()

    def part_copy(buffer, land, send, recv, stage):
        order = list(range(bits))
        return pltpu.make_async_remote_copy(
            src_ref=buffer.at[bit_view(order, stage, False)],
            dst_ref=land[stage],
            send_sem=send.at[stage],
            recv_sem=recv.at[stage],
            device_id=across(order[stage]),
            device_id_type=MESH,
        )

    def part_step(buffer, land, send, recv, stage):
        order = list(range(bits))
        part_copy(buffer, land, send, recv, stage).wait_recv()
        kept = buffer.at[bit_view(order, stage, True)]
        if stage == bits - 1:
            return kept[...].astype(F32) + land[stage][...].astype(F32)
        fold_into(kept, land[stage])
        part_copy(buffer, land, send, recv, stage + 1).start()

    def dkv_args(pair):
        return (
            dkv.at[pair],
            [land.at[pair] for land in dkv_land],
            dk_send.at[pair],
            dk_recv.at[pair],
        )

    dmem_args = (dmem, dmem_land, dm_send, dm_recv)

    def ag_copy(which, step):
        bit = bits - 1 - step
        index = (slice(None),) + tuple(
            slice(None) if place > bit else mine[place] for place in reversed(range(bits))
        )
        buffer = (kbuf, vbuf)[which]
        return pltpu.make_async_remote_copy(
            src_ref=buffer.at[index],
            dst_ref=buffer.at[index],
            send_sem=ag_send.at[which, step],
            recv_sem=ag_recv.at[which, step],
            device_id=across(bit),
            device_id_type=MESH,
        )

    def ag_next(step):
        for which in range(2):
            ag_copy(which, step).wait_recv()
            if step + 1 < bits:
                ag_copy(which, step + 1).start()

    def half_index(chunk):
        index, left = [], chunk
        for _ in range(bits - 1):
            index.append(left % 2 if isinstance(left, int) else lax.rem(left, 2))
            left = left // 2
        return tuple(reversed(index))

    def chunk_of(buffer, pair, chunk):
        return buffer[(pair, *half_index(chunk))].reshape(2 * rows, 128)

    lane = lax.broadcasted_iota(jnp.int32, (rows, 128), 1)
    low = lane < HEAD_DIM
    swap_row = lax.broadcasted_iota(jnp.int32, (128, 128), 0)
    swap_col = lax.broadcasted_iota(jnp.int32, (128, 128), 1)
    swap = (swap_row == lax.rem(swap_col + HEAD_DIM, 128)).astype(F32).astype(BF)

    def split_heads(values, target):
        for group in range(groups):
            tile = values[:, group * 128 : (group + 1) * 128]
            swapped = dot(tile, swap)
            plain = tile.astype(F32)
            first, second = (plain, swapped) if group % 2 == 0 else (swapped, plain)
            here = low if group % 2 == 0 else jnp.logical_not(low)
            target[group, :rows, :] = jnp.where(here, first, 0.0).astype(BF)
            target[group, rows:, :] = jnp.where(here, second, 0.0).astype(BF)

    def join_heads(values):
        return jnp.concatenate([values[:, :rows], values[:, rows:]], axis=0).T

    def head_deltas(values, attended, group):
        turned = values[:, group * 128 : (group + 1) * 128].astype(F32).T
        laid = jnp.concatenate([turned[:HEAD_DIM, :], turned[HEAD_DIM:, :]], axis=1)
        return jnp.sum(laid * attended[group], axis=0, keepdims=True)

    length = lengths[0]
    key_row = lax.broadcasted_iota(jnp.int32, (rows, 2 * rows), 0)

    def kind_of(block):
        return jnp.clip(block - blk + 2, 0, 3)

    def self_scores(group, chunk):
        raw = dot_nt(chunk_of(kbuf, group // 2, chunk), qs[group])
        parts = []
        for inner_block in range(2):
            block = 2 * chunk + inner_block
            part = raw[inner_block * rows : (inner_block + 1) * rows, :]
            part = part + tab[kind_of(block), group]
            parts.append(jnp.where(key_row + block * rows < length, part, MASKED))
        return jnp.concatenate(parts, axis=0)

    x = hidden[...].astype(F32)
    norm_into(x, ln_self, ns, ns_t)
    loads["sk"].wait()
    keys = dot(ns[...], whole("sk")).astype(BF)
    for pair in range(pairs):
        kbuf[(pair, *reversed(mine))] = keys[:, pair * 128 : (pair + 1) * 128]
    pl.semaphore_wait(barrier, len(friends))
    ag_copy(0, 0).start()
    loads["sv"].wait()
    values = dot(ns[...], whole("sv")).astype(BF)
    for pair in range(pairs):
        vbuf[(pair, *reversed(mine))] = values[:, pair * 128 : (pair + 1) * 128]
    ag_copy(1, 0).start()
    loads["sq"].wait()
    split_heads(dot(ns[...], whole("sq")).astype(BF), qs)
    ag_next(0)

    memory_load.wait()
    for source, plain, turned in (("ck", mk, mkT), ("cv", mv, mvT)):
        loads[source].wait()
        result = dot(memory[...], whole(source)).astype(BF)
        for pair in range(pairs):
            plain[pair] = result[:, pair * 128 : (pair + 1) * 128]
            turned[pair * 128 : (pair + 1) * 128, :] = result[:, pair * 128 : (pair + 1) * 128].T
    if bits > 1:
        ag_next(1)

    starts = bucket_starts()
    distance = lane - lax.broadcasted_iota(jnp.int32, (rows, 128), 0)

    def bias_of(which, head_slot):
        shifted = distance + (rows if which == 1 else 0)
        value = jnp.full((rows, 128), rel_bias[0, head_slot], F32)
        for bucket, start in enumerate(starts):
            value = jnp.where(shifted >= start, rel_bias[bucket + 1, head_slot], value)
        if which == 2:
            value = jnp.where(shifted >= 0, value, MASKED)
        return value

    def bias_tables(head_slot, carry):
        group = head_slot // 2
        lanes = pl.ds(pl.multiple_of(lax.rem(head_slot, 2) * rows, rows), rows)
        tab[0, group, :, lanes] = jnp.full((rows, rows), rel_bias[BUCKETS - 1, head_slot], F32)
        tab[1, group, :, lanes] = bias_of(1, head_slot)
        tab[2, group, :, lanes] = bias_of(2, head_slot)
        tab[3, group, :, lanes] = jnp.full((rows, rows), MASKED, F32)
        return carry

    lax.fori_loop(0, 2 * groups, bias_tables, 0)
    for step in range(2, bits):
        ag_next(step)

    def turn_chunk(chunk):
        for pair in range(pairs):
            vT[chunk, pair * 128 : (pair + 1) * 128, :] = chunk_of(vbuf, pair, chunk).T
            kT[chunk, pair * 128 : (pair + 1) * 128, :] = chunk_of(kbuf, pair, chunk).T

    if not long:
        for chunk in range(half_count):
            turn_chunk(chunk)

    def turned_of(kept, buffer, group, chunk):
        if not long:
            return kept[chunk, group * HEAD_DIM : (group + 1) * HEAD_DIM, :]
        first = (group % 2) * HEAD_DIM
        return chunk_of(buffer, group // 2, chunk).T[first : first + HEAD_DIM, :]

    def attend(group):
        tops = jnp.full((1, 2 * rows), MASKED, F32)

        def first_pass(chunk, top):
            part = self_scores(group, chunk)
            if not long:
                scores[group % 2, chunk] = part
            return jnp.maximum(top, jnp.max(part, axis=0, keepdims=True))

        def second_pass(chunk, state):
            total, acc = state
            part = self_scores(group, chunk) if long else scores[group % 2, chunk]
            part = jnp.exp(part - tops)
            total = total + jnp.sum(part, axis=0, keepdims=True)
            return total, acc + dot(turned_of(vT, vbuf, group, chunk), part.astype(BF))

        state = (jnp.zeros((1, 2 * rows), F32), jnp.zeros((HEAD_DIM, 2 * rows), F32))
        if not long:
            for chunk in range(half_count):
                tops = first_pass(chunk, tops)
            for chunk in range(half_count):
                state = second_pass(chunk, state)
        else:
            tops = lax.fori_loop(0, half_count, first_pass, tops)
            state = lax.fori_loop(0, half_count, second_pass, state)
        total, acc = state
        precise = acc / total
        att_self[group] = precise
        lse[group] = tops + jnp.log(total)
        att_tok[:, group * 128 : (group + 1) * 128] = join_heads(precise).astype(BF)

    for group in range(groups):
        attend(group)

    loads["so"].wait()
    for tile in range(tiles):
        push(0, tile, dot_nt(att_tok[...], row_tile("so", tile)))
    valid = lax.broadcasted_iota(jnp.int32, (rows, 1), 0) + blk * rows < length
    bg[...] = jnp.where(valid, out_grad[...].astype(F32), 0.0).astype(BF)
    bg_t[...] = bg[...].T
    after_self[...] = x + summed_all(0)

    norm_into(after_self[...], ln_cross, nc, nc_t)
    loads["cq"].wait()
    split_heads(dot(nc[...], whole("cq")).astype(BF), cqs)
    for group in range(groups):
        part = dot_nt(mk[group // 2], cqs[group])
        part = jnp.exp(part - jnp.max(part, axis=0, keepdims=True))
        part = part * (1.0 / jnp.sum(part, axis=0, keepdims=True))
        probs[group] = part
        acc = dot(mvT[group * HEAD_DIM : (group + 1) * HEAD_DIM, :], part.astype(BF))
        att_cross[group] = acc
        catt_tok[:, group * 128 : (group + 1) * 128] = join_heads(acc).astype(BF)
    loads["co"].wait()
    for tile in range(tiles):
        push(1, tile, dot_nt(catt_tok[...], row_tile("co", tile)))
    after_cross[...] = after_self[...] + summed_all(1)

    norm_into(after_cross[...], ln_ffn, nf, nf_t)
    for name in ("fg", "fu", "fd"):
        loads[name].wait()
    for first, size in lane_tiles(inner.shape[1]):
        lanes = slice(first, first + size)
        gate = dot(nf[...], whole("fg", lanes))
        up = dot(nf[...], whole("fu", lanes))
        back = dot(bg[...], whole("fd", lanes))
        bent = jnp.tanh(GELU_A * (gate + GELU_B * gate * gate * gate))
        share = 0.5 * (1.0 + bent)
        slope = share + 0.5 * gate * (1.0 - bent * bent) * (
            GELU_A * (1.0 + 3.0 * GELU_B * gate * gate)
        )
        bell = gate * share
        inner[:, lanes] = (bell * up).astype(BF)
        gate_grad[:, lanes] = (back * up * slope).astype(BF)
        up_grad[:, lanes] = (back * bell).astype(BF)
    for tile in range(tiles):
        push(
            2,
            tile,
            dot_nt(gate_grad[...], row_tile("fg", tile)) + dot_nt(up_grad[...], row_tile("fu", tile)),
        )
    for tile in range(tiles):
        push(3, tile, dot_nt(inner[...], row_tile("fd", tile)))

    def weight_grad(name, turned, right):
        for first, size in lane_tiles(right.shape[1]):
            lanes = slice(first, first + size)
            for tile in range(tiles):
                result = dot(turned[tile * TILE : (tile + 1) * TILE, :], right[:, lanes]).astype(BF)
                shape = weight[name].shape[2:-1]
                weight[name][(tile // 2, tile % 2, Ellipsis, lanes)] = result.reshape(*shape, size)
        rs_start(name)

    weight_grad("fd", bg_t, inner)
    weight_grad("fg", nf_t, gate_grad)
    weight_grad("fu", nf_t, up_grad)
    normed_grad = summed_all(2)
    cot[...] = jnp.where(valid, out_grad[...].astype(F32), 0.0) + norm_back(
        after_cross[...], ln_ffn, normed_grad, 2
    )
    bg[...] = cot[...].astype(BF)
    bg_t[...] = bg[...].T

    for name in ("fd", "fg", "fu"):
        rs_step(name, 0)
    back = dot(bg[...], whole("co")).astype(BF)
    split_heads(back, ags)
    for pair in range(pairs):
        key_part = value_part = None
        for group in (2 * pair, 2 * pair + 1):
            prob = probs[group]
            prob_grad = dot_nt(mv[pair], ags[group])
            score_grad = (prob * (prob_grad - head_deltas(back, att_cross, group))).astype(BF)
            turned = dot(mkT[group * HEAD_DIM : (group + 1) * HEAD_DIM, :], score_grad)
            qgrad[:, group * 128 : (group + 1) * 128] = join_heads(turned).astype(BF)
            key_new = dot(score_grad, cqs[group])
            value_new = dot(prob.astype(BF), ags[group])
            key_part = key_new if key_part is None else key_part + key_new
            value_part = value_new if value_part is None else value_part + value_new
        shape = dmem.shape[:-1]
        dmem[..., pair * 128 : (pair + 1) * 128] = key_part.astype(BF).reshape(*shape, 128)
        dmem[..., (pairs + pair) * 128 : (pairs + pair + 1) * 128] = value_part.astype(BF).reshape(
            *shape, 128
        )
    for tile in range(tiles):
        push(4, tile, dot_nt(qgrad[...], row_tile("cq", tile)))
    part_copy(*dmem_args, 0).start()
    weight_grad("co", bg_t, catt_tok)
    weight_grad("cq", nc_t, qgrad)
    for tile in range(tiles):
        lanes = slice(tile * TILE, (tile + 1) * TILE)
        layer_out[:, lanes] = (after_cross[:, lanes] + summed(3, tile)).astype(BF)
    normed_grad = summed_all(4)
    cot[...] = cot[...] + norm_back(after_self[...], ln_cross, normed_grad, 1)
    bg[...] = cot[...].astype(BF)
    bg_t[...] = bg[...].T

    back = dot(bg[...], whole("so")).astype(BF)
    split_heads(back, ags)
    part_step(*dmem_args, 0)
    rs_step("fg", 1)
    rs_step("fd", 1)
    near[1] = jnp.zeros(near.shape[1:], BF)
    for name in ("co", "cq"):
        rs_step(name, 0)
    for pair in range(pairs):
        members = (2 * pair, 2 * pair + 1)
        deltas = [head_deltas(back, att_self, group) for group in members]

        def visit(chunk, state, pair=pair, members=members, deltas=deltas):
            state = list(state)
            key_part = value_part = None
            values_here = chunk_of(vbuf, pair, chunk)
            for slot, group in enumerate(members):
                prob = jnp.exp(self_scores(group, chunk) - lse[group])
                prob_grad = dot_nt(values_here, ags[group])
                score_grad = (prob * (prob_grad - deltas[slot])).astype(BF)
                lhs = turned_of(kT, kbuf, group, chunk)
                state[2 * slot] = state[2 * slot] + dot(lhs, score_grad)
                key_new = dot(score_grad, qs[group])
                value_new = dot(prob.astype(BF), ags[group])
                key_part = key_new if key_part is None else key_part + key_new
                value_part = value_new if value_part is None else value_part + value_new
                for inner_block in range(2):
                    kind = kind_of(2 * chunk + inner_block)
                    piece = score_grad[inner_block * rows : (inner_block + 1) * rows, :]
                    near[lax.rem(kind, 3), group] = piece
                    is_far = (kind == 0).astype(F32)
                    state[2 * slot + 1] = state[2 * slot + 1] + is_far * jnp.sum(
                        piece.astype(F32), axis=0, keepdims=True
                    )
            where_to = (pair, *half_index(chunk))
            dkv[(*where_to, slice(None), slice(None), slice(0, 128))] = key_part.astype(BF).reshape(
                2, rows, 128
            )
            dkv[(*where_to, slice(None), slice(None), slice(128, 256))] = value_part.astype(
                BF
            ).reshape(2, rows, 128)
            return tuple(state)

        state = (jnp.zeros((HEAD_DIM, 2 * rows), F32), jnp.zeros((1, 2 * rows), F32)) * 2
        if not long:
            for chunk in range(half_count):
                state = visit(chunk, state)
        else:
            state = lax.fori_loop(0, half_count, visit, state)
        part_copy(*dkv_args(pair), 0).start()
        for slot, group in enumerate(members):
            qgrad[:, group * 128 : (group + 1) * 128] = join_heads(state[2 * slot]).astype(BF)
            bias_sum[BUCKETS : BUCKETS + 1, group * 2 * rows : (group + 1) * 2 * rows] = state[
                2 * slot + 1
            ]
    part_step(*dkv_args(0), 0)
    part_step(*dmem_args, 1)
    weight_grad("so", bg_t, att_tok)
    rs_step("fu", 1)
    part_step(*dkv_args(1), 0)
    rs_step("fg", 2)
    mem_sum = None
    for step in range(2, bits):
        mem_sum = part_step(*dmem_args, step)
    for step in range(1, bits - 1):
        part_step(*dkv_args(0), step)
    query_part = [
        dot_nt(qgrad[...], row_tile("sq", tile)) for tile in range(tiles)
    ]
    weight_grad("sq", ns_t, qgrad)
    for step in range(1, bits - 1):
        part_step(*dkv_args(1), step)
    sums = [part_step(*dkv_args(pair), bits - 1).astype(BF) for pair in range(pairs)]
    kgrad = jnp.concatenate([value[:, :128] for value in sums], axis=1)
    vgrad = jnp.concatenate([value[:, 128:] for value in sums], axis=1)
    for tile in range(tiles):
        push(
            5,
            tile,
            query_part[tile]
            + dot_nt(kgrad, row_tile("sk", tile))
            + dot_nt(vgrad, row_tile("sv", tile)),
        )
    weight_grad("sk", ns_t, kgrad)
    weight_grad("sv", ns_t, vgrad)

    share = mem_rows // blk_count
    mem_sum = mem_sum.astype(BF)
    mkg, mvg = mem_sum[:, : pairs * 128], mem_sum[:, pairs * 128 :]
    mem_part = dot_nt(mkg, whole("ck")) + dot_nt(mvg, whole("cv"))
    half = share // 2
    mem_push[0] = mem_part[:half, :].astype(BF)
    mem_push[1] = mem_part[half:, :].astype(BF)
    mem_copy = pltpu.make_async_remote_copy(
        src_ref=mem_push.at[1 - head],
        dst_ref=mem_land,
        send_sem=mg_send,
        recv_sem=mg_recv,
        device_id=other_head,
        device_id_type=MESH,
    )
    mem_copy.start()
    own_rows = memory[pl.ds(pl.multiple_of(blk * share, share), share), :]
    own_turned = own_rows.T
    weight_grad("ck", own_turned, mkg)
    weight_grad("cv", own_turned, mvg)

    def bucket_line(group, lower, upper):
        line = jnp.zeros((1, 2 * rows), F32)
        wide = jnp.concatenate([distance, distance], axis=1)
        for kind in (1, 2):
            shifted = wide + (rows if kind == 1 else 0)
            here = shifted >= lower
            if upper is not None:
                here = jnp.logical_and(here, shifted < upper)
            piece = near[kind, group].astype(F32)
            line = line + jnp.sum(jnp.where(here, piece, 0.0), axis=0, keepdims=True)
        return line

    bounds = [0, *starts, None]
    for group in range(groups):
        lanes = slice(group * 2 * rows, (group + 1) * 2 * rows)
        for bucket in range(BUCKETS):
            line = bucket_line(group, bounds[bucket], bounds[bucket + 1])
            if bucket == BUCKETS - 1:
                line = line + bias_sum[BUCKETS : BUCKETS + 1, lanes]
            bias_sum[bucket : bucket + 1, lanes] = line
    bias_lane = lax.broadcasted_iota(jnp.int32, (BUCKETS, 128), 1)
    bias_grad = jnp.zeros((BUCKETS, 128), F32)
    for head_slot in range(2 * groups):
        column = jnp.sum(
            bias_sum[:BUCKETS, head_slot * rows : (head_slot + 1) * rows], axis=1, keepdims=True
        )
        bias_grad = jnp.where(bias_lane == head_slot, column, bias_grad)
    first_bias = 3 * (width // 128)
    small[0, first_bias : first_bias + BUCKETS, :] = bias_grad

    normed_grad = summed_all(5)
    hidden_grad[...] = cot[...] + norm_back(hidden[...].astype(F32), ln_self, normed_grad, 0)

    def small_copy(stage):
        return pltpu.make_async_remote_copy(
            src_ref=small.at[stage],
            dst_ref=small_land.at[stage],
            send_sem=sm_send.at[stage],
            recv_sem=sm_recv.at[stage],
            device_id=other_seq if stage == 0 else across(stage - 1),
            device_id_type=MESH,
        )

    small_copy(0).start()
    done = {"fd": 2, "fg": 3, "fu": 2, "co": 1, "cq": 1}
    order = ("fu", "fd", "fg", "co", "cq", "so", "sq", "sk", "sv", "ck", "cv")
    for sweep in range(stages):
        small_copy(sweep).wait_recv()
        total = small[sweep] + small_land[sweep]
        if sweep < stages - 1:
            small[sweep + 1] = total
            small_copy(sweep + 1).start()
        else:
            small_out[...] = total
        for name in order:
            at = done.get(name, 0)
            if at < stages:
                rs_step(name, at)
                done[name] = at + 1
    mem_copy.wait_recv()
    memory_grad[...] = mem_push[head].astype(F32) + mem_land[...].astype(F32)

    for name in NAMES:
        for stage in range(stages):
            rs_copy(name, stage).wait_send()
    for stage in range(stages):
        small_copy(stage).wait_send()
    for which in range(6):
        for tile in range(tiles):
            hx(which, tile).wait_send()
    for which in range(2):
        for step in range(bits):
            ag_copy(which, step).wait_send()
    for step in range(bits):
        part_copy(*dmem_args, step).wait_send()
        for pair in range(pairs):
            part_copy(*dkv_args(pair), step).wait_send()
    mem_copy.wait_send()


def run_layer(lengths, rel_bias, hidden, out_grad, gains, memory, weights, blk_count, stop=None):
    bits = blk_count.bit_length() - 1
    stages = bits + 1
    rows, width = hidden.shape
    groups = weights["sk"].shape[1] // HEAD_DIM
    heads = weights["sq"].shape[1] // HEAD_DIM
    mem_rows = memory.shape[0]
    if rows != 128 or heads != 2 * groups or bucket_starts()[-1] > rows or 1 << bits != blk_count:
        raise ValueError("unexpected sizes")
    pairs = groups // 2
    half_count = blk_count // 2
    stored = 1 if half_count > 4 else half_count
    piece = width // (2 * blk_count)
    lead = (2,) * (bits + 1)
    widths = {name: weights[name].shape[1] for name in NAMES}
    shaped = [weights[name].reshape(*lead, piece, widths[name]) for name in NAMES]
    units = widths["fg"]
    share = mem_rows // blk_count
    small_rows = 3 * (width // 128) + BUCKETS

    vm, sem = pltpu.VMEM, pltpu.SemaphoreType.DMA
    scratch = [vm((*lead, piece, widths[name]), BF) for name in NAMES]
    for name in NAMES:
        for stage in range(stages):
            scratch.append(vm((2,) * (bits - stage) + (piece, widths[name]), BF))
    by_bit = (2,) * bits
    scratch += [
        vm(memory.shape, BF),
        vm((pairs, *by_bit, rows, 128), BF),
        vm((pairs, *by_bit, rows, 128), BF),
        vm((stored, groups * HEAD_DIM, 2 * rows), BF),
        vm((stored, groups * HEAD_DIM, 2 * rows), BF),
        vm((4, groups, rows, 2 * rows), F32),
        vm((3, groups, rows, 2 * rows), BF),
        vm((2, stored, 2 * rows, 2 * rows), F32),
        vm((groups, 2 * rows, 128), BF),
        vm((groups, 2 * rows, 128), BF),
        vm((groups, 2 * rows, 128), BF),
        vm((groups, HEAD_DIM, 2 * rows), F32),
        vm((groups, HEAD_DIM, 2 * rows), F32),
        vm((groups, 1, 2 * rows), F32),
        vm((groups, mem_rows, 2 * rows), F32),
        vm((pairs, mem_rows, 128), BF),
        vm((pairs, mem_rows, 128), BF),
        vm((groups * HEAD_DIM, mem_rows), BF),
        vm((groups * HEAD_DIM, mem_rows), BF),
        vm((6, width // TILE, rows, TILE), BF),
        vm((6, width // TILE, rows, TILE), BF),
        vm((rows, width), F32),
        vm((rows, width), F32),
        vm((rows, width), F32),
        vm((rows, width), BF),
        vm((width, rows), BF),
        vm((rows, width), BF),
        vm((width, rows), BF),
        vm((rows, width), BF),
        vm((width, rows), BF),
        vm((rows, width), BF),
        vm((width, rows), BF),
        vm((rows, heads * HEAD_DIM), BF),
        vm((rows, heads * HEAD_DIM), BF),
        vm((rows, units), BF),
        vm((rows, units), BF),
        vm((rows, units), BF),
        vm((rows, heads * HEAD_DIM), BF),
        vm((pairs, *by_bit, rows, 256), BF),
    ]
    scratch += [vm((pairs, *(2,) * (bits - 1 - stage), rows, 256), BF) for stage in range(bits)]
    scratch += [vm((*by_bit, share, 2 * groups * HEAD_DIM), BF)]
    scratch += [
        vm((*(2,) * (bits - 1 - stage), share, 2 * groups * HEAD_DIM), BF) for stage in range(bits)
    ]
    scratch += [
        vm((2, share // 2, width), BF),
        vm((share // 2, width), BF),
        vm((stages, small_rows, 128), F32),
        vm((stages, small_rows, 128), F32),
        vm((BUCKETS + 8, heads * rows), F32),
        sem((len(NAMES) + 1,)),
        sem((6, width // TILE)),
        sem((6, width // TILE)),
        sem((2, bits)),
        sem((2, bits)),
        sem((len(NAMES), stages)),
        sem((len(NAMES), stages)),
        sem((pairs, bits)),
        sem((pairs, bits)),
        sem((bits,)),
        sem((bits,)),
        sem,
        sem,
        sem((stages,)),
        sem((stages,)),
    ]
    in_vmem = pl.BlockSpec(memory_space=pltpu.VMEM)
    in_smem = pl.BlockSpec(memory_space=pltpu.SMEM)
    in_any = pl.BlockSpec(memory_space=pl.ANY)
    out_shape = [
        jax.ShapeDtypeStruct((rows, width), BF),
        jax.ShapeDtypeStruct((rows, width), F32),
        jax.ShapeDtypeStruct((share // 2, width), F32),
        *(jax.ShapeDtypeStruct((piece, widths[name]), F32) for name in NAMES),
        jax.ShapeDtypeStruct((small_rows, 128), F32),
    ]
    results = pl.pallas_call(
        functools.partial(layer_kernel, (bits, rows, width, groups, mem_rows), stop),
        out_shape=out_shape,
        in_specs=[in_smem, in_smem, *[in_vmem] * 5, *[in_any] * 12],
        out_specs=[in_vmem] * len(out_shape),
        scratch_shapes=scratch,
        compiler_params=pltpu.CompilerParams(
            collective_id=0, has_side_effects=True, vmem_limit_bytes=62 * 1024 * 1024
        ),
        name="layer",
    )(lengths, rel_bias, hidden, out_grad, *gains, memory, *shaped)
    return results[:3], dict(zip(NAMES, results[3:-1])), results[-1]


def body(
    hidden,
    memory,
    lengths,
    out_grad,
    ln_self,
    self_query,
    self_key,
    self_value,
    self_out,
    rel_bias,
    ln_cross,
    cross_query,
    cross_key,
    cross_value,
    cross_out,
    ln_ffn,
    ffn_gate,
    ffn_up,
    feedforward_down_weight,
):
    width = hidden.shape[1]
    blk_count = lax.axis_size("blk")
    weights = dict(
        sk=self_key,
        sv=self_value,
        sq=self_query,
        ck=cross_key,
        cv=cross_value,
        so=self_out,
        cq=cross_query,
        co=cross_out,
        fg=ffn_gate,
        fu=ffn_up,
        fd=feedforward_down_weight,
    )
    gains = [gain.reshape(1, width) for gain in (ln_self, ln_cross, ln_ffn)]
    (layer_out, hidden_grad, memory_grad), grads, small = run_layer(
        lengths, rel_bias, hidden, out_grad, gains, memory, weights, blk_count
    )
    lines = width // 128
    share = width // (2 * blk_count)
    first = (lax.axis_index("seq") * blk_count + lax.axis_index("blk")) * share
    gain_grads = lax.dynamic_slice(small[: 3 * lines].reshape(3, width), (0, first), (3, share))
    bias_grad = small[3 * lines :, : rel_bias.shape[1]]
    return (
        layer_out,
        hidden_grad,
        memory_grad,
        gain_grads[0],
        grads["sq"],
        grads["sk"],
        grads["sv"],
        grads["so"],
        bias_grad,
        gain_grads[1],
        grads["cq"],
        grads["ck"],
        grads["cv"],
        grads["co"],
        gain_grads[2],
        grads["fg"],
        grads["fu"],
        grads["fd"],
    )


def solution(mesh):
    blocks = P(("seq", "blk"), None)
    by_head = P(None, "head")
    shares = P(("seq", "blk"), "head")
    line = P(("seq", "blk"))
    in_specs = (
        blocks,
        P("seq", None),
        P("seq"),
        blocks,
        P(),
        *[by_head] * 5,
        P(),
        *[by_head] * 4,
        P(),
        *[by_head] * 3,
    )
    out_specs = (
        blocks,
        blocks,
        P(("seq", "blk", "head"), None),
        line,
        *[shares] * 4,
        by_head,
        line,
        *[shares] * 4,
        line,
        *[shares] * 3,
    )
    return jax.shard_map(body, mesh=mesh, in_specs=in_specs, out_specs=out_specs, check_vma=False)
```

```python
import functools

import jax
import jax.numpy as jnp
import numpy as np
from jax import lax
from jax.experimental import pallas as pl
from jax.experimental.pallas import tpu as pltpu
from jax.sharding import PartitionSpec as P

MESH = pl.DeviceIdType.MESH
HEAD_DIM = 64
BUCKETS = 32
MAX_DIST = 128
EPSILON = 1e-06
MASKED = -1e30
BF = jnp.bfloat16
F32 = jnp.float32
TILE = 256
GELU_A = float(np.sqrt(2.0 / np.pi))
GELU_B = 0.044715

NAMES = ("sk", "sv", "sq", "ck", "cv", "so", "cq", "co", "fg", "fu", "fd")
LEFTS = ("ns", "nc", "nf", "gf", "gc", "gs", "mem")
LEFT_OF = dict(
    sk="ns", sv="ns", sq="ns", cq="nc", fg="nf", fu="nf", fd="gf", co="gc", so="gs", ck="mem", cv="mem"
)


def bucket_starts():
    exact = BUCKETS // 2
    far = np.ceil(exact * (MAX_DIST / exact) ** (np.arange(1, exact) / exact))
    return [*range(1, exact + 1), *(int(value) for value in far)]


def dot(left, right):
    return jnp.dot(left, right, preferred_element_type=F32)


def dot_nt(left, right):
    return lax.dot_general(left, right, (((1,), (1,)), ((), ())), preferred_element_type=F32)


def lane_tiles(width, step=512):
    return [(first, min(step, width - first)) for first in range(0, width, step)]


class Stop(Exception):
    pass


class Copies:
    def __init__(self):
        self.made, self.started, self.received, self.sent = {}, [], set(), set()

    def start(self, key, copy):
        self.made[key] = copy
        self.started.append(key)
        copy.start()

    def receive(self, key):
        self.received.add(key)
        copy = self.made[key]
        if key[0] == "load":
            copy.wait()
        else:
            copy.wait_recv()

    def drain(self):
        for key in self.started:
            if key not in self.received:
                self.receive(key)
        for key in self.started:
            if key[0] != "load":
                self.made[key].wait_send()


def layer_kernel(shapes, stop, *refs):
    copies = Copies()
    try:
        layer_steps(copies, shapes, stop, *refs)
    except Stop:
        pass
    copies.drain()


def layer_steps(copies, shapes, stop, *refs):
    bits, rows, width, groups, mem_rows = shapes
    stages = bits + 1
    blk_count = 1 << bits
    pairs = groups // 2
    half_count = blk_count // 2
    long = half_count > 4
    refs = list(refs)

    def take(count):
        taken, refs[:count] = refs[:count], []
        return taken

    lengths, rel_bias, hidden, out_grad, ln_self, ln_cross, ln_ffn, memory_in = take(8)
    weights_in = dict(zip(NAMES, take(11)))
    layer_out, hidden_grad, memory_grad = take(3)
    grads_out = dict(zip(NAMES, take(11)))
    results = {"layer_out": layer_out, "hidden_grad": hidden_grad, "memory_grad": memory_grad, **grads_out}
    (small_out,) = take(1)
    weight = dict(zip(NAMES, take(11)))
    left_own = dict(zip(LEFTS, take(len(LEFTS))))
    left_all = dict(zip(LEFTS, take(len(LEFTS))))
    right_all = dict(zip(NAMES, take(11)))
    partial = dict(zip(NAMES, take(11)))
    landing = {name: take(bits - 1) for name in NAMES}
    staged = dict(zip(results, take(len(results))))
    (memory, kbuf, vbuf, vT, kT, tab, near, scores, qs, cqs, ags, att_self, att_cross) = take(13)
    (lse, probs, mk, mv, mkT, mvT, pushed, landed) = take(8)
    (after_self, after_cross, cot, ns, nc, nf, bg) = take(7)
    (dkv,) = take(1)
    dkv_land = take(bits)
    (dmem,) = take(1)
    dmem_land = take(bits)
    (mem_push, mem_land, small, small_land, bias_sum) = take(5)
    (load_sem, hx_send, hx_recv, ag_send, ag_recv, rs_send, rs_recv) = take(7)
    (lf_send, lf_recv, rt_send, rt_recv, out_sem) = take(5)
    (dk_send, dk_recv, dm_send, dm_recv, mg_send, mg_recv, sm_send, sm_recv) = take(8)

    seq, blk, head = (lax.axis_index(name) for name in ("seq", "blk", "head"))
    mine = [lax.rem(blk // (1 << bit), 2) for bit in range(bits)]

    def across(bit):
        return (seq, blk + (1 - 2 * mine[bit]) * (1 << bit), head)

    other_seq = (1 - seq, blk, head)
    other_head = (seq, blk, 1 - head)
    next_blk = across(0)
    member = 2 * seq + mine[0]
    peers = (other_seq, next_blk, (1 - seq, next_blk[1], head))
    peer_slots = (
        2 * (1 - seq) + mine[0],
        2 * seq + 1 - mine[0],
        2 * (1 - seq) + 1 - mine[0],
    )

    loads = {
        name: pltpu.make_async_copy(weights_in[name], weight[name], load_sem.at[slot])
        for slot, name in enumerate(NAMES)
    }
    memory_load = pltpu.make_async_copy(memory_in, memory, load_sem.at[len(NAMES)])
    for name in ("sk", "sv", "sq"):
        copies.start(("load", name), loads[name])
    copies.start(("load", "memory"), memory_load)
    for name in NAMES[3:]:
        copies.start(("load", name), loads[name])

    def checkpoint(place):
        if stop == place:
            raise Stop

    barrier = pltpu.get_barrier_semaphore()
    friends = [*peers, other_head, *(across(bit) for bit in range(1, bits))]
    for friend in friends:
        pl.semaphore_signal(barrier, inc=1, device_id=friend, device_id_type=MESH)

    def give(name):
        slot = list(results).index(name)
        copies.start(
            ("load", "out", name),
            pltpu.make_async_copy(staged[name], results[name], out_sem.at[slot]),
        )

    def whole(name, lanes=slice(None)):
        return weight[name][:, lanes]

    def row_tile(name, tile):
        return weight[name][tile * TILE : (tile + 1) * TILE, :]

    def inverse_norm(values):
        return lax.rsqrt(jnp.mean(values * values, axis=-1, keepdims=True) + EPSILON)

    def norm_into(values, gain, plain, left):
        plain[...] = (values * inverse_norm(values) * gain[...]).astype(BF)
        share_left(left, plain[...])

    def norm_back(values, gain, normed_grad, slot):
        scale = inverse_norm(values)
        unit = values * scale
        unit_grad = normed_grad * gain[...]
        line = jnp.sum(normed_grad * unit, axis=0, keepdims=True)
        for tile in range(width // 128):
            small[0, slot * (width // 128) + tile : slot * (width // 128) + tile + 1, :] = line[
                :, tile * 128 : (tile + 1) * 128
            ]
        return scale * (unit_grad - unit * jnp.mean(unit_grad * unit, axis=-1, keepdims=True))

    def hx(which, tile):
        return pltpu.make_async_remote_copy(
            src_ref=pushed.at[which, tile],
            dst_ref=landed.at[which, tile],
            send_sem=hx_send.at[which, tile],
            recv_sem=hx_recv.at[which, tile],
            device_id=other_head,
            device_id_type=MESH,
        )

    def push(which, tile, value):
        pushed[which, tile] = value.astype(BF)
        copies.start(("hx", which, tile), hx(which, tile))

    def summed(which, tile):
        copies.receive(("hx", which, tile))
        return pushed[which, tile].astype(F32) + landed[which, tile].astype(F32)

    tiles = width // TILE

    def summed_all(which):
        return jnp.concatenate([summed(which, tile) for tile in range(tiles)], axis=1)

    def lanes_of(slot, size):
        return pl.ds(pl.multiple_of(slot * size, size), size)

    def left_place(name, slot):
        if name == "mem":
            return left_all[name].at[slot]
        return left_all[name].at[(slice(None),) * bits + (lanes_of(slot, rows),)]

    def share_left(name, value):
        own = left_own[name]
        turned = value.T
        own[...] = turned.reshape(own.shape)
        here = (seq, *(slice(None),) * (bits - 1), mine[0])
        left_place(name, member)[...] = own[here]
        slot = LEFTS.index(name)
        for way, peer in enumerate(peers):
            there = (peer[0], *(slice(None),) * (bits - 1), mine[0] if way == 0 else 1 - mine[0])
            copies.start(
                ("left", name, way),
                pltpu.make_async_remote_copy(
                    src_ref=own.at[there],
                    dst_ref=left_place(name, member),
                    send_sem=lf_send.at[slot, way],
                    recv_sem=lf_recv.at[slot, way],
                    device_id=peer,
                    device_id_type=MESH,
                ),
            )

    def right_copy(name, way):
        slot = NAMES.index(name)
        place = right_all[name].at[member if way < 2 else peer_slots[1]]
        return pltpu.make_async_remote_copy(
            src_ref=place,
            dst_ref=place,
            send_sem=rt_send.at[slot, way],
            recv_sem=rt_recv.at[slot, way],
            device_id=next_blk if way == 1 else other_seq,
            device_id_type=MESH,
        )

    def share_right(name):
        for way in (1, 0):
            copies.start(("right", name, way), right_copy(name, way))

    def pass_right(name):
        copies.receive(("right", name, 1))
        copies.start(("right", name, 2), right_copy(name, 2))

    def make_partial(name):
        left = LEFT_OF[name]
        for way in range(3):
            if ("left", left, way) not in copies.received:
                copies.receive(("left", left, way))
        copies.receive(("right", name, 0))
        copies.receive(("right", name, 2))
        out = partial[name]
        count, depth, size = right_all[name].shape
        for first, step in lane_tiles(size):
            lanes = slice(first, first + step)
            if left == "mem":
                total = None
                for slot in range(count):
                    part = dot(
                        left_all[left][slot].reshape(width // 4, depth), right_all[name][slot, :, lanes]
                    )
                    total = part if total is None else total + part
            else:
                total = dot(
                    left_all[left][...].reshape(width // 4, count * depth),
                    right_all[name][:, :, lanes].reshape(count * depth, step),
                )
            out[..., lanes] = total.astype(BF).reshape(*out.shape[:-1], step)
        copies.start(("rs", name, 0), rs_copy(name, 0))

    def bit_view(order, stage, keep, low_bit=0):
        index = []
        for bit in reversed(range(low_bit, bits)):
            place = order.index(bit)
            if place < stage:
                index.append(mine[bit])
            elif place == stage:
                index.append(mine[bit] if keep else 1 - mine[bit])
            else:
                index.append(slice(None))
        return tuple(index)

    rs_order = list(range(1, bits))

    def rs_view(name, stage, keep):
        return partial[name].at[bit_view(rs_order, stage, keep, 1)]

    def rs_copy(name, stage):
        slot = NAMES.index(name)
        return pltpu.make_async_remote_copy(
            src_ref=rs_view(name, stage, False),
            dst_ref=landing[name][stage],
            send_sem=rs_send.at[slot, stage],
            recv_sem=rs_recv.at[slot, stage],
            device_id=across(rs_order[stage]),
            device_id_type=MESH,
        )

    def fold_into(kept, got):
        lead = got.shape[:-2]
        for flat in range(int(np.prod(lead))):
            index = tuple(int(value) for value in np.unravel_index(flat, lead)) if lead else (Ellipsis,)
            kept[index] = (kept[index].astype(F32) + got[index].astype(F32)).astype(BF)

    def rs_step(name, stage):
        copies.receive(("rs", name, stage))
        kept, got = rs_view(name, stage, True), landing[name][stage]
        if stage == bits - 2:
            staged[name][...] = kept[...].astype(F32) + got[...].astype(F32)
            give(name)
        else:
            fold_into(kept, got)
            copies.start(("rs", name, stage + 1), rs_copy(name, stage + 1))

    def part_copy(tag, buffer, land, send, recv, stage):
        order = list(range(bits))
        return pltpu.make_async_remote_copy(
            src_ref=buffer.at[bit_view(order, stage, False)],
            dst_ref=land[stage],
            send_sem=send.at[stage],
            recv_sem=recv.at[stage],
            device_id=across(order[stage]),
            device_id_type=MESH,
        )

    def part_start(tag, buffer, land, send, recv, stage):
        copies.start((tag, stage), part_copy(tag, buffer, land, send, recv, stage))

    def part_step(tag, buffer, land, send, recv, stage):
        order = list(range(bits))
        copies.receive((tag, stage))
        kept = buffer.at[bit_view(order, stage, True)]
        if stage == bits - 1:
            return kept[...].astype(F32) + land[stage][...].astype(F32)
        fold_into(kept, land[stage])
        part_start(tag, buffer, land, send, recv, stage + 1)

    def dkv_args(pair):
        return (
            ("dkv", pair),
            dkv.at[pair],
            [land.at[pair] for land in dkv_land],
            dk_send.at[pair],
            dk_recv.at[pair],
        )

    dmem_args = ("dmem", dmem, dmem_land, dm_send, dm_recv)

    def ag_copy(which, step):
        bit = bits - 1 - step
        index = (slice(None),) + tuple(
            slice(None) if place > bit else mine[place] for place in reversed(range(bits))
        )
        buffer = (kbuf, vbuf)[which]
        return pltpu.make_async_remote_copy(
            src_ref=buffer.at[index],
            dst_ref=buffer.at[index],
            send_sem=ag_send.at[which, step],
            recv_sem=ag_recv.at[which, step],
            device_id=across(bit),
            device_id_type=MESH,
        )

    def ag_next(step):
        for which in range(2):
            copies.receive(("ag", which, step))
            if step + 1 < bits:
                copies.start(("ag", which, step + 1), ag_copy(which, step + 1))

    def half_index(chunk):
        index, left = [], chunk
        for _ in range(bits - 1):
            index.append(left % 2 if isinstance(left, int) else lax.rem(left, 2))
            left = left // 2
        return tuple(reversed(index))

    def chunk_of(buffer, pair, chunk):
        return buffer[(pair, *half_index(chunk))].reshape(2 * rows, 128)

    lane = lax.broadcasted_iota(jnp.int32, (rows, 128), 1)
    low = lane < HEAD_DIM
    swap_row = lax.broadcasted_iota(jnp.int32, (128, 128), 0)
    swap_col = lax.broadcasted_iota(jnp.int32, (128, 128), 1)
    swap = (swap_row == lax.rem(swap_col + HEAD_DIM, 128)).astype(F32).astype(BF)

    def split_heads(values, target):
        for group in range(groups):
            tile = values[:, group * 128 : (group + 1) * 128]
            swapped = dot(tile, swap)
            plain = tile.astype(F32)
            first, second = (plain, swapped) if group % 2 == 0 else (swapped, plain)
            here = low if group % 2 == 0 else jnp.logical_not(low)
            target[group, :rows, :] = jnp.where(here, first, 0.0).astype(BF)
            target[group, rows:, :] = jnp.where(here, second, 0.0).astype(BF)

    def join_heads(values):
        return jnp.concatenate([values[:, :rows], values[:, rows:]], axis=0).T

    def head_deltas(values, attended, group):
        turned = values[:, group * 128 : (group + 1) * 128].astype(F32).T
        laid = jnp.concatenate([turned[:HEAD_DIM, :], turned[HEAD_DIM:, :]], axis=1)
        return jnp.sum(laid * attended[group], axis=0, keepdims=True)

    length = lengths[0]
    key_row = lax.broadcasted_iota(jnp.int32, (rows, 2 * rows), 0)

    def kind_of(block):
        return jnp.clip(block - blk + 2, 0, 3)

    def self_scores(group, chunk):
        raw = dot_nt(chunk_of(kbuf, group // 2, chunk), qs[group])
        parts = []
        for inner_block in range(2):
            block = 2 * chunk + inner_block
            part = raw[inner_block * rows : (inner_block + 1) * rows, :]
            part = part + tab[kind_of(block), group]
            parts.append(jnp.where(key_row + block * rows < length, part, MASKED))
        return jnp.concatenate(parts, axis=0)

    checkpoint(0)
    pl.semaphore_wait(barrier, len(friends))
    x = hidden[...].astype(F32)
    norm_into(x, ln_self, ns, "ns")
    copies.receive(("load", "sk"))
    keys = dot(ns[...], whole("sk")).astype(BF)
    for pair in range(pairs):
        kbuf[(pair, *reversed(mine))] = keys[:, pair * 128 : (pair + 1) * 128]
    copies.start(("ag", 0, 0), ag_copy(0, 0))
    copies.receive(("load", "sv"))
    values = dot(ns[...], whole("sv")).astype(BF)
    for pair in range(pairs):
        vbuf[(pair, *reversed(mine))] = values[:, pair * 128 : (pair + 1) * 128]
    copies.start(("ag", 1, 0), ag_copy(1, 0))
    copies.receive(("load", "sq"))
    split_heads(dot(ns[...], whole("sq")).astype(BF), qs)
    ag_next(0)

    copies.receive(("load", "memory"))
    share = mem_rows // blk_count
    share_left("mem", memory[pl.ds(pl.multiple_of(blk * share, share), share), :])
    for source, plain, turned in (("ck", mk, mkT), ("cv", mv, mvT)):
        copies.receive(("load", source))
        result = dot(memory[...], whole(source)).astype(BF)
        for pair in range(pairs):
            plain[pair] = result[:, pair * 128 : (pair + 1) * 128]
            turned[pair * 128 : (pair + 1) * 128, :] = result[:, pair * 128 : (pair + 1) * 128].T
    if bits > 1:
        ag_next(1)

    checkpoint(2)
    starts = bucket_starts()
    distance = lane - lax.broadcasted_iota(jnp.int32, (rows, 128), 0)

    def bias_of(which, head_slot):
        shifted = distance + (rows if which == 1 else 0)
        value = jnp.full((rows, 128), rel_bias[head_slot, 0], F32)
        for bucket, start in enumerate(starts):
            value = jnp.where(shifted >= start, rel_bias[head_slot, bucket + 1], value)
        if which == 2:
            value = jnp.where(shifted >= 0, value, MASKED)
        return value

    def bias_tables(head_slot, carry):
        group = head_slot // 2
        lanes = pl.ds(pl.multiple_of(lax.rem(head_slot, 2) * rows, rows), rows)
        tab[0, group, :, lanes] = jnp.full((rows, rows), rel_bias[head_slot, BUCKETS - 1], F32)
        tab[1, group, :, lanes] = bias_of(1, head_slot)
        tab[2, group, :, lanes] = bias_of(2, head_slot)
        tab[3, group, :, lanes] = jnp.full((rows, rows), MASKED, F32)
        return carry

    lax.fori_loop(0, 2 * groups, bias_tables, 0)
    for step in range(2, bits):
        ag_next(step)

    def turn_chunk(chunk):
        for pair in range(pairs):
            vT[chunk, pair * 128 : (pair + 1) * 128, :] = chunk_of(vbuf, pair, chunk).T
            kT[chunk, pair * 128 : (pair + 1) * 128, :] = chunk_of(kbuf, pair, chunk).T

    if not long:
        for chunk in range(half_count):
            turn_chunk(chunk)

    def turned_of(kept, buffer, group, chunk):
        if not long:
            return kept[chunk, group * HEAD_DIM : (group + 1) * HEAD_DIM, :]
        first = (group % 2) * HEAD_DIM
        return chunk_of(buffer, group // 2, chunk).T[first : first + HEAD_DIM, :]

    def attend(group):
        tops = jnp.full((1, 2 * rows), MASKED, F32)

        def first_pass(chunk, top):
            part = self_scores(group, chunk)
            if not long:
                scores[group % 2, chunk] = part
            return jnp.maximum(top, jnp.max(part, axis=0, keepdims=True))

        def second_pass(chunk, state):
            total, acc = state
            part = self_scores(group, chunk) if long else scores[group % 2, chunk]
            part = jnp.exp(part - tops)
            total = total + jnp.sum(part, axis=0, keepdims=True)
            return total, acc + dot(turned_of(vT, vbuf, group, chunk), part.astype(BF))

        state = (jnp.zeros((1, 2 * rows), F32), jnp.zeros((HEAD_DIM, 2 * rows), F32))
        if not long:
            for chunk in range(half_count):
                tops = first_pass(chunk, tops)
            for chunk in range(half_count):
                state = second_pass(chunk, state)
        else:
            tops = lax.fori_loop(0, half_count, first_pass, tops)
            state = lax.fori_loop(0, half_count, second_pass, state)
        total, acc = state
        precise = acc / total
        att_self[group] = precise
        lse[group] = tops + jnp.log(total)
        right_all["so"][member, :, group * 128 : (group + 1) * 128] = join_heads(precise).astype(BF)

    checkpoint(4)
    for group in range(groups):
        attend(group)

    checkpoint(5)
    copies.receive(("load", "so"))
    for tile in range(tiles):
        push(0, tile, dot_nt(right_all["so"][member], row_tile("so", tile)))
    valid = lax.broadcasted_iota(jnp.int32, (rows, 1), 0) + blk * rows < length
    bg[...] = jnp.where(valid, out_grad[...].astype(F32), 0.0).astype(BF)
    share_left("gf", bg[...])
    after_self[...] = x + summed_all(0)

    checkpoint(6)
    norm_into(after_self[...], ln_cross, nc, "nc")
    copies.receive(("load", "cq"))
    split_heads(dot(nc[...], whole("cq")).astype(BF), cqs)
    for group in range(groups):
        part = dot_nt(mk[group // 2], cqs[group])
        part = jnp.exp(part - jnp.max(part, axis=0, keepdims=True))
        part = part * (1.0 / jnp.sum(part, axis=0, keepdims=True))
        probs[group] = part
        acc = dot(mvT[group * HEAD_DIM : (group + 1) * HEAD_DIM, :], part.astype(BF))
        att_cross[group] = acc
        right_all["co"][member, :, group * 128 : (group + 1) * 128] = join_heads(acc).astype(BF)
    checkpoint(7)
    copies.receive(("load", "co"))
    for tile in range(tiles):
        push(1, tile, dot_nt(right_all["co"][member], row_tile("co", tile)))
    share_right("so")
    share_right("co")
    after_cross[...] = after_self[...] + summed_all(1)

    checkpoint(8)
    norm_into(after_cross[...], ln_ffn, nf, "nf")
    for name in ("fg", "fu", "fd"):
        copies.receive(("load", name))
    for first, size in lane_tiles(weight["fg"].shape[1]):
        lanes = slice(first, first + size)
        gate = dot(nf[...], whole("fg", lanes))
        up = dot(nf[...], whole("fu", lanes))
        back = dot(bg[...], whole("fd", lanes))
        bent = jnp.tanh(GELU_A * (gate + GELU_B * gate * gate * gate))
        opened = 0.5 * (1.0 + bent)
        slope = opened + 0.5 * gate * (1.0 - bent * bent) * (
            GELU_A * (1.0 + 3.0 * GELU_B * gate * gate)
        )
        bell = gate * opened
        right_all["fd"][member, :, lanes] = (bell * up).astype(BF)
        right_all["fg"][member, :, lanes] = (back * up * slope).astype(BF)
        right_all["fu"][member, :, lanes] = (back * bell).astype(BF)
    for name in ("fd", "fg", "fu"):
        share_right(name)
    for tile in range(tiles):
        push(
            2,
            tile,
            dot_nt(right_all["fg"][member], row_tile("fg", tile))
            + dot_nt(right_all["fu"][member], row_tile("fu", tile)),
        )
    for tile in range(tiles):
        push(3, tile, dot_nt(right_all["fd"][member], row_tile("fd", tile)))

    pass_right("so")
    pass_right("co")
    pass_right("fd")
    normed_grad = summed_all(2)
    cot[...] = jnp.where(valid, out_grad[...].astype(F32), 0.0) + norm_back(
        after_cross[...], ln_ffn, normed_grad, 2
    )
    bg[...] = cot[...].astype(BF)
    share_left("gc", bg[...])

    checkpoint(10)
    back = dot(bg[...], whole("co")).astype(BF)
    split_heads(back, ags)
    for pair in range(pairs):
        key_part = value_part = None
        for group in (2 * pair, 2 * pair + 1):
            prob = probs[group]
            prob_grad = dot_nt(mv[pair], ags[group])
            score_grad = (prob * (prob_grad - head_deltas(back, att_cross, group))).astype(BF)
            turned = dot(mkT[group * HEAD_DIM : (group + 1) * HEAD_DIM, :], score_grad)
            right_all["cq"][member, :, group * 128 : (group + 1) * 128] = join_heads(turned).astype(BF)
            key_new = dot(score_grad, cqs[group])
            value_new = dot(prob.astype(BF), ags[group])
            key_part = key_new if key_part is None else key_part + key_new
            value_part = value_new if value_part is None else value_part + value_new
        shape = dmem.shape[:-1]
        dmem[..., pair * 128 : (pair + 1) * 128] = key_part.astype(BF).reshape(*shape, 128)
        dmem[..., (pairs + pair) * 128 : (pairs + pair + 1) * 128] = value_part.astype(BF).reshape(
            *shape, 128
        )
    checkpoint(11)
    for tile in range(tiles):
        push(4, tile, dot_nt(right_all["cq"][member], row_tile("cq", tile)))
    part_start(*dmem_args, 0)
    share_right("cq")
    make_partial("fd")
    pass_right("fg")
    make_partial("co")
    for tile in range(tiles):
        lanes = slice(tile * TILE, (tile + 1) * TILE)
        staged["layer_out"][:, lanes] = (after_cross[:, lanes] + summed(3, tile)).astype(BF)
    give("layer_out")
    normed_grad = summed_all(4)
    cot[...] = cot[...] + norm_back(after_self[...], ln_cross, normed_grad, 1)
    bg[...] = cot[...].astype(BF)
    share_left("gs", bg[...])

    checkpoint(12)
    back = dot(bg[...], whole("so")).astype(BF)
    split_heads(back, ags)
    part_step(*dmem_args, 0)
    make_partial("fg")
    pass_right("fu")
    near[1] = jnp.zeros(near.shape[1:], BF)
    for pair in range(pairs):
        members = (2 * pair, 2 * pair + 1)
        deltas = [head_deltas(back, att_self, group) for group in members]

        def visit(chunk, state, pair=pair, members=members, deltas=deltas):
            state = list(state)
            key_part = value_part = None
            values_here = chunk_of(vbuf, pair, chunk)
            for slot, group in enumerate(members):
                prob = jnp.exp(self_scores(group, chunk) - lse[group])
                prob_grad = dot_nt(values_here, ags[group])
                score_grad = (prob * (prob_grad - deltas[slot])).astype(BF)
                lhs = turned_of(kT, kbuf, group, chunk)
                state[2 * slot] = state[2 * slot] + dot(lhs, score_grad)
                key_new = dot(score_grad, qs[group])
                value_new = dot(prob.astype(BF), ags[group])
                key_part = key_new if key_part is None else key_part + key_new
                value_part = value_new if value_part is None else value_part + value_new
                for inner_block in range(2):
                    kind = kind_of(2 * chunk + inner_block)
                    piece = score_grad[inner_block * rows : (inner_block + 1) * rows, :]
                    near[lax.rem(kind, 3), group] = piece
                    is_far = (kind == 0).astype(F32)
                    state[2 * slot + 1] = state[2 * slot + 1] + is_far * jnp.sum(
                        piece.astype(F32), axis=0, keepdims=True
                    )
            where_to = (pair, *half_index(chunk))
            dkv[(*where_to, slice(None), slice(None), slice(0, 128))] = key_part.astype(BF).reshape(
                2, rows, 128
            )
            dkv[(*where_to, slice(None), slice(None), slice(128, 256))] = value_part.astype(
                BF
            ).reshape(2, rows, 128)
            return tuple(state)

        state = (jnp.zeros((HEAD_DIM, 2 * rows), F32), jnp.zeros((1, 2 * rows), F32)) * 2
        if not long:
            for chunk in range(half_count):
                state = visit(chunk, state)
        else:
            state = lax.fori_loop(0, half_count, visit, state)
        part_start(*dkv_args(pair), 0)
        for slot, group in enumerate(members):
            right_all["sq"][member, :, group * 128 : (group + 1) * 128] = join_heads(
                state[2 * slot]
            ).astype(BF)
            bias_sum[BUCKETS : BUCKETS + 1, group * 2 * rows : (group + 1) * 2 * rows] = state[
                2 * slot + 1
            ]
    checkpoint(13)
    share_right("sq")
    make_partial("fu")
    part_step(*dkv_args(0), 0)
    part_step(*dmem_args, 1)
    pass_right("cq")
    rs_step("fd", 0)
    make_partial("so")
    part_step(*dkv_args(1), 0)
    make_partial("cq")
    mem_sum = None
    for step in range(2, bits):
        mem_sum = part_step(*dmem_args, step)
    mem_sum = mem_sum.astype(BF)
    right_all["ck"][member] = mem_sum[:, : pairs * 128]
    right_all["cv"][member] = mem_sum[:, pairs * 128 :]
    share_right("ck")
    share_right("cv")
    query_part = [
        dot_nt(right_all["sq"][member], row_tile("sq", tile)) for tile in range(tiles)
    ]
    for step in range(1, bits - 1):
        part_step(*dkv_args(0), step)
    rs_step("co", 0)
    rs_step("fg", 0)
    for step in range(1, bits - 1):
        part_step(*dkv_args(1), step)
    pass_right("sq")
    sums = [part_step(*dkv_args(pair), bits - 1).astype(BF) for pair in range(pairs)]
    for pair, value in enumerate(sums):
        right_all["sk"][member, :, pair * 128 : (pair + 1) * 128] = value[:, :128]
        right_all["sv"][member, :, pair * 128 : (pair + 1) * 128] = value[:, 128:]
    share_right("sk")
    share_right("sv")
    for tile in range(tiles):
        push(
            5,
            tile,
            query_part[tile]
            + dot_nt(right_all["sk"][member], row_tile("sk", tile))
            + dot_nt(right_all["sv"][member], row_tile("sv", tile)),
        )
    pass_right("ck")
    pass_right("cv")
    make_partial("sq")
    rs_step("fu", 0)

    checkpoint(14)
    mkg, mvg = right_all["ck"][member], right_all["cv"][member]
    mem_part = dot_nt(mkg, whole("ck")) + dot_nt(mvg, whole("cv"))
    half = share // 2
    mem_push[0] = mem_part[:half, :].astype(BF)
    mem_push[1] = mem_part[half:, :].astype(BF)
    mem_copy = pltpu.make_async_remote_copy(
        src_ref=mem_push.at[1 - head],
        dst_ref=mem_land,
        send_sem=mg_send,
        recv_sem=mg_recv,
        device_id=other_head,
        device_id_type=MESH,
    )
    copies.start(("mem",), mem_copy)
    pass_right("sk")
    pass_right("sv")
    rs_step("so", 0)
    rs_step("cq", 0)

    checkpoint(15)
    def bucket_line(group, lower, upper):
        line = jnp.zeros((1, 2 * rows), F32)
        wide = jnp.concatenate([distance, distance], axis=1)
        for kind in (1, 2):
            shifted = wide + (rows if kind == 1 else 0)
            here = shifted >= lower
            if upper is not None:
                here = jnp.logical_and(here, shifted < upper)
            piece = near[kind, group].astype(F32)
            line = line + jnp.sum(jnp.where(here, piece, 0.0), axis=0, keepdims=True)
        return line

    bounds = [0, *starts, None]
    for group in range(groups):
        lanes = slice(group * 2 * rows, (group + 1) * 2 * rows)
        for bucket in range(BUCKETS):
            line = bucket_line(group, bounds[bucket], bounds[bucket + 1])
            if bucket == BUCKETS - 1:
                line = line + bias_sum[BUCKETS : BUCKETS + 1, lanes]
            bias_sum[bucket : bucket + 1, lanes] = line
    bias_lane = lax.broadcasted_iota(jnp.int32, (BUCKETS, 128), 1)
    bias_grad = jnp.zeros((BUCKETS, 128), F32)
    for head_slot in range(2 * groups):
        column = jnp.sum(
            bias_sum[:BUCKETS, head_slot * rows : (head_slot + 1) * rows], axis=1, keepdims=True
        )
        bias_grad = jnp.where(bias_lane == head_slot, column, bias_grad)
    first_bias = 3 * (width // 128)
    small[0, first_bias : first_bias + BUCKETS, :] = bias_grad

    checkpoint(16)
    normed_grad = summed_all(5)
    staged["hidden_grad"][...] = cot[...] + norm_back(hidden[...].astype(F32), ln_self, normed_grad, 0)
    give("hidden_grad")

    def small_copy(stage):
        return pltpu.make_async_remote_copy(
            src_ref=small.at[stage],
            dst_ref=small_land.at[stage],
            send_sem=sm_send.at[stage],
            recv_sem=sm_recv.at[stage],
            device_id=other_seq if stage == 0 else across(stage - 1),
            device_id_type=MESH,
        )

    def small_step(stage):
        copies.receive(("small", stage))
        total = small[stage] + small_land[stage]
        if stage < stages - 1:
            small[stage + 1] = total
            copies.start(("small", stage + 1), small_copy(stage + 1))
        else:
            small_out[...] = total

    copies.start(("small", 0), small_copy(0))
    for name in ("ck", "cv", "sk", "sv"):
        make_partial(name)
    small_step(0)
    for name in ("fd", "co", "fg", "fu", "so", "cq"):
        for step in range(1, bits - 1):
            rs_step(name, step)
    rs_step("sq", 0)
    small_step(1)
    for step in range(1, bits - 1):
        rs_step("sq", step)
    for name in ("ck", "cv", "sk", "sv"):
        rs_step(name, 0)
    small_step(2)
    for step in range(1, bits - 1):
        for name in ("ck", "cv", "sk", "sv"):
            rs_step(name, step)
    for stage in range(3, stages):
        small_step(stage)
    copies.receive(("mem",))
    staged["memory_grad"][...] = mem_push[head].astype(F32) + mem_land[...].astype(F32)
    give("memory_grad")


def finish_kernel(count, lines, width, *refs):
    sources, small = refs[:count], refs[count]
    targets = refs[count + 1 : 2 * count + 1]
    gain_out, bias_out, sems = refs[2 * count + 1 : 2 * count + 4], refs[2 * count + 4], refs[-1]
    moves = [
        pltpu.make_async_copy(source, target, sems.at[slot])
        for slot, (source, target) in enumerate(zip(sources, targets))
    ]
    for move in moves:
        move.start()
    share = gain_out[0].shape[0]
    per_line = 128 // share
    place = lax.axis_index("seq") * lax.axis_size("blk") + lax.axis_index("blk")
    for slot, target in enumerate(gain_out):
        line = small[pl.ds(slot * lines + place // per_line, 1), :]
        for part in range(per_line):

            @pl.when(lax.rem(place, per_line) == part)
            def _(target=target, line=line, part=part):
                target[...] = line[0, part * share : (part + 1) * share]

    bias_out[...] = small[3 * lines :, :].T[: bias_out.shape[0], :]
    for move in moves:
        move.wait()


def finish(results, small, width, share, heads):
    count = len(results)
    in_any = pl.BlockSpec(memory_space=pl.ANY)
    in_vmem = pl.BlockSpec(memory_space=pltpu.VMEM)
    return pl.pallas_call(
        functools.partial(finish_kernel, count, width // 128, width),
        out_shape=[
            *(jax.ShapeDtypeStruct(result.shape, result.dtype) for result in results),
            *[jax.ShapeDtypeStruct((share,), F32)] * 3,
            jax.ShapeDtypeStruct((heads, BUCKETS), F32),
        ],
        in_specs=[in_vmem] * (count + 1),
        out_specs=[*[in_any] * count, *[in_vmem] * 4],
        scratch_shapes=[pltpu.SemaphoreType.DMA((count,))],
        name="finish",
    )(*results, small)


def run_layer(lengths, rel_bias, hidden, out_grad, gains, memory, weights, blk_count, stop=None):
    bits = blk_count.bit_length() - 1
    stages = bits + 1
    rows, width = hidden.shape
    groups = weights["sk"].shape[1] // HEAD_DIM
    heads = weights["sq"].shape[1] // HEAD_DIM
    mem_rows = memory.shape[0]
    if rows != 128 or heads != 2 * groups or bucket_starts()[-1] > rows or 1 << bits != blk_count:
        raise ValueError("unexpected sizes")
    pairs = groups // 2
    half_count = blk_count // 2
    stored = 1 if half_count > 4 else half_count
    piece = width // (2 * blk_count)
    widths = {name: weights[name].shape[1] for name in NAMES}
    share = mem_rows // blk_count
    small_rows = 3 * (width // 128) + BUCKETS

    vm, sem = pltpu.VMEM, pltpu.SemaphoreType.DMA
    high = (2,) * (bits - 1)
    depth = {name: share if LEFT_OF[name] == "mem" else rows for name in NAMES}
    scratch = [vm((width, widths[name]), BF) for name in NAMES]
    scratch += [
        vm((2, *high, 2, piece, share if left == "mem" else rows), BF) for left in LEFTS
    ]
    scratch += [
        vm((4, *high, piece, share) if left == "mem" else (*high, piece, 4 * rows), BF)
        for left in LEFTS
    ]
    scratch += [vm((4, depth[name], widths[name]), BF) for name in NAMES]
    scratch += [vm((*high, piece, widths[name]), BF) for name in NAMES]
    for name in NAMES:
        for stage in range(bits - 1):
            scratch.append(vm((2,) * (bits - 2 - stage) + (piece, widths[name]), BF))
    by_bit = (2,) * bits
    scratch += [vm((rows, width), BF), vm((rows, width), F32), vm((share // 2, width), F32)]
    scratch += [vm((piece, widths[name]), F32) for name in NAMES]
    scratch += [
        vm(memory.shape, BF),
        vm((pairs, *by_bit, rows, 128), BF),
        vm((pairs, *by_bit, rows, 128), BF),
        vm((stored, groups * HEAD_DIM, 2 * rows), BF),
        vm((stored, groups * HEAD_DIM, 2 * rows), BF),
        vm((4, groups, rows, 2 * rows), F32),
        vm((3, groups, rows, 2 * rows), BF),
        vm((2, stored, 2 * rows, 2 * rows), F32),
        vm((groups, 2 * rows, 128), BF),
        vm((groups, 2 * rows, 128), BF),
        vm((groups, 2 * rows, 128), BF),
        vm((groups, HEAD_DIM, 2 * rows), F32),
        vm((groups, HEAD_DIM, 2 * rows), F32),
        vm((groups, 1, 2 * rows), F32),
        vm((groups, mem_rows, 2 * rows), F32),
        vm((pairs, mem_rows, 128), BF),
        vm((pairs, mem_rows, 128), BF),
        vm((groups * HEAD_DIM, mem_rows), BF),
        vm((groups * HEAD_DIM, mem_rows), BF),
        vm((6, width // TILE, rows, TILE), BF),
        vm((6, width // TILE, rows, TILE), BF),
        vm((rows, width), F32),
        vm((rows, width), F32),
        vm((rows, width), F32),
        vm((rows, width), BF),
        vm((rows, width), BF),
        vm((rows, width), BF),
        vm((rows, width), BF),
        vm((pairs, *by_bit, rows, 256), BF),
    ]
    scratch += [vm((pairs, *(2,) * (bits - 1 - stage), rows, 256), BF) for stage in range(bits)]
    scratch += [vm((*by_bit, share, 2 * groups * HEAD_DIM), BF)]
    scratch += [
        vm((*(2,) * (bits - 1 - stage), share, 2 * groups * HEAD_DIM), BF) for stage in range(bits)
    ]
    scratch += [
        vm((2, share // 2, width), BF),
        vm((share // 2, width), BF),
        vm((stages, small_rows, 128), F32),
        vm((stages, small_rows, 128), F32),
        vm((BUCKETS + 8, heads * rows), F32),
        sem((len(NAMES) + 1,)),
        sem((6, width // TILE)),
        sem((6, width // TILE)),
        sem((2, bits)),
        sem((2, bits)),
        sem((len(NAMES), bits - 1)),
        sem((len(NAMES), bits - 1)),
        sem((len(LEFTS), 3)),
        sem((len(LEFTS), 3)),
        sem((len(NAMES), 3)),
        sem((len(NAMES), 3)),
        sem((3 + len(NAMES),)),
        sem((pairs, bits)),
        sem((pairs, bits)),
        sem((bits,)),
        sem((bits,)),
        sem,
        sem,
        sem((stages,)),
        sem((stages,)),
    ]
    in_vmem = pl.BlockSpec(memory_space=pltpu.VMEM)
    in_smem = pl.BlockSpec(memory_space=pltpu.SMEM)
    in_any = pl.BlockSpec(memory_space=pl.ANY)
    out_shape = [
        jax.ShapeDtypeStruct((rows, width), BF),
        jax.ShapeDtypeStruct((rows, width), F32),
        jax.ShapeDtypeStruct((share // 2, width), F32),
        *(jax.ShapeDtypeStruct((piece, widths[name]), F32) for name in NAMES),
        jax.ShapeDtypeStruct((small_rows, 128), F32),
    ]
    results = pl.pallas_call(
        functools.partial(layer_kernel, (bits, rows, width, groups, mem_rows), stop),
        out_shape=out_shape,
        in_specs=[in_smem, in_smem, *[in_vmem] * 5, *[in_any] * 12],
        out_specs=[*[in_any] * (len(out_shape) - 1), in_vmem],
        scratch_shapes=scratch,
        compiler_params=pltpu.CompilerParams(
            collective_id=0, has_side_effects=True, vmem_limit_bytes=63 * 1024 * 1024
        ),
        name="layer",
    )(
        lengths, rel_bias, hidden, out_grad, *gains, memory, *(weights[name] for name in NAMES)
    )
    return results[:3], dict(zip(NAMES, results[3:-1])), results[-1]


def body(
    hidden,
    memory,
    lengths,
    out_grad,
    ln_self,
    self_query,
    self_key,
    self_value,
    self_out,
    rel_bias,
    ln_cross,
    cross_query,
    cross_key,
    cross_value,
    cross_out,
    ln_ffn,
    ffn_gate,
    ffn_up,
    feedforward_down_weight,
):
    width = hidden.shape[1]
    blk_count = lax.axis_size("blk")
    weights = dict(
        sk=self_key,
        sv=self_value,
        sq=self_query,
        ck=cross_key,
        cv=cross_value,
        so=self_out,
        cq=cross_query,
        co=cross_out,
        fg=ffn_gate,
        fu=ffn_up,
        fd=feedforward_down_weight,
    )
    gains = [gain.reshape(1, width) for gain in (ln_self, ln_cross, ln_ffn)]
    (layer_out, hidden_grad, memory_grad), grads, small = run_layer(
        lengths, rel_bias.T, hidden, out_grad, gains, memory, weights, blk_count
    )
    kept = [layer_out, hidden_grad, memory_grad, *(grads[name] for name in NAMES)]
    *kept, self_gain, cross_gain, ffn_gain, bias_grad = finish(
        kept, small, width, width // (2 * blk_count), rel_bias.shape[1]
    )
    layer_out, hidden_grad, memory_grad = kept[:3]
    grads = dict(zip(NAMES, kept[3:]))
    return (
        layer_out,
        hidden_grad,
        memory_grad,
        self_gain,
        grads["sq"],
        grads["sk"],
        grads["sv"],
        grads["so"],
        bias_grad.T,
        cross_gain,
        grads["cq"],
        grads["ck"],
        grads["cv"],
        grads["co"],
        ffn_gain,
        grads["fg"],
        grads["fu"],
        grads["fd"],
    )


def solution(mesh):
    blocks = P(("seq", "blk"), None)
    by_head = P(None, "head")
    shares = P(("seq", "blk"), "head")
    line = P(("seq", "blk"))
    in_specs = (
        blocks,
        P("seq", None),
        P("seq"),
        blocks,
        P(),
        *[by_head] * 5,
        P(),
        *[by_head] * 4,
        P(),
        *[by_head] * 3,
    )
    out_specs = (
        blocks,
        blocks,
        P(("seq", "blk", "head"), None),
        line,
        *[shares] * 4,
        by_head,
        line,
        *[shares] * 4,
        line,
        *[shares] * 3,
    )
    return jax.shard_map(body, mesh=mesh, in_specs=in_specs, out_specs=out_specs, check_vma=False)
```

```python
import functools

import jax
import jax.numpy as jnp
import numpy as np
from jax import lax
from jax.experimental import pallas as pl
from jax.experimental.pallas import tpu as pltpu
from jax.sharding import PartitionSpec as P

MESH = pl.DeviceIdType.MESH
HEAD_DIM = 64
BUCKETS = 32
MAX_DIST = 128
EPSILON = 1e-06
MASKED = -1e30
BF = jnp.bfloat16
F32 = jnp.float32
TILE = 256
GELU_A = float(np.sqrt(2.0 / np.pi))
GELU_B = 0.044715

NAMES = ("sk", "sv", "sq", "ck", "cv", "so", "cq", "co", "fg", "fu", "fd")
LEFTS = ("ns", "nc", "nf", "gf", "gc", "gs", "mem")
LEFT_OF = dict(
    sk="ns", sv="ns", sq="ns", cq="nc", fg="nf", fu="nf", fd="gf", co="gc", so="gs", ck="mem", cv="mem"
)


def bucket_starts():
    exact = BUCKETS // 2
    far = np.ceil(exact * (MAX_DIST / exact) ** (np.arange(1, exact) / exact))
    return [*range(1, exact + 1), *(int(value) for value in far)]


def dot(left, right):
    return jnp.dot(left, right, preferred_element_type=F32)


def dot_nt(left, right):
    return lax.dot_general(left, right, (((1,), (1,)), ((), ())), preferred_element_type=F32)


def lane_tiles(width, step=512):
    return [(first, min(step, width - first)) for first in range(0, width, step)]
SHARED_BIT = dict(gf=1, gc=1, gs=1)
DIRECT = ("ck", "cv", "sk", "sv")


def shared_bit(name):
    return SHARED_BIT.get(LEFT_OF.get(name, name), 0)


class Stop(Exception):
    pass


class Copies:
    def __init__(self):
        self.made, self.started, self.received, self.sent = {}, [], set(), set()
        self.last = []

    def start(self, key, copy):
        self.made[key] = copy
        self.started.append(key)
        copy.start()

    def receive(self, key):
        self.received.add(key)
        copy = self.made[key]
        if key[0] == "load":
            copy.wait()
        else:
            copy.wait_recv()

    def leave(self, key):
        self.sent.add(key)
        self.made[key].wait_send()

    def drain(self):
        for key in self.started:
            if key not in self.received:
                self.receive(key)
        for key in self.started:
            if key[0] != "load" and key not in self.sent:
                self.leave(key)
        for wait in self.last:
            wait()


def layer_kernel(shapes, stop, *refs):
    copies = Copies()
    try:
        layer_steps(copies, shapes, stop, *refs)
    except Stop:
        pass
    copies.drain()


def layer_steps(copies, shapes, stop, *refs):
    bits, rows, width, groups, mem_rows = shapes
    stages = bits + 1
    blk_count = 1 << bits
    pairs = groups // 2
    half_count = blk_count // 2
    long = half_count > 4
    refs = list(refs)

    def take(count):
        taken, refs[:count] = refs[:count], []
        return taken

    lengths, rel_bias, hidden, out_grad, ln_self, ln_cross, ln_ffn, memory_in = take(8)
    weights_in = dict(zip(NAMES, take(11)))
    layer_out, hidden_grad, memory_grad = take(3)
    grads_out = dict(zip(NAMES, take(11)))
    results = {"layer_out": layer_out, "hidden_grad": hidden_grad, "memory_grad": memory_grad, **grads_out}
    (small_out,) = take(1)
    weight = dict(zip(NAMES, take(11)))
    left_own = dict(zip(LEFTS, take(len(LEFTS))))
    left_all = dict(zip(LEFTS, take(len(LEFTS))))
    right_all = dict(zip(NAMES, take(11)))
    partial = dict(zip(NAMES, take(11)))
    landing = {name: take(1 if name in DIRECT else bits - 1) for name in NAMES}
    staged = dict(zip(results, take(len(results))))
    (memory, kbuf, vbuf, vT, kT, tab, near, scores, qs, cqs, ags, att_self, att_cross) = take(13)
    (lse, probs, mk, mv, mkT, mvT, pushed, landed) = take(8)
    (after_self, after_cross, cot, ns, nc, nf, bg) = take(7)
    (dkv,) = take(1)
    dkv_land = take(bits)
    (dmem,) = take(1)
    dmem_land = take(bits)
    (mem_push, mem_land, small, small_far, far_sum) = take(5)
    (load_sem, hx_send, hx_recv, ag_send, ag_recv, rs_send, rs_recv) = take(7)
    (lf_send, lf_recv, rt_send, rt_recv, out_sem) = take(5)
    (dk_send, dk_recv, dm_send, dm_recv, mg_send, mg_recv, sm_send, sm_recv) = take(8)

    seq, blk, head = (lax.axis_index(name) for name in ("seq", "blk", "head"))
    mine = [lax.rem(blk // (1 << bit), 2) for bit in range(bits)]

    def across(bit):
        return (seq, blk + (1 - 2 * mine[bit]) * (1 << bit), head)

    other_seq = (1 - seq, blk, head)
    other_head = (seq, blk, 1 - head)

    def hop(mask):
        target = blk
        for bit in range(bits):
            if mask >> bit & 1:
                target = target + (1 - 2 * mine[bit]) * (1 << bit)
        return (seq, target, head)

    def member(bit):
        return 2 * seq + mine[bit]

    def peers(bit):
        far = across(bit)
        return (other_seq, far, (1 - seq, far[1], head))

    far_masks = [step << 1 for step in range(1, 1 << (bits - 1))]
    own = {name: member(shared_bit(name)) for name in NAMES}

    loads = {
        name: pltpu.make_async_copy(weights_in[name], weight[name], load_sem.at[slot])
        for slot, name in enumerate(NAMES)
    }
    memory_load = pltpu.make_async_copy(memory_in, memory, load_sem.at[len(NAMES)])
    for name in ("sk", "sv"):
        copies.start(("load", name), loads[name])

    def more_loads():
        copies.start(("load", "sq"), loads["sq"])
        copies.start(("load", "memory"), memory_load)
        for name in NAMES[3:]:
            copies.start(("load", name), loads[name])

    def checkpoint(place):
        if stop == place:
            raise Stop

    barrier = pltpu.get_barrier_semaphore()
    bits_used = sorted({shared_bit(name) for name in LEFTS})
    friends = [other_seq, other_head, across(0)]
    friends += [peers(bit)[2] for bit in bits_used]
    friends += [hop(mask) for mask in far_masks]
    for friend in friends:
        pl.semaphore_signal(barrier, inc=1, device_id=friend, device_id_type=MESH)

    def give(name):
        slot = list(results).index(name)
        copies.start(
            ("load", "out", name),
            pltpu.make_async_copy(staged[name], results[name], out_sem.at[slot]),
        )

    def whole(name, lanes=slice(None)):
        return weight[name][:, lanes]

    def row_tile(name, tile):
        return weight[name][tile * TILE : (tile + 1) * TILE, :]

    def inverse_norm(values):
        return lax.rsqrt(jnp.mean(values * values, axis=-1, keepdims=True) + EPSILON)

    def norm_into(values, gain, plain, left):
        plain[...] = (values * inverse_norm(values) * gain[...]).astype(BF)
        if left is not None:
            share_left(left, plain[...])

    def norm_back(values, gain, normed_grad, slot):
        scale = inverse_norm(values)
        unit = values * scale
        unit_grad = normed_grad * gain[...]
        line = jnp.sum(normed_grad * unit, axis=0, keepdims=True)
        for tile in range(width // 128):
            small[member(0), slot * (width // 128) + tile : slot * (width // 128) + tile + 1, :] = line[
                :, tile * 128 : (tile + 1) * 128
            ]
        return scale * (unit_grad - unit * jnp.mean(unit_grad * unit, axis=-1, keepdims=True))

    def hx(which, tile):
        return pltpu.make_async_remote_copy(
            src_ref=pushed.at[which % 4, tile],
            dst_ref=landed.at[which % 4, tile],
            send_sem=hx_send.at[which, tile],
            recv_sem=hx_recv.at[which, tile],
            device_id=other_head,
            device_id_type=MESH,
        )

    def push(which, tile, value):
        if which >= 4:
            copies.leave(("hx", which - 4, tile))
        pushed[which % 4, tile] = value.astype(BF)
        copies.start(("hx", which, tile), hx(which, tile))

    def summed(which, tile):
        copies.receive(("hx", which, tile))
        return pushed[which % 4, tile].astype(F32) + landed[which % 4, tile].astype(F32)

    tiles = width // TILE

    def summed_all(which):
        return jnp.concatenate([summed(which, tile) for tile in range(tiles)], axis=1)

    def lanes_of(slot, size):
        return pl.ds(pl.multiple_of(slot * size, size), size)

    def left_place(name, slot):
        if name == "mem":
            return left_all[name].at[slot]
        return left_all[name].at[(slice(None),) * bits + (lanes_of(slot, rows),)]

    def share_left(name, value):
        mine_left = left_own[name]
        bit = shared_bit(name)
        turned = value.T
        mine_left[...] = turned.reshape(mine_left.shape)

        def rows_of(half, low):
            index = [half]
            index += [low if place == bit else slice(None) for place in reversed(range(bits))]
            return tuple(index)

        left_place(name, member(bit))[...] = mine_left[rows_of(seq, mine[bit])]
        slot = LEFTS.index(name)
        for way, peer in enumerate(peers(bit)):
            there = rows_of(peer[0], mine[bit] if way == 0 else 1 - mine[bit])
            copies.start(
                ("left", name, way),
                pltpu.make_async_remote_copy(
                    src_ref=mine_left.at[there],
                    dst_ref=left_place(name, member(bit)),
                    send_sem=lf_send.at[slot, way],
                    recv_sem=lf_recv.at[slot, way],
                    device_id=peer,
                    device_id_type=MESH,
                ),
            )

    def right_copy(name, way):
        slot = NAMES.index(name)
        bit = shared_bit(name)
        place = right_all[name].at[own[name] if way < 2 else 2 * seq + 1 - mine[bit]]
        return pltpu.make_async_remote_copy(
            src_ref=place,
            dst_ref=place,
            send_sem=rt_send.at[slot, way],
            recv_sem=rt_recv.at[slot, way],
            device_id=across(bit) if way == 1 else other_seq,
            device_id_type=MESH,
        )

    def share_right(name):
        for way in (1, 0):
            copies.start(("right", name, way), right_copy(name, way))

    def pass_right(name):
        copies.receive(("right", name, 1))
        copies.start(("right", name, 2), right_copy(name, 2))

    def make_partial(name):
        left = LEFT_OF[name]
        for way in range(3):
            if ("left", left, way) not in copies.received:
                copies.receive(("left", left, way))
        copies.receive(("right", name, 0))
        copies.receive(("right", name, 2))
        out = partial[name]
        count, depth, size = right_all[name].shape
        for first, step in lane_tiles(size):
            lanes = slice(first, first + step)
            if left == "mem":
                total = None
                for slot in range(count):
                    part = dot(
                        left_all[left][slot].reshape(width // 4, depth), right_all[name][slot, :, lanes]
                    )
                    total = part if total is None else total + part
            else:
                total = dot(
                    left_all[left][...].reshape(width // 4, count * depth),
                    right_all[name][:, :, lanes].reshape(count * depth, step),
                )
            out[..., lanes] = total.astype(BF).reshape(*out.shape[:-1], step)
        for stage in range(len(far_masks) if name in DIRECT else 1):
            copies.start(("rs", name, stage), rs_copy(name, stage))

    def bit_view(order, stage, keep):
        index = []
        for bit in reversed(range(bits)):
            if bit not in order:
                continue
            place = order.index(bit)
            if place < stage:
                index.append(mine[bit])
            elif place == stage:
                index.append(mine[bit] if keep else 1 - mine[bit])
            else:
                index.append(slice(None))
        return tuple(index)

    def rs_order(name):
        return [bit for bit in range(bits) if bit != shared_bit(name)]

    def rs_view(name, stage, keep):
        return partial[name].at[bit_view(rs_order(name), stage, keep)]

    def rs_copy(name, stage):
        slot = NAMES.index(name)
        if name in DIRECT:
            mask = far_masks[stage]
            place = tuple(
                1 - mine[bit] if mask >> bit & 1 else mine[bit] for bit in reversed(range(1, bits))
            )
            source, target, to = partial[name].at[place], landing[name][0].at[stage], hop(mask)
        else:
            source, target = rs_view(name, stage, False), landing[name][stage]
            to = across(rs_order(name)[stage])
        return pltpu.make_async_remote_copy(
            src_ref=source,
            dst_ref=target,
            send_sem=rs_send.at[slot, stage],
            recv_sem=rs_recv.at[slot, stage],
            device_id=to,
            device_id_type=MESH,
        )

    def fold_into(kept, got):
        lead = got.shape[:-2]
        for flat in range(int(np.prod(lead))):
            index = tuple(int(value) for value in np.unravel_index(flat, lead)) if lead else (Ellipsis,)
            kept[index] = (kept[index].astype(F32) + got[index].astype(F32)).astype(BF)

    def rs_finish(name):
        total = partial[name][tuple(mine[bit] for bit in reversed(range(1, bits)))].astype(F32)
        for stage in range(len(far_masks)):
            copies.receive(("rs", name, stage))
            total = total + landing[name][0][stage].astype(F32)
        staged[name][...] = total
        give(name)

    def rs_step(name, stage):
        copies.receive(("rs", name, stage))
        kept, got = rs_view(name, stage, True), landing[name][stage]
        if stage == bits - 2:
            staged[name][...] = kept[...].astype(F32) + got[...].astype(F32)
            give(name)
        else:
            fold_into(kept, got)
            copies.start(("rs", name, stage + 1), rs_copy(name, stage + 1))

    def part_copy(tag, buffer, land, send, recv, stage):
        order = list(range(bits))
        return pltpu.make_async_remote_copy(
            src_ref=buffer.at[bit_view(order, stage, False)],
            dst_ref=land[stage],
            send_sem=send.at[stage],
            recv_sem=recv.at[stage],
            device_id=across(order[stage]),
            device_id_type=MESH,
        )

    def part_start(tag, buffer, land, send, recv, stage):
        copies.start((tag, stage), part_copy(tag, buffer, land, send, recv, stage))

    def part_step(tag, buffer, land, send, recv, stage):
        order = list(range(bits))
        copies.receive((tag, stage))
        kept = buffer.at[bit_view(order, stage, True)]
        if stage == bits - 1:
            return kept[...].astype(F32) + land[stage][...].astype(F32)
        fold_into(kept, land[stage])
        part_start(tag, buffer, land, send, recv, stage + 1)

    def dkv_args(pair):
        return (
            ("dkv", pair),
            dkv.at[pair],
            [land.at[pair] for land in dkv_land],
            dk_send.at[pair],
            dk_recv.at[pair],
        )

    dmem_args = ("dmem", dmem, dmem_land, dm_send, dm_recv)

    level = blk // 2
    top = half_count - 1

    def ag_copy(which, step, up):
        place, digits = jnp.maximum(level - step, 0), []
        for _ in range(bits - 1):
            digits.append(lax.rem(place, 2))
            place = place // 2
        buffer = (kbuf, vbuf)[which]
        block = buffer.at[(slice(None), *reversed(digits), mine[0])]
        above = (seq, 2 * jnp.minimum(level + 1, top) + mine[0], head)
        return pltpu.make_async_remote_copy(
            src_ref=block,
            dst_ref=block,
            send_sem=ag_send.at[which, step, 0 if up else 1],
            recv_sem=ag_recv.at[which, step, 0 if up else 1],
            device_id=above if up else across(0),
            device_id_type=MESH,
        )

    def ag_step(which, step):
        @pl.when(level >= step)
        def _():
            if step > 0:
                ag_copy(which, step - 1, True).wait_recv()

            @pl.when(level < top)
            def _():
                ag_copy(which, step, True).start()

            ag_copy(which, step, False).start()

        def wait():
            @pl.when(level >= step)
            def _():
                @pl.when(level < top)
                def _():
                    ag_copy(which, step, True).wait_send()

                ag_copy(which, step, False).wait_send()

        copies.last.append(wait)

    def ag_end(which):
        for step in range(half_count):

            @pl.when(level >= step)
            def _(step=step):
                ag_copy(which, step, False).wait_recv()

    def clear_later():
        for place in range(1, half_count):
            digits = tuple(place >> bit & 1 for bit in reversed(range(bits - 1)))

            @pl.when(place > level)
            def _(digits=digits):
                for buffer in (kbuf, vbuf):
                    for pair in range(pairs):
                        buffer[(pair, *digits)] = jnp.zeros((2, rows, 128), BF)

    def half_index(chunk):
        index, left = [], chunk
        for _ in range(bits - 1):
            index.append(left % 2 if isinstance(left, int) else lax.rem(left, 2))
            left = left // 2
        return tuple(reversed(index))

    def chunk_of(buffer, pair, chunk):
        return buffer[(pair, *half_index(chunk))].reshape(2 * rows, 128)

    lane = lax.broadcasted_iota(jnp.int32, (rows, 128), 1)
    low = lane < HEAD_DIM
    swap_row = lax.broadcasted_iota(jnp.int32, (128, 128), 0)
    swap_col = lax.broadcasted_iota(jnp.int32, (128, 128), 1)
    swap = (swap_row == lax.rem(swap_col + HEAD_DIM, 128)).astype(F32).astype(BF)

    def split_heads(values, target):
        for group in range(groups):
            tile = values[:, group * 128 : (group + 1) * 128]
            swapped = dot(tile, swap)
            plain = tile.astype(F32)
            first, second = (plain, swapped) if group % 2 == 0 else (swapped, plain)
            here = low if group % 2 == 0 else jnp.logical_not(low)
            target[group, :rows, :] = jnp.where(here, first, 0.0).astype(BF)
            target[group, rows:, :] = jnp.where(here, second, 0.0).astype(BF)

    def join_heads(values):
        return jnp.concatenate([values[:, :rows], values[:, rows:]], axis=0).T

    def head_deltas(values, attended, group):
        turned = values[:, group * 128 : (group + 1) * 128].astype(F32).T
        laid = jnp.concatenate([turned[:HEAD_DIM, :], turned[HEAD_DIM:, :]], axis=1)
        return jnp.sum(laid * attended[group], axis=0, keepdims=True)

    length = lengths[0]
    reach = jnp.minimum(length, (blk + 1) * rows)
    key_row = lax.broadcasted_iota(jnp.int32, (rows, 2 * rows), 0)

    def kind_of(block):
        return jnp.clip(block - blk + 2, 0, 3)

    def self_scores(group, chunk):
        raw = dot_nt(chunk_of(kbuf, group // 2, chunk), qs[group])
        parts = []
        for inner_block in range(2):
            block = 2 * chunk + inner_block
            part = raw[inner_block * rows : (inner_block + 1) * rows, :]
            part = part + tab[jnp.minimum(kind_of(block), 2), group]
            parts.append(jnp.where(key_row + block * rows < reach, part, MASKED))
        return jnp.concatenate(parts, axis=0)

    checkpoint(0)
    pl.semaphore_wait(barrier, len(friends))
    x = hidden[...].astype(F32)
    norm_into(x, ln_self, ns, None)
    copies.receive(("load", "sk"))
    more_loads()
    keys = dot(ns[...], whole("sk")).astype(BF)
    for pair in range(pairs):
        kbuf[(pair, *reversed(mine))] = keys[:, pair * 128 : (pair + 1) * 128]
    ag_step(0, 0)
    copies.receive(("load", "sv"))
    values = dot(ns[...], whole("sv")).astype(BF)
    for pair in range(pairs):
        vbuf[(pair, *reversed(mine))] = values[:, pair * 128 : (pair + 1) * 128]
    ag_step(1, 0)
    clear_later()
    copies.receive(("load", "sq"))
    split_heads(dot(ns[...], whole("sq")).astype(BF), qs)
    for which in range(2):
        ag_step(which, 1)
    copies.receive(("load", "memory"))
    share = mem_rows // blk_count

    def project_memory(source, plain, turned):
        copies.receive(("load", source))
        result = dot(memory[...], whole(source)).astype(BF)
        for pair in range(pairs):
            plain[pair] = result[:, pair * 128 : (pair + 1) * 128]
            turned[pair * 128 : (pair + 1) * 128, :] = result[:, pair * 128 : (pair + 1) * 128].T

    project_memory("ck", mk, mkT)
    for which in range(2):
        ag_step(which, 2)
    project_memory("cv", mv, mvT)
    for step in range(3, half_count):
        for which in range(2):
            ag_step(which, step)

    starts = bucket_starts()
    distance = lane - lax.broadcasted_iota(jnp.int32, (rows, 128), 0)

    def bias_of(which, head_slot):
        shifted = distance + (rows if which == 1 else 0)
        value = jnp.full((rows, 128), rel_bias[head_slot, 0], F32)
        for bucket, start in enumerate(starts):
            value = jnp.where(shifted >= start, rel_bias[head_slot, bucket + 1], value)
        if which == 2:
            value = jnp.where(shifted >= 0, value, MASKED)
        return value

    def bias_tables(head_slot, carry):
        group = head_slot // 2
        lanes = pl.ds(pl.multiple_of(lax.rem(head_slot, 2) * rows, rows), rows)
        tab[0, group, :, lanes] = jnp.full((rows, rows), rel_bias[head_slot, BUCKETS - 1], F32)
        tab[1, group, :, lanes] = bias_of(1, head_slot)
        tab[2, group, :, lanes] = bias_of(2, head_slot)
        return carry

    lax.fori_loop(0, 2 * groups, bias_tables, 0)
    share_left("ns", ns[...])
    share_left("mem", memory[pl.ds(pl.multiple_of(blk * share, share), share), :])
    for which in range(2):
        ag_end(which)

    def turn_chunk(chunk):
        for pair in range(pairs):
            vT[chunk, pair * 128 : (pair + 1) * 128, :] = chunk_of(vbuf, pair, chunk).T
            kT[chunk, pair * 128 : (pair + 1) * 128, :] = chunk_of(kbuf, pair, chunk).T

    if not long:
        for chunk in range(half_count):
            turn_chunk(chunk)

    def turned_of(kept, buffer, group, chunk):
        if not long:
            return kept[chunk, group * HEAD_DIM : (group + 1) * HEAD_DIM, :]
        first = (group % 2) * HEAD_DIM
        return chunk_of(buffer, group // 2, chunk).T[first : first + HEAD_DIM, :]

    def attend(group):
        tops = jnp.full((1, 2 * rows), MASKED, F32)

        def first_pass(chunk, top):
            part = self_scores(group, chunk)
            if not long:
                scores[group % 2, chunk] = part
            return jnp.maximum(top, jnp.max(part, axis=0, keepdims=True))

        def second_pass(chunk, state):
            total, acc = state
            part = self_scores(group, chunk) if long else scores[group % 2, chunk]
            part = jnp.exp(part - tops)
            total = total + jnp.sum(part, axis=0, keepdims=True)
            return total, acc + dot(turned_of(vT, vbuf, group, chunk), part.astype(BF))

        state = (jnp.zeros((1, 2 * rows), F32), jnp.zeros((HEAD_DIM, 2 * rows), F32))
        if not long:
            for chunk in range(half_count):
                tops = first_pass(chunk, tops)
            for chunk in range(half_count):
                state = second_pass(chunk, state)
        else:
            tops = lax.fori_loop(0, half_count, first_pass, tops)
            state = lax.fori_loop(0, half_count, second_pass, state)
        total, acc = state
        precise = acc / total
        att_self[group] = precise
        lse[group] = tops + jnp.log(total)
        right_all["so"][own["so"], :, group * 128 : (group + 1) * 128] = join_heads(precise).astype(BF)

    checkpoint(4)
    for group in range(groups):
        attend(group)

    checkpoint(5)
    copies.receive(("load", "so"))
    for tile in range(tiles):
        push(0, tile, dot_nt(right_all["so"][own["so"]], row_tile("so", tile)))
    valid = lax.broadcasted_iota(jnp.int32, (rows, 1), 0) + blk * rows < length
    bg[...] = jnp.where(valid, out_grad[...].astype(F32), 0.0).astype(BF)
    share_left("gf", bg[...])
    after_self[...] = x + summed_all(0)

    checkpoint(6)
    norm_into(after_self[...], ln_cross, nc, "nc")
    copies.receive(("load", "cq"))
    split_heads(dot(nc[...], whole("cq")).astype(BF), cqs)
    for group in range(groups):
        part = dot_nt(mk[group // 2], cqs[group])
        part = jnp.exp(part - jnp.max(part, axis=0, keepdims=True))
        part = part * (1.0 / jnp.sum(part, axis=0, keepdims=True))
        probs[group] = part
        acc = dot(mvT[group * HEAD_DIM : (group + 1) * HEAD_DIM, :], part.astype(BF))
        att_cross[group] = acc
        right_all["co"][own["co"], :, group * 128 : (group + 1) * 128] = join_heads(acc).astype(BF)
    checkpoint(7)
    copies.receive(("load", "co"))
    for tile in range(tiles):
        push(1, tile, dot_nt(right_all["co"][own["co"]], row_tile("co", tile)))
    share_right("so")
    share_right("co")
    after_cross[...] = after_self[...] + summed_all(1)

    checkpoint(8)
    norm_into(after_cross[...], ln_ffn, nf, "nf")
    for name in ("fg", "fu", "fd"):
        copies.receive(("load", name))
    for first, size in lane_tiles(weight["fg"].shape[1]):
        lanes = slice(first, first + size)
        gate = dot(nf[...], whole("fg", lanes))
        up = dot(nf[...], whole("fu", lanes))
        back = dot(bg[...], whole("fd", lanes))
        bent = jnp.tanh(GELU_A * (gate + GELU_B * gate * gate * gate))
        opened = 0.5 * (1.0 + bent)
        slope = opened + 0.5 * gate * (1.0 - bent * bent) * (
            GELU_A * (1.0 + 3.0 * GELU_B * gate * gate)
        )
        bell = gate * opened
        right_all["fd"][own["fd"], :, lanes] = (bell * up).astype(BF)
        right_all["fg"][own["fg"], :, lanes] = (back * up * slope).astype(BF)
        right_all["fu"][own["fu"], :, lanes] = (back * bell).astype(BF)
    for name in ("fd", "fg", "fu"):
        share_right(name)
    for tile in range(tiles):
        push(
            2,
            tile,
            dot_nt(right_all["fg"][own["fg"]], row_tile("fg", tile))
            + dot_nt(right_all["fu"][own["fu"]], row_tile("fu", tile)),
        )
    for tile in range(tiles):
        push(3, tile, dot_nt(right_all["fd"][own["fd"]], row_tile("fd", tile)))

    pass_right("so")
    pass_right("co")
    pass_right("fd")
    normed_grad = summed_all(2)
    cot[...] = jnp.where(valid, out_grad[...].astype(F32), 0.0) + norm_back(
        after_cross[...], ln_ffn, normed_grad, 2
    )
    bg[...] = cot[...].astype(BF)
    share_left("gc", bg[...])

    checkpoint(10)
    back = dot(bg[...], whole("co")).astype(BF)
    split_heads(back, ags)
    for pair in range(pairs):
        key_part = value_part = None
        for group in (2 * pair, 2 * pair + 1):
            prob = probs[group]
            prob_grad = dot_nt(mv[pair], ags[group])
            score_grad = (prob * (prob_grad - head_deltas(back, att_cross, group))).astype(BF)
            turned = dot(mkT[group * HEAD_DIM : (group + 1) * HEAD_DIM, :], score_grad)
            right_all["cq"][own["cq"], :, group * 128 : (group + 1) * 128] = join_heads(turned).astype(BF)
            key_new = dot(score_grad, cqs[group])
            value_new = dot(prob.astype(BF), ags[group])
            key_part = key_new if key_part is None else key_part + key_new
            value_part = value_new if value_part is None else value_part + value_new
        shape = dmem.shape[:-1]
        dmem[..., pair * 128 : (pair + 1) * 128] = key_part.astype(BF).reshape(*shape, 128)
        dmem[..., (pairs + pair) * 128 : (pairs + pair + 1) * 128] = value_part.astype(BF).reshape(
            *shape, 128
        )
    checkpoint(11)
    for tile in range(tiles):
        push(4, tile, dot_nt(right_all["cq"][own["cq"]], row_tile("cq", tile)))
    part_start(*dmem_args, 0)
    pass_right("fg")
    make_partial("fg")
    make_partial("fd")
    for tile in range(tiles):
        lanes = slice(tile * TILE, (tile + 1) * TILE)
        staged["layer_out"][:, lanes] = (after_cross[:, lanes] + summed(3, tile)).astype(BF)
    give("layer_out")
    normed_grad = summed_all(4)
    cot[...] = cot[...] + norm_back(after_self[...], ln_cross, normed_grad, 1)
    bg[...] = cot[...].astype(BF)
    share_left("gs", bg[...])

    def add_bias_gradient():
        row = lax.broadcasted_iota(jnp.int32, (rows, rows), 0)
        column = lax.broadcasted_iota(jnp.int32, (rows, rows), 1)
        slot_row = lax.broadcasted_iota(jnp.int32, (2 * groups, rows), 0)
        slot_lane = lax.broadcasted_iota(jnp.int32, (2 * groups, rows), 1)
        bucket = jnp.minimum(slot_lane, BUCKETS // 2)
        for start in bucket_starts()[BUCKETS // 2 :]:
            bucket = bucket + (slot_lane >= start).astype(jnp.int32)
        lines = jnp.zeros((2 * groups, rows), F32)
        last = jnp.zeros((2 * groups, rows), F32)
        for group in range(groups):
            for half in range(2):
                lanes = slice(half * rows, (half + 1) * rows)
                here = near[2, group, :, lanes].astype(F32)
                before = near[1, group, :, lanes].astype(F32)
                tile = here + jnp.where(column < row, before, 0.0)
                for bit in range(rows.bit_length() - 1):
                    moved = pltpu.roll(tile, rows - (1 << bit), 1)
                    tile = jnp.where(lax.rem(row // (1 << bit), 2) == 1, moved, tile)
                line = jnp.sum(tile, axis=0, keepdims=True)
                beyond = jnp.sum(jnp.where(column < row, 0.0, before), axis=0, keepdims=True)
                beyond = beyond + far_sum[group, :, lanes]
                slot = 2 * group + half
                lines = jnp.where(slot_row == slot, line, lines)
                last = jnp.where(slot_row == slot, beyond, last)
        wide = lax.broadcasted_iota(jnp.int32, (2 * groups, rows), 1)
        grid = jnp.zeros((2 * groups, rows), F32)
        for place in range(BUCKETS):
            total = jnp.sum(jnp.where(bucket == place, lines, 0.0), axis=1, keepdims=True)
            if place == BUCKETS - 1:
                total = total + jnp.sum(last, axis=1, keepdims=True)
            grid = jnp.where(wide == place, total, grid)
        first_bias = 3 * (width // 128)
        small[member(0), first_bias : first_bias + 2 * groups, :] = grid

    checkpoint(12)
    back = dot(bg[...], whole("so")).astype(BF)
    split_heads(back, ags)
    pass_right("fu")
    make_partial("fu")
    rs_step("fg", 0)
    near[1] = jnp.zeros(near.shape[1:], BF)
    for pair in range(pairs):
        members = (2 * pair, 2 * pair + 1)
        deltas = [head_deltas(back, att_self, group) for group in members]

        def visit(chunk, state, pair=pair, members=members, deltas=deltas):
            state = list(state)
            key_part = value_part = None
            values_here = chunk_of(vbuf, pair, chunk)
            for slot, group in enumerate(members):
                prob = jnp.exp(self_scores(group, chunk) - lse[group])
                prob_grad = dot_nt(values_here, ags[group])
                score_grad = (prob * (prob_grad - deltas[slot])).astype(BF)
                lhs = turned_of(kT, kbuf, group, chunk)
                state[2 * slot] = state[2 * slot] + dot(lhs, score_grad)
                key_new = dot(score_grad, qs[group])
                value_new = dot(prob.astype(BF), ags[group])
                key_part = key_new if key_part is None else key_part + key_new
                value_part = value_new if value_part is None else value_part + value_new
                for inner_block in range(2):
                    kind = kind_of(2 * chunk + inner_block)
                    piece = score_grad[inner_block * rows : (inner_block + 1) * rows, :]
                    near[lax.rem(kind, 3), group] = piece
                    is_far = (kind == 0).astype(F32)
                    state[2 * slot + 1] = state[2 * slot + 1] + is_far * jnp.sum(
                        piece.astype(F32), axis=0, keepdims=True
                    )
            where_to = (pair, *half_index(chunk))
            dkv[(*where_to, slice(None), slice(None), slice(0, 128))] = key_part.astype(BF).reshape(
                2, rows, 128
            )
            dkv[(*where_to, slice(None), slice(None), slice(128, 256))] = value_part.astype(
                BF
            ).reshape(2, rows, 128)
            return tuple(state)

        state = (jnp.zeros((HEAD_DIM, 2 * rows), F32), jnp.zeros((1, 2 * rows), F32)) * 2
        if not long:
            for chunk in range(half_count):
                state = visit(chunk, state)
        else:
            state = lax.fori_loop(0, half_count, visit, state)
        part_start(*dkv_args(pair), 0)
        if pair == 0:
            part_step(*dmem_args, 0)
            rs_step("fu", 0)
        for slot, group in enumerate(members):
            right_all["sq"][own["sq"], :, group * 128 : (group + 1) * 128] = join_heads(
                state[2 * slot]
            ).astype(BF)
            far_sum[group] = state[2 * slot + 1]
    checkpoint(13)
    share_right("cq")
    make_partial("co")
    share_right("sq")
    part_step(*dkv_args(0), 0)
    rs_step("fd", 0)
    make_partial("so")
    query_part = [
        dot_nt(right_all["sq"][own["sq"]], row_tile("sq", tile)) for tile in range(tiles)
    ]
    for step in range(1, bits - 1):
        rs_step("fg", step)
    part_step(*dkv_args(1), 0)
    part_step(*dmem_args, 1)
    for step in range(1, bits - 1):
        part_step(*dkv_args(0), step)
        part_step(*dkv_args(1), step)
    mem_sum = None
    for step in range(2, bits):
        mem_sum = part_step(*dmem_args, step)
    mem_sum = mem_sum.astype(BF)
    right_all["ck"][own["ck"]] = mem_sum[:, : pairs * 128]
    right_all["cv"][own["cv"]] = mem_sum[:, pairs * 128 :]
    share_right("ck")
    share_right("cv")
    pass_right("cq")
    make_partial("cq")
    sums = [part_step(*dkv_args(pair), bits - 1).astype(BF) for pair in range(pairs)]
    for pair, value in enumerate(sums):
        right_all["sk"][own["sk"], :, pair * 128 : (pair + 1) * 128] = value[:, :128]
        right_all["sv"][own["sv"], :, pair * 128 : (pair + 1) * 128] = value[:, 128:]
    share_right("sk")
    share_right("sv")
    for tile in range(tiles):
        push(
            5,
            tile,
            query_part[tile]
            + dot_nt(right_all["sk"][own["sk"]], row_tile("sk", tile))
            + dot_nt(right_all["sv"][own["sv"]], row_tile("sv", tile)),
        )
    pass_right("sq")
    make_partial("sq")
    rs_step("co", 0)
    rs_step("so", 0)
    for name in ("ck", "cv"):
        pass_right(name)
    for step in range(1, bits - 1):
        rs_step("fu", step)
        rs_step("fd", step)
    add_bias_gradient()

    checkpoint(14)
    mkg, mvg = right_all["ck"][own["ck"]], right_all["cv"][own["cv"]]
    mem_part = dot_nt(mkg, whole("ck")) + dot_nt(mvg, whole("cv"))
    half = share // 2
    mem_push[0] = mem_part[:half, :].astype(BF)
    mem_push[1] = mem_part[half:, :].astype(BF)
    mem_copy = pltpu.make_async_remote_copy(
        src_ref=mem_push.at[1 - head],
        dst_ref=mem_land,
        send_sem=mg_send,
        recv_sem=mg_recv,
        device_id=other_head,
        device_id_type=MESH,
    )
    copies.start(("mem",), mem_copy)
    for name in ("sk", "sv"):
        pass_right(name)
    for name in ("ck", "cv", "sk", "sv"):
        make_partial(name)
    rs_step("cq", 0)

    checkpoint(16)
    normed_grad = summed_all(5)
    staged["hidden_grad"][...] = cot[...] + norm_back(hidden[...].astype(F32), ln_self, normed_grad, 0)
    give("hidden_grad")

    def small_near(way):
        return pltpu.make_async_remote_copy(
            src_ref=small.at[member(0)],
            dst_ref=small.at[member(0)],
            send_sem=sm_send.at[way],
            recv_sem=sm_recv.at[way],
            device_id=peers(0)[way],
            device_id_type=MESH,
        )

    def small_across(way):
        return pltpu.make_async_remote_copy(
            src_ref=small_far.at[blk // 2],
            dst_ref=small_far.at[blk // 2],
            send_sem=sm_send.at[3 + way],
            recv_sem=sm_recv.at[3 + way],
            device_id=hop(far_masks[way]),
            device_id_type=MESH,
        )

    for way in (1, 2, 0):
        copies.start(("small", way), small_near(way))
    for step in range(1, bits - 1):
        for name in ("co", "so", "cq"):
            rs_step(name, step)
    rs_step("sq", 0)
    for way in range(3):
        copies.receive(("small", way))
    small_far[blk // 2] = small[0] + small[1] + small[2] + small[3]
    for way in range(len(far_masks)):
        copies.start(("small", 3 + way), small_across(way))
    for name in ("ck", "cv", "sk", "sv"):
        rs_finish(name)
    for step in range(1, bits - 1):
        rs_step("sq", step)
    for way in range(len(far_masks)):
        copies.receive(("small", 3 + way))
    total = small_far[0]
    for slot in range(1, blk_count // 2):
        total = total + small_far[slot]
    small_out[...] = total
    copies.receive(("mem",))
    staged["memory_grad"][...] = mem_push[head].astype(F32) + mem_land[...].astype(F32)
    give("memory_grad")


def finish_kernel(count, lines, width, *refs):
    sources, small = refs[:count], refs[count]
    targets = refs[count + 1 : 2 * count + 1]
    gain_out, bias_out, sems = refs[2 * count + 1 : 2 * count + 4], refs[2 * count + 4], refs[-1]
    moves = [
        pltpu.make_async_copy(source, target, sems.at[slot])
        for slot, (source, target) in enumerate(zip(sources, targets))
    ]
    for move in moves:
        move.start()
    share = gain_out[0].shape[0]
    per_line = 128 // share
    place = lax.axis_index("seq") * lax.axis_size("blk") + lax.axis_index("blk")
    for slot, target in enumerate(gain_out):
        line = small[pl.ds(slot * lines + place // per_line, 1), :]
        for part in range(per_line):

            @pl.when(lax.rem(place, per_line) == part)
            def _(target=target, line=line, part=part):
                target[...] = line[0, part * share : (part + 1) * share]

    bias_out[...] = small[3 * lines :, : bias_out.shape[1]]
    for move in moves:
        move.wait()


def finish(results, small, width, share, heads):
    count = len(results)
    in_any = pl.BlockSpec(memory_space=pl.ANY)
    in_vmem = pl.BlockSpec(memory_space=pltpu.VMEM)
    return pl.pallas_call(
        functools.partial(finish_kernel, count, width // 128, width),
        out_shape=[
            *(jax.ShapeDtypeStruct(result.shape, result.dtype) for result in results),
            *[jax.ShapeDtypeStruct((share,), F32)] * 3,
            jax.ShapeDtypeStruct((heads, BUCKETS), F32),
        ],
        in_specs=[in_vmem] * (count + 1),
        out_specs=[*[in_any] * count, *[in_vmem] * 4],
        scratch_shapes=[pltpu.SemaphoreType.DMA((count,))],
        name="finish",
    )(*results, small)


def run_layer(lengths, rel_bias, hidden, out_grad, gains, memory, weights, blk_count, stop=None):
    bits = blk_count.bit_length() - 1
    stages = bits + 1
    rows, width = hidden.shape
    groups = weights["sk"].shape[1] // HEAD_DIM
    heads = weights["sq"].shape[1] // HEAD_DIM
    mem_rows = memory.shape[0]
    if rows != 128 or heads != 2 * groups or bucket_starts()[-1] > rows or 1 << bits != blk_count:
        raise ValueError("unexpected sizes")
    pairs = groups // 2
    half_count = blk_count // 2
    long = half_count > 4
    stored = 1 if long else half_count
    piece = width // (2 * blk_count)
    widths = {name: weights[name].shape[1] for name in NAMES}
    share = mem_rows // blk_count
    small_rows = 3 * (width // 128) + heads

    vm, sem = pltpu.VMEM, pltpu.SemaphoreType.DMA
    high = (2,) * (bits - 1)
    depth = {name: share if LEFT_OF[name] == "mem" else rows for name in NAMES}
    scratch = [vm((width, widths[name]), BF) for name in NAMES]
    scratch += [
        vm((2, *high, 2, piece, share if left == "mem" else rows), BF) for left in LEFTS
    ]
    scratch += [
        vm((4, *high, piece, share) if left == "mem" else (*high, piece, 4 * rows), BF)
        for left in LEFTS
    ]
    scratch += [vm((4, depth[name], widths[name]), BF) for name in NAMES]
    scratch += [vm((*high, piece, widths[name]), BF) for name in NAMES]
    for name in NAMES:
        if name in DIRECT:
            scratch.append(vm((half_count - 1, piece, widths[name]), BF))
            continue
        for stage in range(bits - 1):
            scratch.append(vm((2,) * (bits - 2 - stage) + (piece, widths[name]), BF))
    by_bit = (2,) * bits
    scratch += [vm((rows, width), BF), vm((rows, width), F32), vm((share // 2, width), F32)]
    scratch += [vm((piece, widths[name]), F32) for name in NAMES]
    scratch += [
        vm(memory.shape, BF),
        vm((pairs, *by_bit, rows, 128), BF),
        vm((pairs, *by_bit, rows, 128), BF),
        vm((stored, groups * HEAD_DIM, 2 * rows), BF),
        vm((stored, groups * HEAD_DIM, 2 * rows), BF),
        vm((3, groups, rows, 2 * rows), F32),
        vm((3, groups, rows, 2 * rows), BF),
        vm((2, stored, 8 if long else 2 * rows, 2 * rows), F32),
        vm((groups, 2 * rows, 128), BF),
        vm((groups, 2 * rows, 128), BF),
        vm((groups, 2 * rows, 128), BF),
        vm((groups, HEAD_DIM, 2 * rows), F32),
        vm((groups, HEAD_DIM, 2 * rows), F32),
        vm((groups, 1, 2 * rows), F32),
        vm((groups, mem_rows, 2 * rows), F32),
        vm((pairs, mem_rows, 128), BF),
        vm((pairs, mem_rows, 128), BF),
        vm((groups * HEAD_DIM, mem_rows), BF),
        vm((groups * HEAD_DIM, mem_rows), BF),
        vm((4, width // TILE, rows, TILE), BF),
        vm((4, width // TILE, rows, TILE), BF),
        vm((rows, width), F32),
        vm((rows, width), F32),
        vm((rows, width), F32),
        vm((rows, width), BF),
        vm((rows, width), BF),
        vm((rows, width), BF),
        vm((rows, width), BF),
        vm((pairs, *by_bit, rows, 256), BF),
    ]
    scratch += [vm((pairs, *(2,) * (bits - 1 - stage), rows, 256), BF) for stage in range(bits)]
    scratch += [vm((*by_bit, share, 2 * groups * HEAD_DIM), BF)]
    scratch += [
        vm((*(2,) * (bits - 1 - stage), share, 2 * groups * HEAD_DIM), BF) for stage in range(bits)
    ]
    scratch += [
        vm((2, share // 2, width), BF),
        vm((share // 2, width), BF),
        vm((4, small_rows, 128), F32),
        vm((half_count, small_rows, 128), F32),
        vm((groups, 1, 2 * rows), F32),
        sem((len(NAMES) + 1,)),
        sem((6, width // TILE)),
        sem((6, width // TILE)),
        sem((2, half_count, 2)),
        sem((2, half_count, 2)),
        sem((len(NAMES), half_count)),
        sem((len(NAMES), half_count)),
        sem((len(LEFTS), 3)),
        sem((len(LEFTS), 3)),
        sem((len(NAMES), 3)),
        sem((len(NAMES), 3)),
        sem((3 + len(NAMES),)),
        sem((pairs, bits)),
        sem((pairs, bits)),
        sem((bits,)),
        sem((bits,)),
        sem,
        sem,
        sem((half_count + 2,)),
        sem((half_count + 2,)),
    ]
    in_vmem = pl.BlockSpec(memory_space=pltpu.VMEM)
    in_smem = pl.BlockSpec(memory_space=pltpu.SMEM)
    in_any = pl.BlockSpec(memory_space=pl.ANY)
    out_shape = [
        jax.ShapeDtypeStruct((rows, width), BF),
        jax.ShapeDtypeStruct((rows, width), F32),
        jax.ShapeDtypeStruct((share // 2, width), F32),
        *(jax.ShapeDtypeStruct((piece, widths[name]), F32) for name in NAMES),
        jax.ShapeDtypeStruct((small_rows, 128), F32),
    ]
    results = pl.pallas_call(
        functools.partial(layer_kernel, (bits, rows, width, groups, mem_rows), stop),
        out_shape=out_shape,
        in_specs=[in_smem, in_smem, *[in_vmem] * 5, *[in_any] * 12],
        out_specs=[*[in_any] * (len(out_shape) - 1), in_vmem],
        scratch_shapes=scratch,
        compiler_params=pltpu.CompilerParams(
            collective_id=0, has_side_effects=True, vmem_limit_bytes=63 * 1024 * 1024
        ),
        name="layer",
    )(
        lengths, rel_bias, hidden, out_grad, *gains, memory, *(weights[name] for name in NAMES)
    )
    return results[:3], dict(zip(NAMES, results[3:-1])), results[-1]


def body(
    hidden,
    memory,
    lengths,
    out_grad,
    ln_self,
    self_query,
    self_key,
    self_value,
    self_out,
    rel_bias,
    ln_cross,
    cross_query,
    cross_key,
    cross_value,
    cross_out,
    ln_ffn,
    ffn_gate,
    ffn_up,
    feedforward_down_weight,
):
    width = hidden.shape[1]
    blk_count = lax.axis_size("blk")
    weights = dict(
        sk=self_key,
        sv=self_value,
        sq=self_query,
        ck=cross_key,
        cv=cross_value,
        so=self_out,
        cq=cross_query,
        co=cross_out,
        fg=ffn_gate,
        fu=ffn_up,
        fd=feedforward_down_weight,
    )
    gains = [gain.reshape(1, width) for gain in (ln_self, ln_cross, ln_ffn)]
    (layer_out, hidden_grad, memory_grad), grads, small = run_layer(
        lengths, rel_bias.T, hidden, out_grad, gains, memory, weights, blk_count
    )
    kept = [layer_out, hidden_grad, memory_grad, *(grads[name] for name in NAMES)]
    *kept, self_gain, cross_gain, ffn_gain, bias_grad = finish(
        kept, small, width, width // (2 * blk_count), rel_bias.shape[1]
    )
    layer_out, hidden_grad, memory_grad = kept[:3]
    grads = dict(zip(NAMES, kept[3:]))
    return (
        layer_out,
        hidden_grad,
        memory_grad,
        self_gain,
        grads["sq"],
        grads["sk"],
        grads["sv"],
        grads["so"],
        bias_grad.T,
        cross_gain,
        grads["cq"],
        grads["ck"],
        grads["cv"],
        grads["co"],
        ffn_gain,
        grads["fg"],
        grads["fu"],
        grads["fd"],
    )


def solution(mesh):
    blocks = P(("seq", "blk"), None)
    by_head = P(None, "head")
    shares = P(("seq", "blk"), "head")
    line = P(("seq", "blk"))
    in_specs = (
        blocks,
        P("seq", None),
        P("seq"),
        blocks,
        P(),
        *[by_head] * 5,
        P(),
        *[by_head] * 4,
        P(),
        *[by_head] * 3,
    )
    out_specs = (
        blocks,
        blocks,
        P(("seq", "blk", "head"), None),
        line,
        *[shares] * 4,
        by_head,
        line,
        *[shares] * 4,
        line,
        *[shares] * 3,
    )
    return jax.shard_map(body, mesh=mesh, in_specs=in_specs, out_specs=out_specs, check_vma=False)
```

```python
import functools

import jax
import jax.numpy as jnp
import numpy as np
from jax import lax
from jax.experimental import pallas as pl
from jax.experimental.pallas import tpu as pltpu
from jax.sharding import PartitionSpec as P

MESH = pl.DeviceIdType.MESH
HEAD_DIM = 64
BUCKETS = 32
MAX_DIST = 128
EPSILON = 1e-06
MASKED = -1e30
BF = jnp.bfloat16
F32 = jnp.float32
TILE = 256
GELU_A = float(np.sqrt(2.0 / np.pi))
GELU_B = 0.044715

NAMES = ("sk", "sv", "sq", "ck", "cv", "so", "cq", "co", "fg", "fu", "fd")
LEFTS = ("ns", "nc", "nf", "gf", "gc", "gs", "mem")
LEFT_OF = dict(
    sk="ns", sv="ns", sq="ns", cq="nc", fg="nf", fu="nf", fd="gf", co="gc", so="gs", ck="mem", cv="mem"
)


def bucket_starts():
    exact = BUCKETS // 2
    far = np.ceil(exact * (MAX_DIST / exact) ** (np.arange(1, exact) / exact))
    return [*range(1, exact + 1), *(int(value) for value in far)]


def dot(left, right):
    return jnp.dot(left, right, preferred_element_type=F32)


def dot_nt(left, right):
    return lax.dot_general(left, right, (((1,), (1,)), ((), ())), preferred_element_type=F32)


def lane_tiles(width, step=512):
    return [(first, min(step, width - first)) for first in range(0, width, step)]
SHARED_BIT = dict(gf=1, gc=1, gs=1)
DIRECT = ("ck", "cv", "sk", "sv")


def shared_bit(name):
    return SHARED_BIT.get(LEFT_OF.get(name, name), 0)


class Stop(Exception):
    pass


class Copies:
    def __init__(self):
        self.made, self.started, self.received, self.sent = {}, [], set(), set()
        self.last = []

    def start(self, key, copy):
        self.made[key] = copy
        self.started.append(key)
        copy.start()

    def receive(self, key):
        self.received.add(key)
        copy = self.made[key]
        if key[0] == "load":
            copy.wait()
        else:
            copy.wait_recv()

    def leave(self, key):
        self.sent.add(key)
        self.made[key].wait_send()

    def drain(self):
        for key in self.started:
            if key not in self.received:
                self.receive(key)
        for key in self.started:
            if key[0] != "load" and key not in self.sent:
                self.leave(key)
        for wait in self.last:
            wait()


def layer_kernel(shapes, stop, *refs):
    copies = Copies()
    try:
        layer_steps(copies, shapes, stop, *refs)
    except Stop:
        pass
    copies.drain()


def layer_steps(copies, shapes, stop, *refs):
    bits, rows, width, groups, mem_rows = shapes
    stages = bits + 1
    blk_count = 1 << bits
    pairs = groups // 2
    half_count = blk_count // 2
    long = half_count > 4
    refs = list(refs)

    def take(count):
        taken, refs[:count] = refs[:count], []
        return taken

    lengths, rel_bias, hidden, out_grad, ln_self, ln_cross, ln_ffn, memory_in = take(8)
    weights_in = dict(zip(NAMES, take(11)))
    layer_out, hidden_grad, memory_grad = take(3)
    grads_out = dict(zip(NAMES, take(11)))
    results = {"layer_out": layer_out, "hidden_grad": hidden_grad, "memory_grad": memory_grad, **grads_out}
    (small_out,) = take(1)
    weight = dict(zip(NAMES, take(11)))
    left_own = dict(zip(LEFTS, take(len(LEFTS))))
    left_all = dict(zip(LEFTS, take(len(LEFTS))))
    right_all = dict(zip(NAMES, take(11)))
    partial = dict(zip(NAMES, take(11)))
    landing = {name: take(1 if name in DIRECT else bits - 1) for name in NAMES}
    staged = dict(zip(results, take(len(results))))
    (memory, kbuf, vbuf, vT, kT, tab, near, scores, qs, cqs, ags, att_self, att_cross) = take(13)
    (lse, probs, mk, mv, mkT, mvT, pushed, landed) = take(8)
    (after_self, after_cross, cot, ns, nc, nf, bg) = take(7)
    (dkv,) = take(1)
    dkv_land = take(bits)
    (dmem,) = take(1)
    dmem_land = take(bits)
    (mem_push, mem_land, small, small_far, far_sum) = take(5)
    (load_sem, hx_send, hx_recv, ag_send, ag_recv, rs_send, rs_recv) = take(7)
    (lf_send, lf_recv, rt_send, rt_recv, out_sem) = take(5)
    (dk_send, dk_recv, dm_send, dm_recv, mg_send, mg_recv, sm_send, sm_recv) = take(8)

    seq, blk, head = (lax.axis_index(name) for name in ("seq", "blk", "head"))
    mine = [lax.rem(blk // (1 << bit), 2) for bit in range(bits)]

    def across(bit):
        return (seq, blk + (1 - 2 * mine[bit]) * (1 << bit), head)

    other_seq = (1 - seq, blk, head)
    other_head = (seq, blk, 1 - head)

    def hop(mask):
        target = blk
        for bit in range(bits):
            if mask >> bit & 1:
                target = target + (1 - 2 * mine[bit]) * (1 << bit)
        return (seq, target, head)

    def member(bit):
        return 2 * seq + mine[bit]

    def peers(bit):
        far = across(bit)
        return (other_seq, far, (1 - seq, far[1], head))

    far_masks = [step << 1 for step in range(1, 1 << (bits - 1))]
    own = {name: member(shared_bit(name)) for name in NAMES}

    loads = {
        name: pltpu.make_async_copy(weights_in[name], weight[name], load_sem.at[slot])
        for slot, name in enumerate(NAMES)
    }
    memory_load = pltpu.make_async_copy(memory_in, memory, load_sem.at[len(NAMES)])
    for name in ("sk", "sv"):
        copies.start(("load", name), loads[name])

    def more_loads():
        copies.start(("load", "sq"), loads["sq"])
        copies.start(("load", "memory"), memory_load)
        for name in NAMES[3:]:
            copies.start(("load", name), loads[name])

    def checkpoint(place):
        if stop == place:
            raise Stop

    barrier = pltpu.get_barrier_semaphore()
    bits_used = sorted({shared_bit(name) for name in LEFTS})
    friends = [other_seq, other_head, across(0)]
    friends += [peers(bit)[2] for bit in bits_used]
    friends += [hop(mask) for mask in far_masks]
    for friend in friends:
        pl.semaphore_signal(barrier, inc=1, device_id=friend, device_id_type=MESH)

    def give(name):
        slot = list(results).index(name)
        copies.start(
            ("load", "out", name),
            pltpu.make_async_copy(staged[name], results[name], out_sem.at[slot]),
        )

    def whole(name, lanes=slice(None)):
        return weight[name][:, lanes]

    def row_tile(name, tile):
        return weight[name][tile * TILE : (tile + 1) * TILE, :]

    def inverse_norm(values):
        return lax.rsqrt(jnp.mean(values * values, axis=-1, keepdims=True) + EPSILON)

    def norm_into(values, gain, plain, left):
        plain[...] = (values * inverse_norm(values) * gain[...]).astype(BF)
        if left is not None:
            share_left(left, plain[...])

    def norm_back(values, gain, normed_grad, slot):
        scale = inverse_norm(values)
        unit = values * scale
        unit_grad = normed_grad * gain[...]
        line = jnp.sum(normed_grad * unit, axis=0, keepdims=True)
        for tile in range(width // 128):
            small[member(0), slot * (width // 128) + tile : slot * (width // 128) + tile + 1, :] = line[
                :, tile * 128 : (tile + 1) * 128
            ]
        return scale * (unit_grad - unit * jnp.mean(unit_grad * unit, axis=-1, keepdims=True))

    def hx(which, tile):
        return pltpu.make_async_remote_copy(
            src_ref=pushed.at[which % 4, tile],
            dst_ref=landed.at[which % 4, tile],
            send_sem=hx_send.at[which, tile],
            recv_sem=hx_recv.at[which, tile],
            device_id=other_head,
            device_id_type=MESH,
        )

    def push(which, tile, value):
        if which >= 4:
            copies.leave(("hx", which - 4, tile))
        pushed[which % 4, tile] = value.astype(BF)
        copies.start(("hx", which, tile), hx(which, tile))

    def summed(which, tile):
        copies.receive(("hx", which, tile))
        return pushed[which % 4, tile].astype(F32) + landed[which % 4, tile].astype(F32)

    tiles = width // TILE

    def summed_all(which):
        return jnp.concatenate([summed(which, tile) for tile in range(tiles)], axis=1)

    def lanes_of(slot, size):
        return pl.ds(pl.multiple_of(slot * size, size), size)

    def left_place(name, slot):
        if name == "mem":
            return left_all[name].at[slot]
        return left_all[name].at[(slice(None),) * bits + (lanes_of(slot, rows),)]

    def share_left(name, value):
        mine_left = left_own[name]
        bit = shared_bit(name)
        turned = value.T
        mine_left[...] = turned.reshape(mine_left.shape)

        def rows_of(half, low):
            index = [half]
            index += [low if place == bit else slice(None) for place in reversed(range(bits))]
            return tuple(index)

        left_place(name, member(bit))[...] = mine_left[rows_of(seq, mine[bit])]
        slot = LEFTS.index(name)
        for way, peer in enumerate(peers(bit)):
            there = rows_of(peer[0], mine[bit] if way == 0 else 1 - mine[bit])
            copies.start(
                ("left", name, way),
                pltpu.make_async_remote_copy(
                    src_ref=mine_left.at[there],
                    dst_ref=left_place(name, member(bit)),
                    send_sem=lf_send.at[slot, way],
                    recv_sem=lf_recv.at[slot, way],
                    device_id=peer,
                    device_id_type=MESH,
                ),
            )

    def right_copy(name, way, part=0, lanes=None):
        slot = NAMES.index(name)
        bit = shared_bit(name)
        place = right_all[name].at[own[name] if way < 2 else 2 * seq + 1 - mine[bit]]
        if lanes is not None:
            place = place.at[:, lanes]
        return pltpu.make_async_remote_copy(
            src_ref=place,
            dst_ref=place,
            send_sem=rt_send.at[slot, way, part],
            recv_sem=rt_recv.at[slot, way, part],
            device_id=across(bit) if way == 1 else other_seq,
            device_id_type=MESH,
        )

    def share_right(name, part=0, lanes=None):
        for way in (1, 0):
            copies.start(("right", name, way, part), right_copy(name, way, part, lanes))

    def parts_of(name, way):
        return [key for key in copies.started if key[:3] == ("right", name, way)]

    def pass_right(name):
        for key in parts_of(name, 1):
            copies.receive(key)
        copies.start(("right", name, 2, 0), right_copy(name, 2))

    def make_partial(name):
        left = LEFT_OF[name]
        for way in range(3):
            if ("left", left, way) not in copies.received:
                copies.receive(("left", left, way))
        for way in (0, 2):
            for key in parts_of(name, way):
                copies.receive(key)
        out = partial[name]
        count, depth, size = right_all[name].shape
        for first, step in lane_tiles(size):
            lanes = slice(first, first + step)
            if left == "mem":
                total = None
                for slot in range(count):
                    part = dot(
                        left_all[left][slot].reshape(width // 4, depth), right_all[name][slot, :, lanes]
                    )
                    total = part if total is None else total + part
            else:
                total = dot(
                    left_all[left][...].reshape(width // 4, count * depth),
                    right_all[name][:, :, lanes].reshape(count * depth, step),
                )
            out[..., lanes] = total.astype(BF).reshape(*out.shape[:-1], step)
        for stage in range(len(far_masks) if name in DIRECT else 1):
            copies.start(("rs", name, stage), rs_copy(name, stage))

    def bit_view(order, stage, keep):
        index = []
        for bit in reversed(range(bits)):
            if bit not in order:
                continue
            place = order.index(bit)
            if place < stage:
                index.append(mine[bit])
            elif place == stage:
                index.append(mine[bit] if keep else 1 - mine[bit])
            else:
                index.append(slice(None))
        return tuple(index)

    def rs_order(name):
        return [bit for bit in range(bits) if bit != shared_bit(name)]

    def rs_view(name, stage, keep):
        return partial[name].at[bit_view(rs_order(name), stage, keep)]

    def rs_copy(name, stage):
        slot = NAMES.index(name)
        if name in DIRECT:
            mask = far_masks[stage]
            place = tuple(
                1 - mine[bit] if mask >> bit & 1 else mine[bit] for bit in reversed(range(1, bits))
            )
            source, target, to = partial[name].at[place], landing[name][0].at[stage], hop(mask)
        else:
            source, target = rs_view(name, stage, False), landing[name][stage]
            to = across(rs_order(name)[stage])
        return pltpu.make_async_remote_copy(
            src_ref=source,
            dst_ref=target,
            send_sem=rs_send.at[slot, stage],
            recv_sem=rs_recv.at[slot, stage],
            device_id=to,
            device_id_type=MESH,
        )

    def fold_into(kept, got):
        lead = got.shape[:-2]
        for flat in range(int(np.prod(lead))):
            index = tuple(int(value) for value in np.unravel_index(flat, lead)) if lead else (Ellipsis,)
            kept[index] = (kept[index].astype(F32) + got[index].astype(F32)).astype(BF)

    def rs_finish(name):
        total = partial[name][tuple(mine[bit] for bit in reversed(range(1, bits)))].astype(F32)
        for stage in range(len(far_masks)):
            copies.receive(("rs", name, stage))
            total = total + landing[name][0][stage].astype(F32)
        staged[name][...] = total
        give(name)

    def rs_step(name, stage):
        copies.receive(("rs", name, stage))
        kept, got = rs_view(name, stage, True), landing[name][stage]
        if stage == bits - 2:
            staged[name][...] = kept[...].astype(F32) + got[...].astype(F32)
            give(name)
        else:
            fold_into(kept, got)
            copies.start(("rs", name, stage + 1), rs_copy(name, stage + 1))

    def part_copy(tag, buffer, land, send, recv, stage):
        order = list(range(bits))
        return pltpu.make_async_remote_copy(
            src_ref=buffer.at[bit_view(order, stage, False)],
            dst_ref=land[stage],
            send_sem=send.at[stage],
            recv_sem=recv.at[stage],
            device_id=across(order[stage]),
            device_id_type=MESH,
        )

    def part_start(tag, buffer, land, send, recv, stage):
        copies.start((tag, stage), part_copy(tag, buffer, land, send, recv, stage))

    def part_step(tag, buffer, land, send, recv, stage):
        order = list(range(bits))
        copies.receive((tag, stage))
        kept = buffer.at[bit_view(order, stage, True)]
        if stage == bits - 1:
            return kept[...].astype(F32) + land[stage][...].astype(F32)
        fold_into(kept, land[stage])
        part_start(tag, buffer, land, send, recv, stage + 1)

    def dkv_args(pair):
        return (
            ("dkv", pair),
            dkv.at[pair],
            [land.at[pair] for land in dkv_land],
            dk_send.at[pair],
            dk_recv.at[pair],
        )

    dmem_args = ("dmem", dmem, dmem_land, dm_send, dm_recv)

    level = blk // 2
    top = half_count - 1

    def ag_copy(which, step, up):
        place, digits = jnp.maximum(level - step, 0), []
        for _ in range(bits - 1):
            digits.append(lax.rem(place, 2))
            place = place // 2
        buffer = (kbuf, vbuf)[which]
        block = buffer.at[(slice(None), *reversed(digits), mine[0])]
        above = (seq, 2 * jnp.minimum(level + 1, top) + mine[0], head)
        return pltpu.make_async_remote_copy(
            src_ref=block,
            dst_ref=block,
            send_sem=ag_send.at[which, step, 0 if up else 1],
            recv_sem=ag_recv.at[which, step, 0 if up else 1],
            device_id=above if up else across(0),
            device_id_type=MESH,
        )

    def ag_step(which, step):
        @pl.when(level >= step)
        def _():
            if step > 0:
                ag_copy(which, step - 1, True).wait_recv()

            @pl.when(level < top)
            def _():
                ag_copy(which, step, True).start()

            ag_copy(which, step, False).start()

        def wait():
            @pl.when(level >= step)
            def _():
                @pl.when(level < top)
                def _():
                    ag_copy(which, step, True).wait_send()

                ag_copy(which, step, False).wait_send()

        copies.last.append(wait)

    def ag_end(which):
        for step in range(half_count):

            @pl.when(level >= step)
            def _(step=step):
                ag_copy(which, step, False).wait_recv()

    def clear_later():
        for place in range(1, half_count):
            digits = tuple(place >> bit & 1 for bit in reversed(range(bits - 1)))

            @pl.when(place > level)
            def _(digits=digits):
                for buffer in (kbuf, vbuf):
                    for pair in range(pairs):
                        buffer[(pair, *digits)] = jnp.zeros((2, rows, 128), BF)

    def half_index(chunk):
        index, left = [], chunk
        for _ in range(bits - 1):
            index.append(left % 2 if isinstance(left, int) else lax.rem(left, 2))
            left = left // 2
        return tuple(reversed(index))

    def chunk_of(buffer, pair, chunk):
        return buffer[(pair, *half_index(chunk))].reshape(2 * rows, 128)

    lane = lax.broadcasted_iota(jnp.int32, (rows, 128), 1)
    low = lane < HEAD_DIM
    swap_row = lax.broadcasted_iota(jnp.int32, (128, 128), 0)
    swap_col = lax.broadcasted_iota(jnp.int32, (128, 128), 1)
    swap = (swap_row == lax.rem(swap_col + HEAD_DIM, 128)).astype(F32).astype(BF)

    def split_heads(values, target):
        for group in range(groups):
            tile = values[:, group * 128 : (group + 1) * 128]
            swapped = dot(tile, swap)
            plain = tile.astype(F32)
            first, second = (plain, swapped) if group % 2 == 0 else (swapped, plain)
            here = low if group % 2 == 0 else jnp.logical_not(low)
            target[group, :rows, :] = jnp.where(here, first, 0.0).astype(BF)
            target[group, rows:, :] = jnp.where(here, second, 0.0).astype(BF)

    def join_heads(values):
        return jnp.concatenate([values[:, :rows], values[:, rows:]], axis=0).T

    def head_deltas(values, attended, group):
        turned = values[:, group * 128 : (group + 1) * 128].astype(F32).T
        laid = jnp.concatenate([turned[:HEAD_DIM, :], turned[HEAD_DIM:, :]], axis=1)
        return jnp.sum(laid * attended[group], axis=0, keepdims=True)

    length = lengths[0]
    reach = jnp.minimum(length, (blk + 1) * rows)
    key_row = lax.broadcasted_iota(jnp.int32, (rows, 2 * rows), 0)

    def kind_of(block):
        return jnp.clip(block - blk + 2, 0, 3)

    def self_scores(group, chunk):
        raw = dot_nt(chunk_of(kbuf, group // 2, chunk), qs[group])
        parts = []
        for inner_block in range(2):
            block = 2 * chunk + inner_block
            part = raw[inner_block * rows : (inner_block + 1) * rows, :]
            part = part + tab[jnp.minimum(kind_of(block), 2), group]
            parts.append(jnp.where(key_row + block * rows < reach, part, MASKED))
        return jnp.concatenate(parts, axis=0)

    checkpoint(0)
    pl.semaphore_wait(barrier, len(friends))
    x = hidden[...].astype(F32)
    norm_into(x, ln_self, ns, None)
    copies.receive(("load", "sk"))
    more_loads()
    keys = dot(ns[...], whole("sk")).astype(BF)
    for pair in range(pairs):
        kbuf[(pair, *reversed(mine))] = keys[:, pair * 128 : (pair + 1) * 128]
    ag_step(0, 0)
    copies.receive(("load", "sv"))
    values = dot(ns[...], whole("sv")).astype(BF)
    for pair in range(pairs):
        vbuf[(pair, *reversed(mine))] = values[:, pair * 128 : (pair + 1) * 128]
    ag_step(1, 0)
    clear_later()
    copies.receive(("load", "sq"))
    split_heads(dot(ns[...], whole("sq")).astype(BF), qs)
    for which in range(2):
        ag_step(which, 1)
    copies.receive(("load", "memory"))
    share = mem_rows // blk_count

    def project_memory(source, plain, turned):
        copies.receive(("load", source))
        result = dot(memory[...], whole(source)).astype(BF)
        for pair in range(pairs):
            plain[pair] = result[:, pair * 128 : (pair + 1) * 128]
            turned[pair * 128 : (pair + 1) * 128, :] = result[:, pair * 128 : (pair + 1) * 128].T

    project_memory("ck", mk, mkT)
    for which in range(2):
        ag_step(which, 2)
    project_memory("cv", mv, mvT)
    for step in range(3, half_count):
        for which in range(2):
            ag_step(which, step)

    starts = bucket_starts()
    distance = lane - lax.broadcasted_iota(jnp.int32, (rows, 128), 0)

    def bias_of(which, head_slot):
        shifted = distance + (rows if which == 1 else 0)
        value = jnp.full((rows, 128), rel_bias[head_slot, 0], F32)
        for bucket, start in enumerate(starts):
            value = jnp.where(shifted >= start, rel_bias[head_slot, bucket + 1], value)
        if which == 2:
            value = jnp.where(shifted >= 0, value, MASKED)
        return value

    def bias_tables(head_slot, carry):
        group = head_slot // 2
        lanes = pl.ds(pl.multiple_of(lax.rem(head_slot, 2) * rows, rows), rows)
        tab[0, group, :, lanes] = jnp.full((rows, rows), rel_bias[head_slot, BUCKETS - 1], F32)
        tab[1, group, :, lanes] = bias_of(1, head_slot)
        tab[2, group, :, lanes] = bias_of(2, head_slot)
        return carry

    lax.fori_loop(0, 2 * groups, bias_tables, 0)
    share_left("ns", ns[...])
    share_left("mem", memory[pl.ds(pl.multiple_of(blk * share, share), share), :])
    for which in range(2):
        ag_end(which)

    def turn_chunk(chunk):
        for pair in range(pairs):
            vT[chunk, pair * 128 : (pair + 1) * 128, :] = chunk_of(vbuf, pair, chunk).T
            kT[chunk, pair * 128 : (pair + 1) * 128, :] = chunk_of(kbuf, pair, chunk).T

    if not long:
        for chunk in range(half_count):
            turn_chunk(chunk)

    def turned_of(kept, buffer, group, chunk):
        if not long:
            return kept[chunk, group * HEAD_DIM : (group + 1) * HEAD_DIM, :]
        first = (group % 2) * HEAD_DIM
        return chunk_of(buffer, group // 2, chunk).T[first : first + HEAD_DIM, :]

    def attend(group):
        tops = jnp.full((1, 2 * rows), MASKED, F32)

        def first_pass(chunk, top):
            part = self_scores(group, chunk)
            if not long:
                scores[group % 2, chunk] = part
            return jnp.maximum(top, jnp.max(part, axis=0, keepdims=True))

        def second_pass(chunk, state):
            total, acc = state
            part = self_scores(group, chunk) if long else scores[group % 2, chunk]
            part = jnp.exp(part - tops)
            total = total + jnp.sum(part, axis=0, keepdims=True)
            return total, acc + dot(turned_of(vT, vbuf, group, chunk), part.astype(BF))

        state = (jnp.zeros((1, 2 * rows), F32), jnp.zeros((HEAD_DIM, 2 * rows), F32))
        if not long:
            for chunk in range(half_count):
                tops = first_pass(chunk, tops)
            for chunk in range(half_count):
                state = second_pass(chunk, state)
        else:
            tops = lax.fori_loop(0, half_count, first_pass, tops)
            state = lax.fori_loop(0, half_count, second_pass, state)
        total, acc = state
        precise = acc / total
        att_self[group] = precise
        lse[group] = tops + jnp.log(total)
        right_all["so"][own["so"], :, group * 128 : (group + 1) * 128] = join_heads(precise).astype(BF)

    checkpoint(4)
    for group in range(groups):
        attend(group)

    checkpoint(5)
    copies.receive(("load", "so"))
    for tile in range(tiles):
        push(0, tile, dot_nt(right_all["so"][own["so"]], row_tile("so", tile)))
    valid = lax.broadcasted_iota(jnp.int32, (rows, 1), 0) + blk * rows < length
    bg[...] = jnp.where(valid, out_grad[...].astype(F32), 0.0).astype(BF)
    share_left("gf", bg[...])
    after_self[...] = x + summed_all(0)

    checkpoint(6)
    norm_into(after_self[...], ln_cross, nc, "nc")
    copies.receive(("load", "cq"))
    split_heads(dot(nc[...], whole("cq")).astype(BF), cqs)
    for group in range(groups):
        part = dot_nt(mk[group // 2], cqs[group])
        part = jnp.exp(part - jnp.max(part, axis=0, keepdims=True))
        part = part * (1.0 / jnp.sum(part, axis=0, keepdims=True))
        probs[group] = part
        acc = dot(mvT[group * HEAD_DIM : (group + 1) * HEAD_DIM, :], part.astype(BF))
        att_cross[group] = acc
        right_all["co"][own["co"], :, group * 128 : (group + 1) * 128] = join_heads(acc).astype(BF)
    checkpoint(7)
    copies.receive(("load", "co"))
    for tile in range(tiles):
        push(1, tile, dot_nt(right_all["co"][own["co"]], row_tile("co", tile)))
    share_right("so")
    share_right("co")
    after_cross[...] = after_self[...] + summed_all(1)

    checkpoint(8)
    norm_into(after_cross[...], ln_ffn, nf, "nf")
    for name in ("fg", "fu", "fd"):
        copies.receive(("load", name))
    for part, (first, size) in enumerate(lane_tiles(weight["fg"].shape[1])):
        lanes = slice(first, first + size)
        gate = dot(nf[...], whole("fg", lanes))
        up = dot(nf[...], whole("fu", lanes))
        back = dot(bg[...], whole("fd", lanes))
        bent = jnp.tanh(GELU_A * (gate + GELU_B * gate * gate * gate))
        opened = 0.5 * (1.0 + bent)
        slope = opened + 0.5 * gate * (1.0 - bent * bent) * (
            GELU_A * (1.0 + 3.0 * GELU_B * gate * gate)
        )
        bell = gate * opened
        right_all["fd"][own["fd"], :, lanes] = (bell * up).astype(BF)
        right_all["fg"][own["fg"], :, lanes] = (back * up * slope).astype(BF)
        right_all["fu"][own["fu"], :, lanes] = (back * bell).astype(BF)
        share_right("fd", part, lanes)
        share_right("fg", part, lanes)
    share_right("fu")
    for tile in range(tiles):
        push(
            2,
            tile,
            dot_nt(right_all["fg"][own["fg"]], row_tile("fg", tile))
            + dot_nt(right_all["fu"][own["fu"]], row_tile("fu", tile)),
        )
    for tile in range(tiles):
        push(3, tile, dot_nt(right_all["fd"][own["fd"]], row_tile("fd", tile)))

    pass_right("so")
    pass_right("co")
    normed_grad = summed_all(2)
    cot[...] = jnp.where(valid, out_grad[...].astype(F32), 0.0) + norm_back(
        after_cross[...], ln_ffn, normed_grad, 2
    )
    bg[...] = cot[...].astype(BF)
    share_left("gc", bg[...])

    checkpoint(10)
    back = dot(bg[...], whole("co")).astype(BF)
    split_heads(back, ags)
    for pair in range(pairs):
        key_part = value_part = None
        for group in (2 * pair, 2 * pair + 1):
            prob = probs[group]
            prob_grad = dot_nt(mv[pair], ags[group])
            score_grad = (prob * (prob_grad - head_deltas(back, att_cross, group))).astype(BF)
            turned = dot(mkT[group * HEAD_DIM : (group + 1) * HEAD_DIM, :], score_grad)
            right_all["cq"][own["cq"], :, group * 128 : (group + 1) * 128] = join_heads(turned).astype(BF)
            key_new = dot(score_grad, cqs[group])
            value_new = dot(prob.astype(BF), ags[group])
            key_part = key_new if key_part is None else key_part + key_new
            value_part = value_new if value_part is None else value_part + value_new
        shape = dmem.shape[:-1]
        dmem[..., pair * 128 : (pair + 1) * 128] = key_part.astype(BF).reshape(*shape, 128)
        dmem[..., (pairs + pair) * 128 : (pairs + pair + 1) * 128] = value_part.astype(BF).reshape(
            *shape, 128
        )
    checkpoint(11)
    for tile in range(tiles):
        push(4, tile, dot_nt(right_all["cq"][own["cq"]], row_tile("cq", tile)))
    share_right("cq")
    part_start(*dmem_args, 0)
    pass_right("fd")
    pass_right("fg")
    make_partial("fg")
    make_partial("co")
    make_partial("fd")
    for tile in range(tiles):
        lanes = slice(tile * TILE, (tile + 1) * TILE)
        staged["layer_out"][:, lanes] = (after_cross[:, lanes] + summed(3, tile)).astype(BF)
    give("layer_out")
    normed_grad = summed_all(4)
    cot[...] = cot[...] + norm_back(after_self[...], ln_cross, normed_grad, 1)
    bg[...] = cot[...].astype(BF)
    share_left("gs", bg[...])

    def add_bias_gradient():
        row = lax.broadcasted_iota(jnp.int32, (rows, rows), 0)
        column = lax.broadcasted_iota(jnp.int32, (rows, rows), 1)
        slot_row = lax.broadcasted_iota(jnp.int32, (2 * groups, rows), 0)
        slot_lane = lax.broadcasted_iota(jnp.int32, (2 * groups, rows), 1)
        bucket = jnp.minimum(slot_lane, BUCKETS // 2)
        for start in bucket_starts()[BUCKETS // 2 :]:
            bucket = bucket + (slot_lane >= start).astype(jnp.int32)
        lines = jnp.zeros((2 * groups, rows), F32)
        last = jnp.zeros((2 * groups, rows), F32)
        for group in range(groups):
            for half in range(2):
                lanes = slice(half * rows, (half + 1) * rows)
                here = near[2, group, :, lanes].astype(F32)
                before = near[1, group, :, lanes].astype(F32)
                tile = here + jnp.where(column < row, before, 0.0)
                for bit in range(rows.bit_length() - 1):
                    moved = pltpu.roll(tile, rows - (1 << bit), 1)
                    tile = jnp.where(lax.rem(row // (1 << bit), 2) == 1, moved, tile)
                line = jnp.sum(tile, axis=0, keepdims=True)
                beyond = jnp.sum(jnp.where(column < row, 0.0, before), axis=0, keepdims=True)
                beyond = beyond + far_sum[group, :, lanes]
                slot = 2 * group + half
                lines = jnp.where(slot_row == slot, line, lines)
                last = jnp.where(slot_row == slot, beyond, last)
        wide = lax.broadcasted_iota(jnp.int32, (2 * groups, rows), 1)
        grid = jnp.zeros((2 * groups, rows), F32)
        for place in range(BUCKETS):
            total = jnp.sum(jnp.where(bucket == place, lines, 0.0), axis=1, keepdims=True)
            if place == BUCKETS - 1:
                total = total + jnp.sum(last, axis=1, keepdims=True)
            grid = jnp.where(wide == place, total, grid)
        first_bias = 3 * (width // 128)
        small[member(0), first_bias : first_bias + 2 * groups, :] = grid

    checkpoint(12)
    back = dot(bg[...], whole("so")).astype(BF)
    split_heads(back, ags)
    pass_right("fu")
    make_partial("fu")
    pass_right("cq")
    rs_step("fg", 0)
    near[1] = jnp.zeros(near.shape[1:], BF)
    for pair in range(pairs):
        members = (2 * pair, 2 * pair + 1)
        deltas = [head_deltas(back, att_self, group) for group in members]

        def visit(chunk, state, pair=pair, members=members, deltas=deltas):
            state = list(state)
            key_part = value_part = None
            values_here = chunk_of(vbuf, pair, chunk)
            for slot, group in enumerate(members):
                prob = jnp.exp(self_scores(group, chunk) - lse[group])
                prob_grad = dot_nt(values_here, ags[group])
                score_grad = (prob * (prob_grad - deltas[slot])).astype(BF)
                lhs = turned_of(kT, kbuf, group, chunk)
                state[2 * slot] = state[2 * slot] + dot(lhs, score_grad)
                key_new = dot(score_grad, qs[group])
                value_new = dot(prob.astype(BF), ags[group])
                key_part = key_new if key_part is None else key_part + key_new
                value_part = value_new if value_part is None else value_part + value_new
                for inner_block in range(2):
                    kind = kind_of(2 * chunk + inner_block)
                    piece = score_grad[inner_block * rows : (inner_block + 1) * rows, :]
                    near[lax.rem(kind, 3), group] = piece
                    is_far = (kind == 0).astype(F32)
                    state[2 * slot + 1] = state[2 * slot + 1] + is_far * jnp.sum(
                        piece.astype(F32), axis=0, keepdims=True
                    )
            where_to = (pair, *half_index(chunk))
            dkv[(*where_to, slice(None), slice(None), slice(0, 128))] = key_part.astype(BF).reshape(
                2, rows, 128
            )
            dkv[(*where_to, slice(None), slice(None), slice(128, 256))] = value_part.astype(
                BF
            ).reshape(2, rows, 128)
            return tuple(state)

        state = (jnp.zeros((HEAD_DIM, 2 * rows), F32), jnp.zeros((1, 2 * rows), F32)) * 2
        if not long:
            for chunk in range(half_count):
                state = visit(chunk, state)
        else:
            state = lax.fori_loop(0, half_count, visit, state)
        part_start(*dkv_args(pair), 0)
        if pair == 0:
            make_partial("so")
            part_step(*dmem_args, 0)
            rs_step("fu", 0)
        for slot, group in enumerate(members):
            right_all["sq"][own["sq"], :, group * 128 : (group + 1) * 128] = join_heads(
                state[2 * slot]
            ).astype(BF)
            far_sum[group] = state[2 * slot + 1]
    checkpoint(13)
    share_right("sq")
    make_partial("cq")
    rs_step("co", 0)
    part_step(*dmem_args, 1)
    part_step(*dkv_args(0), 0)
    rs_step("fd", 0)
    query_part = [
        dot_nt(right_all["sq"][own["sq"]], row_tile("sq", tile)) for tile in range(tiles)
    ]
    for step in range(1, bits - 1):
        rs_step("fg", step)
    part_step(*dkv_args(1), 0)
    mem_sum = None
    for step in range(2, bits):
        mem_sum = part_step(*dmem_args, step)
    mem_sum = mem_sum.astype(BF)
    right_all["ck"][own["ck"]] = mem_sum[:, : pairs * 128]
    right_all["cv"][own["cv"]] = mem_sum[:, pairs * 128 :]
    share_right("ck")
    share_right("cv")
    for step in range(1, bits - 1):
        part_step(*dkv_args(0), step)
        part_step(*dkv_args(1), step)
    rs_step("so", 0)
    pass_right("sq")
    make_partial("sq")
    for step in range(1, bits - 1):
        rs_step("fu", step)
    sums = [part_step(*dkv_args(pair), bits - 1).astype(BF) for pair in range(pairs)]
    for pair, value in enumerate(sums):
        right_all["sk"][own["sk"], :, pair * 128 : (pair + 1) * 128] = value[:, :128]
        right_all["sv"][own["sv"], :, pair * 128 : (pair + 1) * 128] = value[:, 128:]
    share_right("sk")
    share_right("sv")
    for tile in range(tiles):
        push(
            5,
            tile,
            query_part[tile]
            + dot_nt(right_all["sk"][own["sk"]], row_tile("sk", tile))
            + dot_nt(right_all["sv"][own["sv"]], row_tile("sv", tile)),
        )
    rs_step("cq", 0)
    for name in ("ck", "cv"):
        pass_right(name)
        make_partial(name)
    add_bias_gradient()
    for step in range(1, bits - 1):
        rs_step("co", step)
        rs_step("fd", step)

    checkpoint(14)
    mkg, mvg = right_all["ck"][own["ck"]], right_all["cv"][own["cv"]]
    mem_part = dot_nt(mkg, whole("ck")) + dot_nt(mvg, whole("cv"))
    half = share // 2
    mem_push[0] = mem_part[:half, :].astype(BF)
    mem_push[1] = mem_part[half:, :].astype(BF)
    mem_copy = pltpu.make_async_remote_copy(
        src_ref=mem_push.at[1 - head],
        dst_ref=mem_land,
        send_sem=mg_send,
        recv_sem=mg_recv,
        device_id=other_head,
        device_id_type=MESH,
    )
    copies.start(("mem",), mem_copy)
    for name in ("sk", "sv"):
        pass_right(name)
    for name in ("sk", "sv"):
        make_partial(name)

    checkpoint(16)
    normed_grad = summed_all(5)
    staged["hidden_grad"][...] = cot[...] + norm_back(hidden[...].astype(F32), ln_self, normed_grad, 0)
    give("hidden_grad")

    def small_near(way):
        return pltpu.make_async_remote_copy(
            src_ref=small.at[member(0)],
            dst_ref=small.at[member(0)],
            send_sem=sm_send.at[way],
            recv_sem=sm_recv.at[way],
            device_id=peers(0)[way],
            device_id_type=MESH,
        )

    def small_across(way):
        return pltpu.make_async_remote_copy(
            src_ref=small_far.at[blk // 2],
            dst_ref=small_far.at[blk // 2],
            send_sem=sm_send.at[3 + way],
            recv_sem=sm_recv.at[3 + way],
            device_id=hop(far_masks[way]),
            device_id_type=MESH,
        )

    for way in (1, 2, 0):
        copies.start(("small", way), small_near(way))
    for way in range(3):
        copies.receive(("small", way))
    small_far[blk // 2] = small[0] + small[1] + small[2] + small[3]
    for way in range(len(far_masks)):
        copies.start(("small", 3 + way), small_across(way))
    rs_step("sq", 0)
    for step in range(1, bits - 1):
        for name in ("so", "cq"):
            rs_step(name, step)
    for name in ("ck", "cv", "sk", "sv"):
        rs_finish(name)
    for step in range(1, bits - 1):
        rs_step("sq", step)
    for way in range(len(far_masks)):
        copies.receive(("small", 3 + way))
    total = small_far[0]
    for slot in range(1, blk_count // 2):
        total = total + small_far[slot]
    small_out[...] = total
    copies.receive(("mem",))
    staged["memory_grad"][...] = mem_push[head].astype(F32) + mem_land[...].astype(F32)
    give("memory_grad")


def finish_kernel(count, lines, width, *refs):
    sources, small = refs[:count], refs[count]
    targets = refs[count + 1 : 2 * count + 1]
    gain_out, bias_out, sems = refs[2 * count + 1 : 2 * count + 4], refs[2 * count + 4], refs[-1]
    moves = [
        pltpu.make_async_copy(source, target, sems.at[slot])
        for slot, (source, target) in enumerate(zip(sources, targets))
    ]
    for move in moves:
        move.start()
    share = gain_out[0].shape[0]
    per_line = 128 // share
    place = lax.axis_index("seq") * lax.axis_size("blk") + lax.axis_index("blk")
    for slot, target in enumerate(gain_out):
        line = small[pl.ds(slot * lines + place // per_line, 1), :]
        for part in range(per_line):

            @pl.when(lax.rem(place, per_line) == part)
            def _(target=target, line=line, part=part):
                target[...] = line[0, part * share : (part + 1) * share]

    bias_out[...] = small[3 * lines :, : bias_out.shape[1]]
    for move in moves:
        move.wait()


def finish(results, small, width, share, heads):
    count = len(results)
    in_any = pl.BlockSpec(memory_space=pl.ANY)
    in_vmem = pl.BlockSpec(memory_space=pltpu.VMEM)
    return pl.pallas_call(
        functools.partial(finish_kernel, count, width // 128, width),
        out_shape=[
            *(jax.ShapeDtypeStruct(result.shape, result.dtype) for result in results),
            *[jax.ShapeDtypeStruct((share,), F32)] * 3,
            jax.ShapeDtypeStruct((heads, BUCKETS), F32),
        ],
        in_specs=[in_vmem] * (count + 1),
        out_specs=[*[in_any] * count, *[in_vmem] * 4],
        scratch_shapes=[pltpu.SemaphoreType.DMA((count,))],
        name="finish",
    )(*results, small)


def run_layer(lengths, rel_bias, hidden, out_grad, gains, memory, weights, blk_count, stop=None):
    bits = blk_count.bit_length() - 1
    stages = bits + 1
    rows, width = hidden.shape
    groups = weights["sk"].shape[1] // HEAD_DIM
    heads = weights["sq"].shape[1] // HEAD_DIM
    mem_rows = memory.shape[0]
    if rows != 128 or heads != 2 * groups or bucket_starts()[-1] > rows or 1 << bits != blk_count:
        raise ValueError("unexpected sizes")
    pairs = groups // 2
    half_count = blk_count // 2
    long = half_count > 4
    stored = 1 if long else half_count
    piece = width // (2 * blk_count)
    widths = {name: weights[name].shape[1] for name in NAMES}
    share = mem_rows // blk_count
    small_rows = 3 * (width // 128) + heads

    vm, sem = pltpu.VMEM, pltpu.SemaphoreType.DMA
    high = (2,) * (bits - 1)
    depth = {name: share if LEFT_OF[name] == "mem" else rows for name in NAMES}
    scratch = [vm((width, widths[name]), BF) for name in NAMES]
    scratch += [
        vm((2, *high, 2, piece, share if left == "mem" else rows), BF) for left in LEFTS
    ]
    scratch += [
        vm((4, *high, piece, share) if left == "mem" else (*high, piece, 4 * rows), BF)
        for left in LEFTS
    ]
    scratch += [vm((4, depth[name], widths[name]), BF) for name in NAMES]
    scratch += [vm((*high, piece, widths[name]), BF) for name in NAMES]
    for name in NAMES:
        if name in DIRECT:
            scratch.append(vm((half_count - 1, piece, widths[name]), BF))
            continue
        for stage in range(bits - 1):
            scratch.append(vm((2,) * (bits - 2 - stage) + (piece, widths[name]), BF))
    by_bit = (2,) * bits
    scratch += [vm((rows, width), BF), vm((rows, width), F32), vm((share // 2, width), F32)]
    scratch += [vm((piece, widths[name]), F32) for name in NAMES]
    scratch += [
        vm(memory.shape, BF),
        vm((pairs, *by_bit, rows, 128), BF),
        vm((pairs, *by_bit, rows, 128), BF),
        vm((stored, groups * HEAD_DIM, 2 * rows), BF),
        vm((stored, groups * HEAD_DIM, 2 * rows), BF),
        vm((3, groups, rows, 2 * rows), F32),
        vm((3, groups, rows, 2 * rows), BF),
        vm((2, stored, 8 if long else 2 * rows, 2 * rows), F32),
        vm((groups, 2 * rows, 128), BF),
        vm((groups, 2 * rows, 128), BF),
        vm((groups, 2 * rows, 128), BF),
        vm((groups, HEAD_DIM, 2 * rows), F32),
        vm((groups, HEAD_DIM, 2 * rows), F32),
        vm((groups, 1, 2 * rows), F32),
        vm((groups, mem_rows, 2 * rows), F32),
        vm((pairs, mem_rows, 128), BF),
        vm((pairs, mem_rows, 128), BF),
        vm((groups * HEAD_DIM, mem_rows), BF),
        vm((groups * HEAD_DIM, mem_rows), BF),
        vm((4, width // TILE, rows, TILE), BF),
        vm((4, width // TILE, rows, TILE), BF),
        vm((rows, width), F32),
        vm((rows, width), F32),
        vm((rows, width), F32),
        vm((rows, width), BF),
        vm((rows, width), BF),
        vm((rows, width), BF),
        vm((rows, width), BF),
        vm((pairs, *by_bit, rows, 256), BF),
    ]
    scratch += [vm((pairs, *(2,) * (bits - 1 - stage), rows, 256), BF) for stage in range(bits)]
    scratch += [vm((*by_bit, share, 2 * groups * HEAD_DIM), BF)]
    scratch += [
        vm((*(2,) * (bits - 1 - stage), share, 2 * groups * HEAD_DIM), BF) for stage in range(bits)
    ]
    scratch += [
        vm((2, share // 2, width), BF),
        vm((share // 2, width), BF),
        vm((4, small_rows, 128), F32),
        vm((half_count, small_rows, 128), F32),
        vm((groups, 1, 2 * rows), F32),
        sem((len(NAMES) + 1,)),
        sem((6, width // TILE)),
        sem((6, width // TILE)),
        sem((2, half_count, 2)),
        sem((2, half_count, 2)),
        sem((len(NAMES), half_count)),
        sem((len(NAMES), half_count)),
        sem((len(LEFTS), 3)),
        sem((len(LEFTS), 3)),
        sem((len(NAMES), 3, 3)),
        sem((len(NAMES), 3, 3)),
        sem((3 + len(NAMES),)),
        sem((pairs, bits)),
        sem((pairs, bits)),
        sem((bits,)),
        sem((bits,)),
        sem,
        sem,
        sem((half_count + 2,)),
        sem((half_count + 2,)),
    ]
    in_vmem = pl.BlockSpec(memory_space=pltpu.VMEM)
    in_smem = pl.BlockSpec(memory_space=pltpu.SMEM)
    in_any = pl.BlockSpec(memory_space=pl.ANY)
    out_shape = [
        jax.ShapeDtypeStruct((rows, width), BF),
        jax.ShapeDtypeStruct((rows, width), F32),
        jax.ShapeDtypeStruct((share // 2, width), F32),
        *(jax.ShapeDtypeStruct((piece, widths[name]), F32) for name in NAMES),
        jax.ShapeDtypeStruct((small_rows, 128), F32),
    ]
    results = pl.pallas_call(
        functools.partial(layer_kernel, (bits, rows, width, groups, mem_rows), stop),
        out_shape=out_shape,
        in_specs=[in_smem, in_smem, *[in_vmem] * 5, *[in_any] * 12],
        out_specs=[*[in_any] * (len(out_shape) - 1), in_vmem],
        scratch_shapes=scratch,
        compiler_params=pltpu.CompilerParams(
            collective_id=0, has_side_effects=True, vmem_limit_bytes=63 * 1024 * 1024
        ),
        name="layer",
    )(
        lengths, rel_bias, hidden, out_grad, *gains, memory, *(weights[name] for name in NAMES)
    )
    return results[:3], dict(zip(NAMES, results[3:-1])), results[-1]


def body(
    hidden,
    memory,
    lengths,
    out_grad,
    ln_self,
    self_query,
    self_key,
    self_value,
    self_out,
    rel_bias,
    ln_cross,
    cross_query,
    cross_key,
    cross_value,
    cross_out,
    ln_ffn,
    ffn_gate,
    ffn_up,
    feedforward_down_weight,
):
    width = hidden.shape[1]
    blk_count = lax.axis_size("blk")
    weights = dict(
        sk=self_key,
        sv=self_value,
        sq=self_query,
        ck=cross_key,
        cv=cross_value,
        so=self_out,
        cq=cross_query,
        co=cross_out,
        fg=ffn_gate,
        fu=ffn_up,
        fd=feedforward_down_weight,
    )
    gains = [gain.reshape(1, width) for gain in (ln_self, ln_cross, ln_ffn)]
    (layer_out, hidden_grad, memory_grad), grads, small = run_layer(
        lengths, rel_bias.T, hidden, out_grad, gains, memory, weights, blk_count
    )
    kept = [layer_out, hidden_grad, memory_grad, *(grads[name] for name in NAMES)]
    *kept, self_gain, cross_gain, ffn_gain, bias_grad = finish(
        kept, small, width, width // (2 * blk_count), rel_bias.shape[1]
    )
    layer_out, hidden_grad, memory_grad = kept[:3]
    grads = dict(zip(NAMES, kept[3:]))
    return (
        layer_out,
        hidden_grad,
        memory_grad,
        self_gain,
        grads["sq"],
        grads["sk"],
        grads["sv"],
        grads["so"],
        bias_grad.T,
        cross_gain,
        grads["cq"],
        grads["ck"],
        grads["cv"],
        grads["co"],
        ffn_gain,
        grads["fg"],
        grads["fu"],
        grads["fd"],
    )


def solution(mesh):
    blocks = P(("seq", "blk"), None)
    by_head = P(None, "head")
    shares = P(("seq", "blk"), "head")
    line = P(("seq", "blk"))
    in_specs = (
        blocks,
        P("seq", None),
        P("seq"),
        blocks,
        P(),
        *[by_head] * 5,
        P(),
        *[by_head] * 4,
        P(),
        *[by_head] * 3,
    )
    out_specs = (
        blocks,
        blocks,
        P(("seq", "blk", "head"), None),
        line,
        *[shares] * 4,
        by_head,
        line,
        *[shares] * 4,
        line,
        *[shares] * 3,
    )
    return jax.shard_map(body, mesh=mesh, in_specs=in_specs, out_specs=out_specs, check_vma=False)
```

```python
import functools

import jax
import jax.numpy as jnp
import numpy as np
from jax import lax
from jax.experimental import pallas as pl
from jax.experimental.pallas import tpu as pltpu
from jax.sharding import PartitionSpec as P

MESH = pl.DeviceIdType.MESH
HEAD_DIM = 64
BUCKETS = 32
MAX_DIST = 128
EPSILON = 1e-06
MASKED = -1e30
BF = jnp.bfloat16
F32 = jnp.float32
TILE = 256
GELU_A = float(np.sqrt(2.0 / np.pi))
GELU_B = 0.044715

NAMES = ("sk", "sv", "sq", "ck", "cv", "so", "cq", "co", "fg", "fu", "fd")
LEFTS = ("ns", "nc", "nf", "gf", "gc", "gs", "mem")
LEFT_OF = dict(
    sk="ns", sv="ns", sq="ns", cq="nc", fg="nf", fu="nf", fd="gf", co="gc", so="gs", ck="mem", cv="mem"
)


def bucket_starts():
    exact = BUCKETS // 2
    far = np.ceil(exact * (MAX_DIST / exact) ** (np.arange(1, exact) / exact))
    return [*range(1, exact + 1), *(int(value) for value in far)]


def dot(left, right):
    return jnp.dot(left, right, preferred_element_type=F32)


def dot_nt(left, right):
    return lax.dot_general(left, right, (((1,), (1,)), ((), ())), preferred_element_type=F32)


def lane_tiles(width, step=512):
    return [(first, min(step, width - first)) for first in range(0, width, step)]
SHARED_BIT = dict(gf=1, gc=1, gs=1)
DIRECT = ("sk", "sv")


def shared_bit(name):
    return SHARED_BIT.get(LEFT_OF.get(name, name), 0)


class Stop(Exception):
    pass


class Copies:
    def __init__(self):
        self.made, self.started, self.received, self.sent = {}, [], set(), set()
        self.last = []

    def start(self, key, copy):
        self.made[key] = copy
        self.started.append(key)
        copy.start()

    def receive(self, key):
        self.received.add(key)
        copy = self.made[key]
        if key[0] == "load":
            copy.wait()
        else:
            copy.wait_recv()

    def leave(self, key):
        self.sent.add(key)
        self.made[key].wait_send()

    def drain(self):
        for key in self.started:
            if key not in self.received:
                self.receive(key)
        for key in self.started:
            if key[0] != "load" and key not in self.sent:
                self.leave(key)
        for wait in self.last:
            wait()


def layer_kernel(shapes, stop, *refs):
    copies = Copies()
    try:
        layer_steps(copies, shapes, stop, *refs)
    except Stop:
        pass
    copies.drain()


def layer_steps(copies, shapes, stop, *refs):
    bits, rows, width, groups, mem_rows = shapes
    stages = bits + 1
    blk_count = 1 << bits
    pairs = groups // 2
    half_count = blk_count // 2
    long = half_count > 4
    refs = list(refs)

    def take(count):
        taken, refs[:count] = refs[:count], []
        return taken

    lengths, rel_bias, hidden, out_grad, ln_self, ln_cross, ln_ffn, memory_in = take(8)
    weights_in = dict(zip(NAMES, take(11)))
    layer_out, hidden_grad, memory_grad = take(3)
    grads_out = dict(zip(NAMES, take(11)))
    results = {"layer_out": layer_out, "hidden_grad": hidden_grad, "memory_grad": memory_grad, **grads_out}
    (small_out,) = take(1)
    weight = dict(zip(NAMES, take(11)))
    left_own = dict(zip(LEFTS, take(len(LEFTS))))
    left_all = dict(zip(LEFTS, take(len(LEFTS))))
    right_all = dict(zip(NAMES, take(11)))
    partial = dict(zip(NAMES, take(11)))
    landing = {name: take(1 if name in DIRECT else bits - 1) for name in NAMES}
    staged = dict(zip(results, take(len(results))))
    (memory, kbuf, vbuf, vT, kT, tab, near, scores, qs, cqs, ags, att_self, att_cross) = take(13)
    (lse, probs, mk, mv, mkT, mvT, pushed, landed) = take(8)
    (after_self, after_cross, cot, ns, nc, nf, bg, inner_grad) = take(8)
    (dkv,) = take(1)
    dkv_land = take(bits)
    (dmem,) = take(1)
    dmem_land = take(bits)
    (mem_push, mem_land, small, small_far, far_sum) = take(5)
    (load_sem, hx_send, hx_recv, ag_send, ag_recv, rs_send, rs_recv) = take(7)
    (lf_send, lf_recv, rt_send, rt_recv, out_sem) = take(5)
    (dk_send, dk_recv, dm_send, dm_recv, mg_send, mg_recv, sm_send, sm_recv) = take(8)

    seq, blk, head = (lax.axis_index(name) for name in ("seq", "blk", "head"))
    mine = [lax.rem(blk // (1 << bit), 2) for bit in range(bits)]

    def across(bit):
        return (seq, blk + (1 - 2 * mine[bit]) * (1 << bit), head)

    other_seq = (1 - seq, blk, head)
    other_head = (seq, blk, 1 - head)

    def hop(mask):
        target = blk
        for bit in range(bits):
            if mask >> bit & 1:
                target = target + (1 - 2 * mine[bit]) * (1 << bit)
        return (seq, target, head)

    def member(bit):
        return 2 * seq + mine[bit]

    def peers(bit):
        far = across(bit)
        return (other_seq, far, (1 - seq, far[1], head))

    far_masks = [step << 1 for step in range(1, 1 << (bits - 1))]
    own = {name: member(shared_bit(name)) for name in NAMES}

    loads = {
        name: pltpu.make_async_copy(weights_in[name], weight[name], load_sem.at[slot])
        for slot, name in enumerate(NAMES)
    }
    memory_load = pltpu.make_async_copy(memory_in, memory, load_sem.at[len(NAMES)])
    for name in ("sk", "sv"):
        copies.start(("load", name), loads[name])

    def more_loads():
        copies.start(("load", "sq"), loads["sq"])
        copies.start(("load", "memory"), memory_load)
        for name in NAMES[3:]:
            copies.start(("load", name), loads[name])

    def checkpoint(place):
        if stop == place:
            raise Stop

    barrier = pltpu.get_barrier_semaphore()
    bits_used = sorted({shared_bit(name) for name in LEFTS})
    friends = [other_seq, other_head, across(0)]
    friends += [peers(bit)[2] for bit in bits_used]
    friends += [hop(mask) for mask in far_masks]
    for friend in friends:
        pl.semaphore_signal(barrier, inc=1, device_id=friend, device_id_type=MESH)

    def give(name):
        slot = list(results).index(name)
        copies.start(
            ("load", "out", name),
            pltpu.make_async_copy(staged[name], results[name], out_sem.at[slot]),
        )

    def whole(name, lanes=slice(None)):
        return weight[name][:, lanes]

    def row_tile(name, tile):
        return weight[name][tile * TILE : (tile + 1) * TILE, :]

    def inverse_norm(values):
        return lax.rsqrt(jnp.mean(values * values, axis=-1, keepdims=True) + EPSILON)

    def norm_into(values, gain, plain, left):
        plain[...] = (values * inverse_norm(values) * gain[...]).astype(BF)
        if left is not None:
            share_left(left, plain[...])

    def norm_back(values, gain, normed_grad, slot):
        scale = inverse_norm(values)
        unit = values * scale
        unit_grad = normed_grad * gain[...]
        line = jnp.sum(normed_grad * unit, axis=0, keepdims=True)
        for tile in range(width // 128):
            small[member(0), slot * (width // 128) + tile : slot * (width // 128) + tile + 1, :] = line[
                :, tile * 128 : (tile + 1) * 128
            ]
        return scale * (unit_grad - unit * jnp.mean(unit_grad * unit, axis=-1, keepdims=True))

    def hx(which, tile):
        return pltpu.make_async_remote_copy(
            src_ref=pushed.at[which % 4, tile],
            dst_ref=landed.at[which % 4, tile],
            send_sem=hx_send.at[which, tile],
            recv_sem=hx_recv.at[which, tile],
            device_id=other_head,
            device_id_type=MESH,
        )

    def push(which, tile, value):
        if which >= 4:
            copies.leave(("hx", which - 4, tile))
        pushed[which % 4, tile] = value.astype(BF)
        copies.start(("hx", which, tile), hx(which, tile))

    def summed(which, tile):
        copies.receive(("hx", which, tile))
        return pushed[which % 4, tile].astype(F32) + landed[which % 4, tile].astype(F32)

    tiles = width // TILE

    def summed_all(which):
        return jnp.concatenate([summed(which, tile) for tile in range(tiles)], axis=1)

    def lanes_of(slot, size):
        return pl.ds(pl.multiple_of(slot * size, size), size)

    def left_place(name, slot):
        if name == "mem":
            return left_all[name].at[slot]
        return left_all[name].at[(slice(None),) * bits + (lanes_of(slot, rows),)]

    def share_left(name, value):
        mine_left = left_own[name]
        bit = shared_bit(name)
        turned = value.T
        mine_left[...] = turned.reshape(mine_left.shape)

        def rows_of(half, low):
            index = [half]
            index += [low if place == bit else slice(None) for place in reversed(range(bits))]
            return tuple(index)

        left_place(name, member(bit))[...] = mine_left[rows_of(seq, mine[bit])]
        slot = LEFTS.index(name)
        for way, peer in enumerate(peers(bit)):
            there = rows_of(peer[0], mine[bit] if way == 0 else 1 - mine[bit])
            copies.start(
                ("left", name, way),
                pltpu.make_async_remote_copy(
                    src_ref=mine_left.at[there],
                    dst_ref=left_place(name, member(bit)),
                    send_sem=lf_send.at[slot, way],
                    recv_sem=lf_recv.at[slot, way],
                    device_id=peer,
                    device_id_type=MESH,
                ),
            )

    def right_copy(name, way, part=0, lanes=None):
        slot = NAMES.index(name)
        bit = shared_bit(name)
        place = right_all[name].at[own[name] if way < 2 else 2 * seq + 1 - mine[bit]]
        if lanes is not None:
            place = place.at[:, lanes]
        return pltpu.make_async_remote_copy(
            src_ref=place,
            dst_ref=place,
            send_sem=rt_send.at[slot, way, part],
            recv_sem=rt_recv.at[slot, way, part],
            device_id=across(bit) if way == 1 else other_seq,
            device_id_type=MESH,
        )

    def share_right(name, part=0, lanes=None):
        for way in (1, 0):
            copies.start(("right", name, way, part), right_copy(name, way, part, lanes))

    def parts_of(name, way):
        return [key for key in copies.started if key[:3] == ("right", name, way)]

    def pass_right(name):
        for key in parts_of(name, 1):
            copies.receive(key)
        copies.start(("right", name, 2, 0), right_copy(name, 2))

    def make_partial(name):
        left = LEFT_OF[name]
        for way in range(3):
            if ("left", left, way) not in copies.received:
                copies.receive(("left", left, way))
        for way in (0, 2):
            for key in parts_of(name, way):
                copies.receive(key)
        out = partial[name]
        count, depth, size = right_all[name].shape
        for first, step in lane_tiles(size):
            lanes = slice(first, first + step)
            if left == "mem":
                total = None
                for slot in range(count):
                    part = dot(
                        left_all[left][slot].reshape(width // 4, depth), right_all[name][slot, :, lanes]
                    )
                    total = part if total is None else total + part
            else:
                total = dot(
                    left_all[left][...].reshape(width // 4, count * depth),
                    right_all[name][:, :, lanes].reshape(count * depth, step),
                )
            out[..., lanes] = total.astype(BF).reshape(*out.shape[:-1], step)
        for stage in range(len(far_masks) if name in DIRECT else 1):
            copies.start(("rs", name, stage), rs_copy(name, stage))

    def bit_view(order, stage, keep):
        index = []
        for bit in reversed(range(bits)):
            if bit not in order:
                continue
            place = order.index(bit)
            if place < stage:
                index.append(mine[bit])
            elif place == stage:
                index.append(mine[bit] if keep else 1 - mine[bit])
            else:
                index.append(slice(None))
        return tuple(index)

    def rs_order(name):
        return [bit for bit in range(bits) if bit != shared_bit(name)]

    def rs_view(name, stage, keep):
        return partial[name].at[bit_view(rs_order(name), stage, keep)]

    def rs_copy(name, stage):
        slot = NAMES.index(name)
        if name in DIRECT:
            mask = far_masks[stage]
            place = tuple(
                1 - mine[bit] if mask >> bit & 1 else mine[bit] for bit in reversed(range(1, bits))
            )
            source, target, to = partial[name].at[place], landing[name][0].at[stage], hop(mask)
        else:
            source, target = rs_view(name, stage, False), landing[name][stage]
            to = across(rs_order(name)[stage])
        return pltpu.make_async_remote_copy(
            src_ref=source,
            dst_ref=target,
            send_sem=rs_send.at[slot, stage],
            recv_sem=rs_recv.at[slot, stage],
            device_id=to,
            device_id_type=MESH,
        )

    def fold_into(kept, got):
        lead = got.shape[:-2]
        for flat in range(int(np.prod(lead))):
            index = tuple(int(value) for value in np.unravel_index(flat, lead)) if lead else (Ellipsis,)
            kept[index] = (kept[index].astype(F32) + got[index].astype(F32)).astype(BF)

    def rs_finish(name):
        total = partial[name][tuple(mine[bit] for bit in reversed(range(1, bits)))].astype(F32)
        for stage in range(len(far_masks)):
            copies.receive(("rs", name, stage))
            total = total + landing[name][0][stage].astype(F32)
        staged[name][...] = total
        give(name)

    def rs_step(name, stage):
        copies.receive(("rs", name, stage))
        kept, got = rs_view(name, stage, True), landing[name][stage]
        if stage == bits - 2:
            staged[name][...] = kept[...].astype(F32) + got[...].astype(F32)
            give(name)
        else:
            fold_into(kept, got)
            copies.start(("rs", name, stage + 1), rs_copy(name, stage + 1))

    def part_copy(tag, buffer, land, send, recv, stage):
        order = list(range(bits))
        return pltpu.make_async_remote_copy(
            src_ref=buffer.at[bit_view(order, stage, False)],
            dst_ref=land[stage],
            send_sem=send.at[stage],
            recv_sem=recv.at[stage],
            device_id=across(order[stage]),
            device_id_type=MESH,
        )

    def part_start(tag, buffer, land, send, recv, stage):
        copies.start((tag, stage), part_copy(tag, buffer, land, send, recv, stage))

    def part_step(tag, buffer, land, send, recv, stage):
        order = list(range(bits))
        copies.receive((tag, stage))
        kept = buffer.at[bit_view(order, stage, True)]
        if stage == bits - 1:
            return kept[...].astype(F32) + land[stage][...].astype(F32)
        fold_into(kept, land[stage])
        part_start(tag, buffer, land, send, recv, stage + 1)

    def dkv_args(pair):
        return (
            ("dkv", pair),
            dkv.at[pair],
            [land.at[pair] for land in dkv_land],
            dk_send.at[pair],
            dk_recv.at[pair],
        )

    dmem_args = ("dmem", dmem, dmem_land, dm_send, dm_recv)

    level = blk // 2
    top = half_count - 1

    def ag_copy(which, step, up):
        place, digits = jnp.maximum(level - step, 0), []
        for _ in range(bits - 1):
            digits.append(lax.rem(place, 2))
            place = place // 2
        buffer = (kbuf, vbuf)[which]
        block = buffer.at[(slice(None), *reversed(digits), mine[0])]
        above = (seq, 2 * jnp.minimum(level + 1, top) + mine[0], head)
        return pltpu.make_async_remote_copy(
            src_ref=block,
            dst_ref=block,
            send_sem=ag_send.at[which, step, 0 if up else 1],
            recv_sem=ag_recv.at[which, step, 0 if up else 1],
            device_id=above if up else across(0),
            device_id_type=MESH,
        )

    def ag_step(which, step):
        @pl.when(level >= step)
        def _():
            if step > 0:
                ag_copy(which, step - 1, True).wait_recv()

            @pl.when(level < top)
            def _():
                ag_copy(which, step, True).start()

            ag_copy(which, step, False).start()

        def wait():
            @pl.when(level >= step)
            def _():
                @pl.when(level < top)
                def _():
                    ag_copy(which, step, True).wait_send()

                ag_copy(which, step, False).wait_send()

        copies.last.append(wait)

    def ag_end(which):
        for step in range(half_count):

            @pl.when(level >= step)
            def _(step=step):
                ag_copy(which, step, False).wait_recv()

    def clear_later():
        for place in range(1, half_count):
            digits = tuple(place >> bit & 1 for bit in reversed(range(bits - 1)))

            @pl.when(place > level)
            def _(digits=digits):
                for buffer in (kbuf, vbuf):
                    for pair in range(pairs):
                        buffer[(pair, *digits)] = jnp.zeros((2, rows, 128), BF)

    def half_index(chunk):
        index, left = [], chunk
        for _ in range(bits - 1):
            index.append(left % 2 if isinstance(left, int) else lax.rem(left, 2))
            left = left // 2
        return tuple(reversed(index))

    def chunk_of(buffer, pair, chunk):
        return buffer[(pair, *half_index(chunk))].reshape(2 * rows, 128)

    lane = lax.broadcasted_iota(jnp.int32, (rows, 128), 1)
    low = lane < HEAD_DIM
    swap_row = lax.broadcasted_iota(jnp.int32, (128, 128), 0)
    swap_col = lax.broadcasted_iota(jnp.int32, (128, 128), 1)
    swap = (swap_row == lax.rem(swap_col + HEAD_DIM, 128)).astype(F32).astype(BF)

    def split_heads(values, target):
        for group in range(groups):
            tile = values[:, group * 128 : (group + 1) * 128]
            swapped = dot(tile, swap)
            plain = tile.astype(F32)
            first, second = (plain, swapped) if group % 2 == 0 else (swapped, plain)
            here = low if group % 2 == 0 else jnp.logical_not(low)
            target[group, :rows, :] = jnp.where(here, first, 0.0).astype(BF)
            target[group, rows:, :] = jnp.where(here, second, 0.0).astype(BF)

    def join_heads(values):
        return jnp.concatenate([values[:, :rows], values[:, rows:]], axis=0).T

    def head_deltas(values, attended, group):
        turned = values[:, group * 128 : (group + 1) * 128].astype(F32).T
        laid = jnp.concatenate([turned[:HEAD_DIM, :], turned[HEAD_DIM:, :]], axis=1)
        return jnp.sum(laid * attended[group], axis=0, keepdims=True)

    length = lengths[0]
    reach = jnp.minimum(length, (blk + 1) * rows)
    key_row = lax.broadcasted_iota(jnp.int32, (rows, 2 * rows), 0)

    def kind_of(block):
        return jnp.clip(block - blk + 2, 0, 3)

    def self_scores(group, chunk):
        raw = dot_nt(chunk_of(kbuf, group // 2, chunk), qs[group])
        parts = []
        for inner_block in range(2):
            block = 2 * chunk + inner_block
            part = raw[inner_block * rows : (inner_block + 1) * rows, :]
            part = part + tab[jnp.minimum(kind_of(block), 2), group]
            parts.append(jnp.where(key_row + block * rows < reach, part, MASKED))
        return jnp.concatenate(parts, axis=0)

    checkpoint(0)
    pl.semaphore_wait(barrier, len(friends))
    x = hidden[...].astype(F32)
    norm_into(x, ln_self, ns, None)
    copies.receive(("load", "sk"))
    more_loads()
    keys = dot(ns[...], whole("sk")).astype(BF)
    for pair in range(pairs):
        kbuf[(pair, *reversed(mine))] = keys[:, pair * 128 : (pair + 1) * 128]
    ag_step(0, 0)
    copies.receive(("load", "sv"))
    values = dot(ns[...], whole("sv")).astype(BF)
    for pair in range(pairs):
        vbuf[(pair, *reversed(mine))] = values[:, pair * 128 : (pair + 1) * 128]
    ag_step(1, 0)
    clear_later()
    copies.receive(("load", "sq"))
    split_heads(dot(ns[...], whole("sq")).astype(BF), qs)
    for which in range(2):
        ag_step(which, 1)
    copies.receive(("load", "memory"))
    share = mem_rows // blk_count

    def project_memory(source, plain, turned):
        copies.receive(("load", source))
        result = dot(memory[...], whole(source)).astype(BF)
        for pair in range(pairs):
            plain[pair] = result[:, pair * 128 : (pair + 1) * 128]
            turned[pair * 128 : (pair + 1) * 128, :] = result[:, pair * 128 : (pair + 1) * 128].T

    project_memory("ck", mk, mkT)
    for which in range(2):
        ag_step(which, 2)
    project_memory("cv", mv, mvT)
    for step in range(3, half_count):
        for which in range(2):
            ag_step(which, step)

    starts = bucket_starts()
    distance = lane - lax.broadcasted_iota(jnp.int32, (rows, 128), 0)

    def bias_of(which, head_slot):
        shifted = distance + (rows if which == 1 else 0)
        value = jnp.full((rows, 128), rel_bias[head_slot, 0], F32)
        for bucket, start in enumerate(starts):
            value = jnp.where(shifted >= start, rel_bias[head_slot, bucket + 1], value)
        if which == 2:
            value = jnp.where(shifted >= 0, value, MASKED)
        return value

    def bias_tables(head_slot, carry):
        group = head_slot // 2
        lanes = pl.ds(pl.multiple_of(lax.rem(head_slot, 2) * rows, rows), rows)
        tab[0, group, :, lanes] = jnp.full((rows, rows), rel_bias[head_slot, BUCKETS - 1], F32)
        tab[1, group, :, lanes] = bias_of(1, head_slot)
        tab[2, group, :, lanes] = bias_of(2, head_slot)
        return carry

    lax.fori_loop(0, 2 * groups, bias_tables, 0)
    share_left("ns", ns[...])
    share_left("mem", memory[pl.ds(pl.multiple_of(blk * share, share), share), :])
    for which in range(2):
        ag_end(which)

    def turn_chunk(chunk):
        for pair in range(pairs):
            vT[chunk, pair * 128 : (pair + 1) * 128, :] = chunk_of(vbuf, pair, chunk).T
            kT[chunk, pair * 128 : (pair + 1) * 128, :] = chunk_of(kbuf, pair, chunk).T

    if not long:
        for chunk in range(half_count):
            turn_chunk(chunk)

    def turned_of(kept, buffer, group, chunk):
        if not long:
            return kept[chunk, group * HEAD_DIM : (group + 1) * HEAD_DIM, :]
        first = (group % 2) * HEAD_DIM
        return chunk_of(buffer, group // 2, chunk).T[first : first + HEAD_DIM, :]

    def attend(group):
        tops = jnp.full((1, 2 * rows), MASKED, F32)

        def first_pass(chunk, top):
            part = self_scores(group, chunk)
            if not long:
                scores[group % 2, chunk] = part
            return jnp.maximum(top, jnp.max(part, axis=0, keepdims=True))

        def second_pass(chunk, state):
            total, acc = state
            part = self_scores(group, chunk) if long else scores[group % 2, chunk]
            part = jnp.exp(part - tops)
            total = total + jnp.sum(part, axis=0, keepdims=True)
            return total, acc + dot(turned_of(vT, vbuf, group, chunk), part.astype(BF))

        state = (jnp.zeros((1, 2 * rows), F32), jnp.zeros((HEAD_DIM, 2 * rows), F32))
        if not long:
            for chunk in range(half_count):
                tops = first_pass(chunk, tops)
            for chunk in range(half_count):
                state = second_pass(chunk, state)
        else:
            tops = lax.fori_loop(0, half_count, first_pass, tops)
            state = lax.fori_loop(0, half_count, second_pass, state)
        total, acc = state
        precise = acc / total
        att_self[group] = precise
        lse[group] = tops + jnp.log(total)
        right_all["so"][own["so"], :, group * 128 : (group + 1) * 128] = join_heads(precise).astype(BF)

    checkpoint(4)
    for group in range(groups):
        attend(group)

    checkpoint(5)
    copies.receive(("load", "so"))
    for tile in range(tiles):
        push(0, tile, dot_nt(right_all["so"][own["so"]], row_tile("so", tile)))
    valid = lax.broadcasted_iota(jnp.int32, (rows, 1), 0) + blk * rows < length
    bg[...] = jnp.where(valid, out_grad[...].astype(F32), 0.0).astype(BF)
    share_left("gf", bg[...])
    if not long:
        copies.receive(("load", "fd"))
        inner_grad[...] = dot(bg[...], whole("fd"))
    after_self[...] = x + summed_all(0)

    checkpoint(6)
    norm_into(after_self[...], ln_cross, nc, "nc")
    copies.receive(("load", "cq"))
    split_heads(dot(nc[...], whole("cq")).astype(BF), cqs)
    for group in range(groups):
        part = dot_nt(mk[group // 2], cqs[group])
        part = jnp.exp(part - jnp.max(part, axis=0, keepdims=True))
        part = part * (1.0 / jnp.sum(part, axis=0, keepdims=True))
        probs[group] = part
        acc = dot(mvT[group * HEAD_DIM : (group + 1) * HEAD_DIM, :], part.astype(BF))
        att_cross[group] = acc
        right_all["co"][own["co"], :, group * 128 : (group + 1) * 128] = join_heads(acc).astype(BF)
    checkpoint(7)
    copies.receive(("load", "co"))
    for tile in range(tiles):
        push(1, tile, dot_nt(right_all["co"][own["co"]], row_tile("co", tile)))
    share_right("so")
    share_right("co")
    after_cross[...] = after_self[...] + summed_all(1)

    checkpoint(8)
    norm_into(after_cross[...], ln_ffn, nf, "nf")
    for name in ("fg", "fu", "fd"):
        if ("load", name) not in copies.received:
            copies.receive(("load", name))
    for part, (first, size) in enumerate(lane_tiles(weight["fg"].shape[1])):
        lanes = slice(first, first + size)
        gate = dot(nf[...], whole("fg", lanes))
        up = dot(nf[...], whole("fu", lanes))
        back = dot(bg[...], whole("fd", lanes)) if long else inner_grad[:, lanes]
        bent = jnp.tanh(GELU_A * (gate + GELU_B * gate * gate * gate))
        opened = 0.5 * (1.0 + bent)
        slope = opened + 0.5 * gate * (1.0 - bent * bent) * (
            GELU_A * (1.0 + 3.0 * GELU_B * gate * gate)
        )
        bell = gate * opened
        right_all["fd"][own["fd"], :, lanes] = (bell * up).astype(BF)
        right_all["fg"][own["fg"], :, lanes] = (back * up * slope).astype(BF)
        right_all["fu"][own["fu"], :, lanes] = (back * bell).astype(BF)
        share_right("fd", part, lanes)
        share_right("fg", part, lanes)
    share_right("fu")
    for tile in range(tiles):
        push(
            2,
            tile,
            dot_nt(right_all["fg"][own["fg"]], row_tile("fg", tile))
            + dot_nt(right_all["fu"][own["fu"]], row_tile("fu", tile)),
        )

    pass_right("so")
    pass_right("co")
    normed_grad = summed_all(2)
    cot[...] = jnp.where(valid, out_grad[...].astype(F32), 0.0) + norm_back(
        after_cross[...], ln_ffn, normed_grad, 2
    )
    bg[...] = cot[...].astype(BF)
    share_left("gc", bg[...])

    checkpoint(10)
    back = dot(bg[...], whole("co")).astype(BF)
    split_heads(back, ags)
    for pair in range(pairs):
        key_part = value_part = None
        for group in (2 * pair, 2 * pair + 1):
            prob = probs[group]
            prob_grad = dot_nt(mv[pair], ags[group])
            score_grad = (prob * (prob_grad - head_deltas(back, att_cross, group))).astype(BF)
            turned = dot(mkT[group * HEAD_DIM : (group + 1) * HEAD_DIM, :], score_grad)
            right_all["cq"][own["cq"], :, group * 128 : (group + 1) * 128] = join_heads(turned).astype(BF)
            key_new = dot(score_grad, cqs[group])
            value_new = dot(prob.astype(BF), ags[group])
            key_part = key_new if key_part is None else key_part + key_new
            value_part = value_new if value_part is None else value_part + value_new
        shape = dmem.shape[:-1]
        dmem[..., pair * 128 : (pair + 1) * 128] = key_part.astype(BF).reshape(*shape, 128)
        dmem[..., (pairs + pair) * 128 : (pairs + pair + 1) * 128] = value_part.astype(BF).reshape(
            *shape, 128
        )
    checkpoint(11)
    for tile in range(tiles):
        push(4, tile, dot_nt(right_all["cq"][own["cq"]], row_tile("cq", tile)))
    share_right("cq")
    part_start(*dmem_args, 0)
    pass_right("fd")
    pass_right("fg")
    make_partial("fg")
    for tile in range(tiles):
        push(3, tile, dot_nt(right_all["fd"][own["fd"]], row_tile("fd", tile)))
    make_partial("fd")
    make_partial("co")
    normed_grad = summed_all(4)
    cot[...] = cot[...] + norm_back(after_self[...], ln_cross, normed_grad, 1)
    bg[...] = cot[...].astype(BF)
    share_left("gs", bg[...])

    def add_bias_gradient():
        row = lax.broadcasted_iota(jnp.int32, (rows, rows), 0)
        column = lax.broadcasted_iota(jnp.int32, (rows, rows), 1)
        slot_row = lax.broadcasted_iota(jnp.int32, (2 * groups, rows), 0)
        slot_lane = lax.broadcasted_iota(jnp.int32, (2 * groups, rows), 1)
        bucket = jnp.minimum(slot_lane, BUCKETS // 2)
        for start in bucket_starts()[BUCKETS // 2 :]:
            bucket = bucket + (slot_lane >= start).astype(jnp.int32)
        lines = jnp.zeros((2 * groups, rows), F32)
        last = jnp.zeros((2 * groups, rows), F32)
        for group in range(groups):
            for half in range(2):
                lanes = slice(half * rows, (half + 1) * rows)
                here = near[2, group, :, lanes].astype(F32)
                before = near[1, group, :, lanes].astype(F32)
                tile = here + jnp.where(column < row, before, 0.0)
                for bit in range(rows.bit_length() - 1):
                    moved = pltpu.roll(tile, rows - (1 << bit), 1)
                    tile = jnp.where(lax.rem(row // (1 << bit), 2) == 1, moved, tile)
                line = jnp.sum(tile, axis=0, keepdims=True)
                beyond = jnp.sum(jnp.where(column < row, 0.0, before), axis=0, keepdims=True)
                beyond = beyond + far_sum[group, :, lanes]
                slot = 2 * group + half
                lines = jnp.where(slot_row == slot, line, lines)
                last = jnp.where(slot_row == slot, beyond, last)
        wide = lax.broadcasted_iota(jnp.int32, (2 * groups, rows), 1)
        grid = jnp.zeros((2 * groups, rows), F32)
        for place in range(BUCKETS):
            total = jnp.sum(jnp.where(bucket == place, lines, 0.0), axis=1, keepdims=True)
            if place == BUCKETS - 1:
                total = total + jnp.sum(last, axis=1, keepdims=True)
            grid = jnp.where(wide == place, total, grid)
        first_bias = 3 * (width // 128)
        small[member(0), first_bias : first_bias + 2 * groups, :] = grid

    checkpoint(12)
    back = dot(bg[...], whole("so")).astype(BF)
    split_heads(back, ags)
    pass_right("fu")
    make_partial("fu")
    pass_right("cq")
    rs_step("fg", 0)
    near[1] = jnp.zeros(near.shape[1:], BF)
    for pair in range(pairs):
        members = (2 * pair, 2 * pair + 1)
        deltas = [head_deltas(back, att_self, group) for group in members]

        def visit(chunk, state, pair=pair, members=members, deltas=deltas):
            state = list(state)
            key_part = value_part = None
            values_here = chunk_of(vbuf, pair, chunk)
            for slot, group in enumerate(members):
                prob = jnp.exp(self_scores(group, chunk) - lse[group])
                prob_grad = dot_nt(values_here, ags[group])
                score_grad = (prob * (prob_grad - deltas[slot])).astype(BF)
                lhs = turned_of(kT, kbuf, group, chunk)
                state[2 * slot] = state[2 * slot] + dot(lhs, score_grad)
                key_new = dot(score_grad, qs[group])
                value_new = dot(prob.astype(BF), ags[group])
                key_part = key_new if key_part is None else key_part + key_new
                value_part = value_new if value_part is None else value_part + value_new
                for inner_block in range(2):
                    kind = kind_of(2 * chunk + inner_block)
                    piece = score_grad[inner_block * rows : (inner_block + 1) * rows, :]
                    near[lax.rem(kind, 3), group] = piece
                    is_far = (kind == 0).astype(F32)
                    state[2 * slot + 1] = state[2 * slot + 1] + is_far * jnp.sum(
                        piece.astype(F32), axis=0, keepdims=True
                    )
            where_to = (pair, *half_index(chunk))
            dkv[(*where_to, slice(None), slice(None), slice(0, 128))] = key_part.astype(BF).reshape(
                2, rows, 128
            )
            dkv[(*where_to, slice(None), slice(None), slice(128, 256))] = value_part.astype(
                BF
            ).reshape(2, rows, 128)
            return tuple(state)

        state = (jnp.zeros((HEAD_DIM, 2 * rows), F32), jnp.zeros((1, 2 * rows), F32)) * 2
        if not long:
            for chunk in range(half_count):
                state = visit(chunk, state)
        else:
            state = lax.fori_loop(0, half_count, visit, state)
        part_start(*dkv_args(pair), 0)
        if pair == 0:
            make_partial("so")
            part_step(*dmem_args, 0)
            rs_step("fu", 0)
        for slot, group in enumerate(members):
            right_all["sq"][own["sq"], :, group * 128 : (group + 1) * 128] = join_heads(
                state[2 * slot]
            ).astype(BF)
            far_sum[group] = state[2 * slot + 1]
    checkpoint(13)
    share_right("sq")
    make_partial("cq")
    for tile in range(tiles):
        lanes = slice(tile * TILE, (tile + 1) * TILE)
        staged["layer_out"][:, lanes] = (after_cross[:, lanes] + summed(3, tile)).astype(BF)
    give("layer_out")
    rs_step("co", 0)
    part_step(*dmem_args, 1)
    part_step(*dkv_args(0), 0)
    rs_step("fd", 0)
    query_part = [
        dot_nt(right_all["sq"][own["sq"]], row_tile("sq", tile)) for tile in range(tiles)
    ]
    for step in range(1, bits - 1):
        rs_step("fg", step)
    part_step(*dkv_args(1), 0)
    mem_sum = None
    for step in range(2, bits):
        mem_sum = part_step(*dmem_args, step)
    mem_sum = mem_sum.astype(BF)
    right_all["ck"][own["ck"]] = mem_sum[:, : pairs * 128]
    right_all["cv"][own["cv"]] = mem_sum[:, pairs * 128 :]
    share_right("ck")
    share_right("cv")
    for step in range(1, bits - 1):
        part_step(*dkv_args(0), step)
        part_step(*dkv_args(1), step)
    rs_step("so", 0)
    pass_right("sq")
    make_partial("sq")
    for step in range(1, bits - 1):
        rs_step("fu", step)
    sums = [part_step(*dkv_args(pair), bits - 1).astype(BF) for pair in range(pairs)]
    for pair, value in enumerate(sums):
        right_all["sk"][own["sk"], :, pair * 128 : (pair + 1) * 128] = value[:, :128]
        right_all["sv"][own["sv"], :, pair * 128 : (pair + 1) * 128] = value[:, 128:]
    share_right("sk")
    share_right("sv")
    for tile in range(tiles):
        push(
            5,
            tile,
            query_part[tile]
            + dot_nt(right_all["sk"][own["sk"]], row_tile("sk", tile))
            + dot_nt(right_all["sv"][own["sv"]], row_tile("sv", tile)),
        )
    rs_step("cq", 0)
    for name in ("ck", "cv"):
        pass_right(name)
        make_partial(name)
    add_bias_gradient()
    for step in range(1, bits - 1):
        rs_step("co", step)
        rs_step("fd", step)

    checkpoint(14)
    mkg, mvg = right_all["ck"][own["ck"]], right_all["cv"][own["cv"]]
    mem_part = dot_nt(mkg, whole("ck")) + dot_nt(mvg, whole("cv"))
    half = share // 2
    mem_push[0] = mem_part[:half, :].astype(BF)
    mem_push[1] = mem_part[half:, :].astype(BF)
    mem_copy = pltpu.make_async_remote_copy(
        src_ref=mem_push.at[1 - head],
        dst_ref=mem_land,
        send_sem=mg_send,
        recv_sem=mg_recv,
        device_id=other_head,
        device_id_type=MESH,
    )
    copies.start(("mem",), mem_copy)
    for name in ("sk", "sv"):
        pass_right(name)
    for name in ("sk", "sv"):
        make_partial(name)
    for name in ("ck", "cv"):
        rs_step(name, 0)

    checkpoint(16)
    normed_grad = summed_all(5)
    staged["hidden_grad"][...] = cot[...] + norm_back(hidden[...].astype(F32), ln_self, normed_grad, 0)
    give("hidden_grad")

    def small_near(way):
        return pltpu.make_async_remote_copy(
            src_ref=small.at[member(0)],
            dst_ref=small.at[member(0)],
            send_sem=sm_send.at[way],
            recv_sem=sm_recv.at[way],
            device_id=peers(0)[way],
            device_id_type=MESH,
        )

    def small_across(way):
        return pltpu.make_async_remote_copy(
            src_ref=small_far.at[blk // 2],
            dst_ref=small_far.at[blk // 2],
            send_sem=sm_send.at[3 + way],
            recv_sem=sm_recv.at[3 + way],
            device_id=hop(far_masks[way]),
            device_id_type=MESH,
        )

    for way in (1, 2, 0):
        copies.start(("small", way), small_near(way))
    for way in range(3):
        copies.receive(("small", way))
    small_far[blk // 2] = small[0] + small[1] + small[2] + small[3]
    for way in range(len(far_masks)):
        copies.start(("small", 3 + way), small_across(way))
    rs_step("sq", 0)
    for step in range(1, bits - 1):
        for name in ("so", "cq"):
            rs_step(name, step)
    for step in range(1, bits - 1):
        for name in ("ck", "cv"):
            rs_step(name, step)
    for name in ("sk", "sv"):
        rs_finish(name)
    for step in range(1, bits - 1):
        rs_step("sq", step)
    for way in range(len(far_masks)):
        copies.receive(("small", 3 + way))
    total = small_far[0]
    for slot in range(1, blk_count // 2):
        total = total + small_far[slot]
    small_out[...] = total
    copies.receive(("mem",))
    staged["memory_grad"][...] = mem_push[head].astype(F32) + mem_land[...].astype(F32)
    give("memory_grad")


def finish_kernel(count, lines, width, *refs):
    sources, small = refs[:count], refs[count]
    targets = refs[count + 1 : 2 * count + 1]
    gain_out, bias_out, sems = refs[2 * count + 1 : 2 * count + 4], refs[2 * count + 4], refs[-1]
    moves = [
        pltpu.make_async_copy(source, target, sems.at[slot])
        for slot, (source, target) in enumerate(zip(sources, targets))
    ]
    for move in moves:
        move.start()
    share = gain_out[0].shape[0]
    per_line = 128 // share
    place = lax.axis_index("seq") * lax.axis_size("blk") + lax.axis_index("blk")
    for slot, target in enumerate(gain_out):
        line = small[pl.ds(slot * lines + place // per_line, 1), :]
        for part in range(per_line):

            @pl.when(lax.rem(place, per_line) == part)
            def _(target=target, line=line, part=part):
                target[...] = line[0, part * share : (part + 1) * share]

    bias_out[...] = small[3 * lines :, : bias_out.shape[1]]
    for move in moves:
        move.wait()


def finish(results, small, width, share, heads):
    count = len(results)
    in_any = pl.BlockSpec(memory_space=pl.ANY)
    in_vmem = pl.BlockSpec(memory_space=pltpu.VMEM)
    return pl.pallas_call(
        functools.partial(finish_kernel, count, width // 128, width),
        out_shape=[
            *(jax.ShapeDtypeStruct(result.shape, result.dtype) for result in results),
            *[jax.ShapeDtypeStruct((share,), F32)] * 3,
            jax.ShapeDtypeStruct((heads, BUCKETS), F32),
        ],
        in_specs=[in_vmem] * (count + 1),
        out_specs=[*[in_any] * count, *[in_vmem] * 4],
        scratch_shapes=[pltpu.SemaphoreType.DMA((count,))],
        name="finish",
    )(*results, small)


def run_layer(lengths, rel_bias, hidden, out_grad, gains, memory, weights, blk_count, stop=None):
    bits = blk_count.bit_length() - 1
    stages = bits + 1
    rows, width = hidden.shape
    groups = weights["sk"].shape[1] // HEAD_DIM
    heads = weights["sq"].shape[1] // HEAD_DIM
    mem_rows = memory.shape[0]
    if rows != 128 or heads != 2 * groups or bucket_starts()[-1] > rows or 1 << bits != blk_count:
        raise ValueError("unexpected sizes")
    pairs = groups // 2
    half_count = blk_count // 2
    long = half_count > 4
    stored = 1 if long else half_count
    piece = width // (2 * blk_count)
    widths = {name: weights[name].shape[1] for name in NAMES}
    share = mem_rows // blk_count
    small_rows = 3 * (width // 128) + heads

    vm, sem = pltpu.VMEM, pltpu.SemaphoreType.DMA
    high = (2,) * (bits - 1)
    depth = {name: share if LEFT_OF[name] == "mem" else rows for name in NAMES}
    scratch = [vm((width, widths[name]), BF) for name in NAMES]
    scratch += [
        vm((2, *high, 2, piece, share if left == "mem" else rows), BF) for left in LEFTS
    ]
    scratch += [
        vm((4, *high, piece, share) if left == "mem" else (*high, piece, 4 * rows), BF)
        for left in LEFTS
    ]
    scratch += [vm((4, depth[name], widths[name]), BF) for name in NAMES]
    scratch += [vm((*high, piece, widths[name]), BF) for name in NAMES]
    for name in NAMES:
        if name in DIRECT:
            scratch.append(vm((half_count - 1, piece, widths[name]), BF))
            continue
        for stage in range(bits - 1):
            scratch.append(vm((2,) * (bits - 2 - stage) + (piece, widths[name]), BF))
    by_bit = (2,) * bits
    scratch += [vm((rows, width), BF), vm((rows, width), F32), vm((share // 2, width), F32)]
    scratch += [vm((piece, widths[name]), F32) for name in NAMES]
    scratch += [
        vm(memory.shape, BF),
        vm((pairs, *by_bit, rows, 128), BF),
        vm((pairs, *by_bit, rows, 128), BF),
        vm((stored, groups * HEAD_DIM, 2 * rows), BF),
        vm((stored, groups * HEAD_DIM, 2 * rows), BF),
        vm((3, groups, rows, 2 * rows), F32),
        vm((3, groups, rows, 2 * rows), BF),
        vm((2, stored, 8 if long else 2 * rows, 2 * rows), F32),
        vm((groups, 2 * rows, 128), BF),
        vm((groups, 2 * rows, 128), BF),
        vm((groups, 2 * rows, 128), BF),
        vm((groups, HEAD_DIM, 2 * rows), F32),
        vm((groups, HEAD_DIM, 2 * rows), F32),
        vm((groups, 1, 2 * rows), F32),
        vm((groups, mem_rows, 2 * rows), F32),
        vm((pairs, mem_rows, 128), BF),
        vm((pairs, mem_rows, 128), BF),
        vm((groups * HEAD_DIM, mem_rows), BF),
        vm((groups * HEAD_DIM, mem_rows), BF),
        vm((4, width // TILE, rows, TILE), BF),
        vm((4, width // TILE, rows, TILE), BF),
        vm((rows, width), F32),
        vm((rows, width), F32),
        vm((rows, width), F32),
        vm((rows, width), BF),
        vm((rows, width), BF),
        vm((rows, width), BF),
        vm((rows, width), BF),
        vm((8 if long else rows, widths["fd"]), F32),
        vm((pairs, *by_bit, rows, 256), BF),
    ]
    scratch += [vm((pairs, *(2,) * (bits - 1 - stage), rows, 256), BF) for stage in range(bits)]
    scratch += [vm((*by_bit, share, 2 * groups * HEAD_DIM), BF)]
    scratch += [
        vm((*(2,) * (bits - 1 - stage), share, 2 * groups * HEAD_DIM), BF) for stage in range(bits)
    ]
    scratch += [
        vm((2, share // 2, width), BF),
        vm((share // 2, width), BF),
        vm((4, small_rows, 128), F32),
        vm((half_count, small_rows, 128), F32),
        vm((groups, 1, 2 * rows), F32),
        sem((len(NAMES) + 1,)),
        sem((6, width // TILE)),
        sem((6, width // TILE)),
        sem((2, half_count, 2)),
        sem((2, half_count, 2)),
        sem((len(NAMES), half_count)),
        sem((len(NAMES), half_count)),
        sem((len(LEFTS), 3)),
        sem((len(LEFTS), 3)),
        sem((len(NAMES), 3, 3)),
        sem((len(NAMES), 3, 3)),
        sem((3 + len(NAMES),)),
        sem((pairs, bits)),
        sem((pairs, bits)),
        sem((bits,)),
        sem((bits,)),
        sem,
        sem,
        sem((half_count + 2,)),
        sem((half_count + 2,)),
    ]
    in_vmem = pl.BlockSpec(memory_space=pltpu.VMEM)
    in_smem = pl.BlockSpec(memory_space=pltpu.SMEM)
    in_any = pl.BlockSpec(memory_space=pl.ANY)
    out_shape = [
        jax.ShapeDtypeStruct((rows, width), BF),
        jax.ShapeDtypeStruct((rows, width), F32),
        jax.ShapeDtypeStruct((share // 2, width), F32),
        *(jax.ShapeDtypeStruct((piece, widths[name]), F32) for name in NAMES),
        jax.ShapeDtypeStruct((small_rows, 128), F32),
    ]
    results = pl.pallas_call(
        functools.partial(layer_kernel, (bits, rows, width, groups, mem_rows), stop),
        out_shape=out_shape,
        in_specs=[in_smem, in_smem, *[in_vmem] * 5, *[in_any] * 12],
        out_specs=[*[in_any] * (len(out_shape) - 1), in_vmem],
        scratch_shapes=scratch,
        compiler_params=pltpu.CompilerParams(
            collective_id=0, has_side_effects=True, vmem_limit_bytes=63 * 1024 * 1024
        ),
        name="layer",
    )(
        lengths, rel_bias, hidden, out_grad, *gains, memory, *(weights[name] for name in NAMES)
    )
    return results[:3], dict(zip(NAMES, results[3:-1])), results[-1]


def body(
    hidden,
    memory,
    lengths,
    out_grad,
    ln_self,
    self_query,
    self_key,
    self_value,
    self_out,
    rel_bias,
    ln_cross,
    cross_query,
    cross_key,
    cross_value,
    cross_out,
    ln_ffn,
    ffn_gate,
    ffn_up,
    feedforward_down_weight,
):
    width = hidden.shape[1]
    blk_count = lax.axis_size("blk")
    weights = dict(
        sk=self_key,
        sv=self_value,
        sq=self_query,
        ck=cross_key,
        cv=cross_value,
        so=self_out,
        cq=cross_query,
        co=cross_out,
        fg=ffn_gate,
        fu=ffn_up,
        fd=feedforward_down_weight,
    )
    gains = [gain.reshape(1, width) for gain in (ln_self, ln_cross, ln_ffn)]
    (layer_out, hidden_grad, memory_grad), grads, small = run_layer(
        lengths, rel_bias.T, hidden, out_grad, gains, memory, weights, blk_count
    )
    kept = [layer_out, hidden_grad, memory_grad, *(grads[name] for name in NAMES)]
    *kept, self_gain, cross_gain, ffn_gain, bias_grad = finish(
        kept, small, width, width // (2 * blk_count), rel_bias.shape[1]
    )
    layer_out, hidden_grad, memory_grad = kept[:3]
    grads = dict(zip(NAMES, kept[3:]))
    return (
        layer_out,
        hidden_grad,
        memory_grad,
        self_gain,
        grads["sq"],
        grads["sk"],
        grads["sv"],
        grads["so"],
        bias_grad.T,
        cross_gain,
        grads["cq"],
        grads["ck"],
        grads["cv"],
        grads["co"],
        ffn_gain,
        grads["fg"],
        grads["fu"],
        grads["fd"],
    )


def solution(mesh):
    blocks = P(("seq", "blk"), None)
    by_head = P(None, "head")
    shares = P(("seq", "blk"), "head")
    line = P(("seq", "blk"))
    in_specs = (
        blocks,
        P("seq", None),
        P("seq"),
        blocks,
        P(),
        *[by_head] * 5,
        P(),
        *[by_head] * 4,
        P(),
        *[by_head] * 3,
    )
    out_specs = (
        blocks,
        blocks,
        P(("seq", "blk", "head"), None),
        line,
        *[shares] * 4,
        by_head,
        line,
        *[shares] * 4,
        line,
        *[shares] * 3,
    )
    return jax.shard_map(body, mesh=mesh, in_specs=in_specs, out_specs=out_specs, check_vma=False)
```
